32 devices in a mesh: dp: 8 (over z, y), head: 4 (over x, core).
Axes of the slice: x: 2, y: 2, z: 4, core: 2. Of those that a mesh axis runs over, the one named last changes fastest.
Arguments:
- tokens: bfloat16 [24576, 768], P(('dp', 'head')), may hold values from -15 to 15
- segment_ids: int32 [24576], P('dp'), may hold values from 0 to 189, as said below
- cotangent: bfloat16 [24576, 768], P(('dp', 'head')), may hold values from -6 to 6
- clip_norm: float32 [1], replicated, as said below
- master_qkv: float32 [768, 2304], P('dp'), may hold values from -0.21875 to 0.21875
- master_out: float32 [768, 768], P('dp'), may hold values from -0.875 to 0.875
- master_gu: float32 [768, 6144], P('dp'), may hold values from -0.72168784 to 0.72168784
- master_down: float32 [3072, 768], P('dp'), may hold values from -0.109375 to 0.109375
- master_vec: float32 [6, 768], P(None, 'dp')
- first_qkv: float32 [768, 2304], P('dp')
- first_out: float32 [768, 768], P('dp')
- first_gu: float32 [768, 6144], P('dp')
- first_down: float32 [3072, 768], P('dp')
- first_vec: float32 [6, 768], P(None, 'dp')
- second_qkv: float32 [768, 2304], P('dp'), as said below
- second_out: float32 [768, 768], P('dp'), as said below
- second_gu: float32 [768, 6144], P('dp'), as said below
- second_down: float32 [3072, 768], P('dp'), as said below
- second_vec: float32 [6, 768], P(None, 'dp'), as said below
Outputs:
- output: bfloat16 [24576, 768], P(('dp', 'head'))
- grad_input: float32 [24576, 768], P(('dp', 'head'))
- new_qkv: float32 [768, 2304], P('dp')
- moment1_qkv: float32 [768, 2304], P('dp')
- moment2_qkv: float32 [768, 2304], P('dp')
- copy_qkv: bfloat16 [768, 2304], P('dp')
- new_out: float32 [768, 768], P('dp')
- moment1_out: float32 [768, 768], P('dp')
- moment2_out: float32 [768, 768], P('dp')
- copy_out: bfloat16 [768, 768], P('dp')
- new_gu: float32 [768, 6144], P('dp')
- moment1_gu: float32 [768, 6144], P('dp')
- moment2_gu: float32 [768, 6144], P('dp')
- copy_gu: bfloat16 [768, 6144], P('dp')
- new_down: float32 [3072, 768], P('dp')
- moment1_down: float32 [3072, 768], P('dp')
- moment2_down: float32 [3072, 768], P('dp')
- copy_down: bfloat16 [3072, 768], P('dp')
- new_vec: float32 [6, 768], P(None, 'dp')
- moment1_vec: float32 [6, 768], P(None, 'dp')
- moment2_vec: float32 [6, 768], P(None, 'dp')
- copy_vec: bfloat16 [6, 768], P(None, 'dp')
- grad_norm: float32 [1], replicated
The draws below stay inside these ranges and needn't reach their ends.
Inputs may be any that keep to these rules, and one draw needn't show every extreme that they name: `segment_ids`: ids never fall; each aligned block of 1024 tokens holds whole sequences of 128, 256 or 512 tokens, and no id appears in two blocks; block k's ids lie within 8 * k to 8 * k + 5. `clip_norm`: Positive. `second_qkv`: Positive. `second_out`: Positive. `second_gu`: Positive. `second_down`: Positive. `second_vec`: Positive.
All inputs are finite; a program needn't handle non-finite values.
Results may differ from the reference program's by a relative error of at most 0.019.
The reference program's roundings to bfloat16 on the way count: a program that leaves them out, or rounds other values in their place, can miss the bound.
Values may be sent and summed in bfloat16 or wider, within the bound.
No kernel may reach another device: no remote copies, remote signals or barrier semaphores. Data moves between devices by JAX's collectives and lax.ppermute only.
A program may use at most 192 MiB of HBM per device.

```python
import math
import jax
import jax.numpy as jnp
import numpy as np
from jax import lax

D = 768
HEADS = 12
HEAD_DIM = 64
FF = 3072
PACK = 1024
TOKENS = 24576
PARAMS = 9441792


LAYOUTS = np.array([[0, 0, 0, 0, 1, 1, 2, 2], [0, 0, 1, 1, 1, 1, 2, 2], [0, 1, 2, 3, 4, 4, 4, 4], [0, 1, 2, 2, 2, 2, 3, 4], [0, 0, 1, 1, 2, 3, 4, 5], [0, 1, 1, 2, 3, 3, 4, 5]], dtype=np.int32)


def column_ramp(key, width):
    top_ratio = 3.0
    place = jnp.arange(width).astype(jnp.float32) / (width - 1)
    rough = jnp.exp(jax.random.uniform(key, (width,), jnp.float32, 0.0, math.log(2.0)))
    return jnp.exp(math.log(top_ratio) * place) * rough / 2.5


def draw_tokens(key, part):
    ramp = column_ramp(jax.random.fold_in(key, 11), D)
    base = jnp.clip(jax.random.normal(jax.random.fold_in(key, 12), (TOKENS, D), jnp.float32), -6.0, 6.0)
    return (base * ramp[None, :]).astype(jnp.bfloat16)


def draw_master_gu(key, part):
    ramp = column_ramp(jax.random.fold_in(key, 21), FF)
    scales = jnp.concatenate((jnp.ones((FF,), jnp.float32), ramp * 1.5))
    base = jnp.clip(jax.random.normal(jax.random.fold_in(key, 22), (D, 2 * FF), jnp.float32), -6.0, 6.0)
    limit = 20.0 * D ** (-0.5)
    return jnp.clip(base * D ** (-0.5) * scales[None, :], -limit, limit)


def draw_segment_ids(key, part):
    pack_count = TOKENS // PACK
    chosen_rows = jax.random.randint(key, (pack_count,), 0, LAYOUTS.shape[0])
    chosen_rows = chosen_rows.at[pack_count - 1].set(4)
    local_ids = jnp.asarray(LAYOUTS, jnp.int32)[chosen_rows]
    seg_values = local_ids + 8 * jnp.arange(pack_count, dtype=jnp.int32)[:, None]
    return jnp.repeat(seg_values, PACK // 8, axis=1).reshape(TOKENS).astype(jnp.int32)


def draw_clip_norm(key, part):
    unit_draw = jax.random.uniform(key, (1,), jnp.float32, 0.005, 0.01)
    return unit_draw * math.sqrt(PARAMS * TOKENS)


def grad_size(boost):
    return 0.012 * boost * math.sqrt(TOKENS)


def first_draw(key, array_shape, boost):
    return jax.random.normal(key, array_shape, jnp.float32) * (0.11 * grad_size(boost))


def second_draw(key, array_shape, boost):
    factors = jnp.exp(jax.random.uniform(key, array_shape, jnp.float32, 0.0, math.log(4.0)))
    return factors * (0.001 * grad_size(boost) ** 2)


def draw_master_vec(key, part):
    noise = jax.random.normal(jax.random.fold_in(key, 31), (6, D), jnp.float32)
    ramp = column_ramp(jax.random.fold_in(key, 32), D)
    row_index = jnp.arange(6)
    gain_two = 1.0 + 0.15 * noise
    gain_one = ramp[None, :] * (1.0 + 0.1 * noise)
    rest = 0.3 * noise
    return jnp.where((row_index == 0)[:, None], gain_one, jnp.where((row_index == 2)[:, None], gain_two, rest))


def draw_first_qkv(key, part):
    return first_draw(key, (D, 3 * D), 1.0)


def draw_first_out(key, part):
    return first_draw(key, (D, D), 1.0)


def draw_first_gu(key, part):
    return first_draw(key, (D, 2 * FF), 1.0)


def draw_first_down(key, part):
    return first_draw(key, (FF, D), 1.0)


def draw_first_vec(key, part):
    return first_draw(key, (6, D), 2.0)


def draw_second_qkv(key, part):
    return second_draw(key, (D, 3 * D), 1.0)


def draw_second_out(key, part):
    return second_draw(key, (D, D), 1.0)


def draw_second_gu(key, part):
    return second_draw(key, (D, 2 * FF), 1.0)


def draw_second_down(key, part):
    return second_draw(key, (FF, D), 1.0)


def draw_second_vec(key, part):
    return second_draw(key, (6, D), 2.0)


def steps_of(own_key, dims, cuts, smallest, top_value):
    gain, own = 1.0, jax.random.fold_in(own_key, 6)
    for position, blocks in cuts:
        steps = jnp.exp(jax.random.uniform(jax.random.fold_in(own, position), (blocks,), jnp.float32, smallest / len(cuts), top_value / len(cuts)))
        gain = gain * jnp.repeat(steps, dims[position] // blocks).reshape([-1 if axis == position else 1 for axis in range(len(dims))])
    return gain


def bell_draw(stream_key, dims, deviation, most, split=(), kind=jnp.bfloat16):
    values = deviation * jax.random.normal(stream_key, dims, jnp.float32)
    if split:
        values = values * steps_of(stream_key, dims, split, -0.22, 0.18)
    return jnp.clip(values, -most, most).astype(kind)


def setup_inputs(seed: int = 0) -> dict:
    streams_of = jax.random.split(jax.random.key(seed), 20)
    return {
        "tokens": draw_tokens(jax.random.fold_in(streams_of[19], 71), 0),
        "segment_ids": draw_segment_ids(jax.random.fold_in(streams_of[19], 71), 0),
        "cotangent": bell_draw(streams_of[2], (TOKENS, D), 1.0, 6.0, ((0, 32),)),
        "clip_norm": draw_clip_norm(jax.random.fold_in(streams_of[19], 71), 0),
        "master_qkv": bell_draw(streams_of[4], (D, 3 * D), D ** -0.5, 0.21875, ((0, 8),), jnp.float32),
        "master_out": bell_draw(streams_of[5], (D, D), (D // 16) ** -0.5, 0.875, ((0, 8),), jnp.float32),
        "master_gu": draw_master_gu(jax.random.fold_in(streams_of[19], 71), 0),
        "master_down": bell_draw(streams_of[7], (FF, D), FF ** -0.5, 0.109375, ((0, 8),), jnp.float32),
        "master_vec": draw_master_vec(jax.random.fold_in(streams_of[19], 71), 0),
        "first_qkv": draw_first_qkv(jax.random.fold_in(streams_of[19], 71), 0),
        "first_out": draw_first_out(jax.random.fold_in(streams_of[19], 71), 0),
        "first_gu": draw_first_gu(jax.random.fold_in(streams_of[19], 71), 0),
        "first_down": draw_first_down(jax.random.fold_in(streams_of[19], 71), 0),
        "first_vec": draw_first_vec(jax.random.fold_in(streams_of[19], 71), 0),
        "second_qkv": draw_second_qkv(jax.random.fold_in(streams_of[19], 71), 0),
        "second_out": draw_second_out(jax.random.fold_in(streams_of[19], 71), 0),
        "second_gu": draw_second_gu(jax.random.fold_in(streams_of[19], 71), 0),
        "second_down": draw_second_down(jax.random.fold_in(streams_of[19], 71), 0),
        "second_vec": draw_second_vec(jax.random.fold_in(streams_of[19], 71), 0),
    }


@jax.custom_vjp
def low(v):
    return lax.optimization_barrier(v.astype(jnp.bfloat16)).astype(jnp.float32)

@jax.custom_vjp
def low_back(v):
    return v

def low_keep(v):
    return (low(v), None)

def low_pass(kept, grad):
    return (grad,)

def back_keep(v):
    return (v, None)

def back_low(kept, grad):
    return (low(grad),)
low.defvjp(low_keep, low_pass)
low_back.defvjp(back_keep, back_low)
SLOPES = [2.0 ** (-(level + 1)) for level in range(8)] + [2.0 ** (-(level + 0.5)) for level in range(4)]
LN_EPS = 1e-05
BETA_ONE = 0.9
BETA_TWO = 0.999
ADAM_EPS = 1e-08
CORR_ONE = 1.0 - 0.9 ** 10
CORR_TWO = 1.0 - 0.999 ** 10
RATE_MAT = 0.05
RATE_VEC = 0.5
DECAY_MAT = 0.01
HIGH = lax.Precision.HIGHEST

def layer_norm(hidden, gain_vec, shift_vec):
    center = hidden - lax.optimization_barrier(jnp.mean(hidden, axis=-1, keepdims=True))
    spread = lax.optimization_barrier(jnp.mean(center * center, axis=-1, keepdims=True))
    return center * lax.rsqrt(spread + LN_EPS) * gain_vec + shift_vec

def gating(joined):
    half_width = joined.shape[-1] // 2
    return jax.nn.gelu(joined[:, :half_width], approximate=False) * joined[:, half_width:]

def adam_update(master, first_mom, second, grad_term, factor, step_rate, decay_rate):
    clipped = grad_term * factor
    first_new = BETA_ONE * first_mom + (1.0 - BETA_ONE) * clipped
    second_new = BETA_TWO * second + (1.0 - BETA_TWO) * clipped * clipped
    direction = first_new / CORR_ONE / (jnp.sqrt(second_new / CORR_TWO) + ADAM_EPS)
    master_new = master - step_rate * (direction + decay_rate * master)
    return (master_new, first_new, second_new, master_new.astype(jnp.bfloat16))

def rounded(master):
    return lax.optimization_barrier(master.astype(jnp.bfloat16)).astype(jnp.float32)

def reference(tokens, segment_ids, cotangent, clip_norm, master_qkv, master_out, master_gu, master_down, master_vec, first_qkv, first_out, first_gu, first_down, first_vec, second_qkv, second_out, second_gu, second_down, second_vec):
    score_scale = HEAD_DIM ** (-0.5)
    slope_table = jnp.asarray(np.array(SLOPES), jnp.float32)
    pack_count = TOKENS // PACK

    def attend(pieces):
        query_pack, key_pack, value_pack, seg_pack = pieces
        scores = jnp.einsum('qhd,khd->hqk', query_pack, key_pack, precision=HIGH) * score_scale
        positions = jnp.arange(PACK).astype(jnp.float32)
        distance = jnp.abs(positions[:, None] - positions[None, :])
        same_seq = seg_pack[:, None] == seg_pack[None, :]
        scores = low_back(jnp.where(same_seq[None], scores - slope_table[:, None, None] * distance[None], -1000000000.0))
        soft_weights = low(jax.nn.softmax(scores, axis=-1))
        return jnp.einsum('hqk,khd->qhd', soft_weights, value_pack, precision=HIGH)

    def forward(inputs, weight_qkv, weight_out, weight_gu, weight_down, vectors):
        joined = jnp.dot(inputs, weight_qkv, precision=HIGH, preferred_element_type=jnp.float32)
        queries = low(low_back(joined[:, :D])).reshape(pack_count, PACK, HEADS, HEAD_DIM)
        keys_all = low(low_back(joined[:, D:2 * D])).reshape(pack_count, PACK, HEADS, HEAD_DIM)
        values_all = low(low_back(joined[:, 2 * D:])).reshape(pack_count, PACK, HEADS, HEAD_DIM)
        context = lax.map(jax.checkpoint(attend), (queries, keys_all, values_all, segment_ids.reshape(pack_count, PACK)))
        context = low(low_back(context.reshape(TOKENS, D)))
        attn_out = low_back(jnp.dot(context, weight_out, precision=HIGH, preferred_element_type=jnp.float32))
        first_sum = inputs + attn_out + vectors[4]
        normed_one = layer_norm(first_sum, vectors[0], vectors[1])
        gate_up = low_back(jnp.dot(low(normed_one), weight_gu, precision=HIGH, preferred_element_type=jnp.float32))
        hidden = low(gating(gate_up))
        ffn_out = low_back(jnp.dot(hidden, weight_down, precision=HIGH, preferred_element_type=jnp.float32))
        second_sum = normed_one + ffn_out + vectors[5]
        return layer_norm(second_sum, vectors[2], vectors[3])
    inputs = tokens.astype(jnp.float32)
    result, pullback = jax.vjp(forward, inputs, rounded(master_qkv), rounded(master_out), rounded(master_gu), rounded(master_down), rounded(master_vec))
    grads = pullback(cotangent.astype(jnp.float32))
    squares = jnp.float32(0.0)
    for grad_term in grads[1:]:
        squares = squares + jnp.sum(grad_term * grad_term)
    grad_norm = jnp.sqrt(squares)
    factor = jnp.minimum(1.0, clip_norm[0] / grad_norm)
    up_qkv = adam_update(master_qkv, first_qkv, second_qkv, grads[1], factor, RATE_MAT, DECAY_MAT)
    up_out = adam_update(master_out, first_out, second_out, grads[2], factor, RATE_MAT, DECAY_MAT)
    up_gu = adam_update(master_gu, first_gu, second_gu, grads[3], factor, RATE_MAT, DECAY_MAT)
    up_down = adam_update(master_down, first_down, second_down, grads[4], factor, RATE_MAT, DECAY_MAT)
    up_vec = adam_update(master_vec, first_vec, second_vec, grads[5], factor, RATE_VEC, 0.0)
    return (result.astype(jnp.bfloat16), grads[0], up_qkv[0], up_qkv[1], up_qkv[2], up_qkv[3], up_out[0], up_out[1], up_out[2], up_out[3], up_gu[0], up_gu[1], up_gu[2], up_gu[3], up_down[0], up_down[1], up_down[2], up_down[3], up_vec[0], up_vec[1], up_vec[2], up_vec[3], grad_norm.reshape(1))
```

```python
import functools

import jax
import jax.numpy as jnp
import numpy as np
from jax import lax
from jax.experimental import pallas as pl
from jax.experimental.pallas import tpu as pltpu
from jax.sharding import PartitionSpec as P

HEADS = 12
HEAD_DIM = 64
BLOCK = 128
HALO = 384
MIB = 1024 * 1024

SLOPES = [2.0 ** (-(level + 1)) for level in range(8)] + [
    2.0 ** (-(level + 0.5)) for level in range(4)
]
LN_EPS = 1e-05
BETA_ONE = 0.9
BETA_TWO = 0.999
ADAM_EPS = 1e-08
CORR_ONE = 1.0 - 0.9**10
CORR_TWO = 1.0 - 0.999**10
RATE_MAT = 0.05
RATE_VEC = 0.5
DECAY_MAT = 0.01

BF16 = jnp.bfloat16
F32 = jnp.float32


def dot_nn(left, right):
    return lax.dot_general(left, right, (((1,), (0,)), ((), ())), preferred_element_type=F32)


def dot_nt(left, right):
    return lax.dot_general(left, right, (((1,), (1,)), ((), ())), preferred_element_type=F32)


def dot_tn(left, right):
    return lax.dot_general(left, right, (((0,), (0,)), ((), ())), preferred_element_type=F32)


def piece_copies(pieces, places, whole, sems, first):
    copies = []
    for number, (piece, (row, col)) in enumerate(zip(pieces, places)):
        rows, cols = piece.shape
        copies.append(
            pltpu.make_async_copy(
                piece, whole.at[pl.ds(row, rows), pl.ds(col, cols)], sems.at[first + number]
            )
        )
    return copies


def qkv_kernel(places_of, n_pieces, window_ref, *refs):
    pieces = refs[:n_pieces]
    pairs_ref, whole_ref, sems = refs[n_pieces:]

    @pl.when(pl.program_id(0) == 0)
    def _():
        copies = piece_copies(pieces, places_of(), whole_ref, sems, 0)
        for copy in copies:
            copy.start()
        for copy in copies:
            copy.wait()

    rows = window_ref[...]
    for third in range(3):
        width = 6 * BLOCK
        part = dot_nn(rows, whole_ref[:, third * width : (third + 1) * width]).astype(BF16)
        for pair in range(6):
            pairs_ref[third * 6 + pair] = part[:, pair * BLOCK : (pair + 1) * BLOCK]


def qkv_call(window, pieces, places_of):
    rows, width = window.shape
    tile = HALO
    return pl.pallas_call(
        functools.partial(qkv_kernel, places_of, len(pieces)),
        grid=(rows // tile,),
        in_specs=[pl.BlockSpec((tile, width), lambda i: (i, 0))]
        + [pl.BlockSpec(memory_space=pl.ANY)] * len(pieces),
        out_specs=[
            pl.BlockSpec((18, tile, BLOCK), lambda i: (0, i, 0)),
            pl.BlockSpec((width, 3 * width), lambda i: (0, 0)),
        ],
        out_shape=[
            jax.ShapeDtypeStruct((18, rows, BLOCK), BF16),
            jax.ShapeDtypeStruct((width, 3 * width), BF16),
        ],
        scratch_shapes=[pltpu.SemaphoreType.DMA((len(pieces),))],
        compiler_params=pltpu.CompilerParams(
            dimension_semantics=("arbitrary",), vmem_limit_bytes=32 * MIB
        ),
        cost_estimate=pl.CostEstimate(
            flops=2 * rows * width * 3 * width,
            bytes_accessed=2 * (rows * width * 4 + 6 * width * width),
            transcendentals=0,
        ),
        name="qkv",
    )(window, *pieces)


def run_of(ids_ref, block, count):
    own = ids_ref[block]

    def same(other):
        inside = jnp.logical_and(other >= 0, other < count)
        return jnp.logical_and(inside, ids_ref[jnp.clip(other, 0, count - 1)] == own)

    before = sum(same(block - step).astype(jnp.int32) for step in (1, 2, 3))
    after = sum(same(block + step).astype(jnp.int32) for step in (1, 2, 3))
    return block - before, before + after + 1


def halves_of(rows):
    lane = lax.broadcasted_iota(jnp.int32, rows.shape, 1)
    zero = jnp.zeros_like(rows)
    return jnp.concatenate(
        (jnp.where(lane < HEAD_DIM, rows, zero), jnp.where(lane < HEAD_DIM, zero, rows)), axis=0
    )


def fill_distances(table_ref):
    shape = table_ref.shape
    key = lax.broadcasted_iota(jnp.int32, shape, 0) - 3 * BLOCK
    query = lax.broadcasted_iota(jnp.int32, shape, 1)
    table_ref[...] = jnp.abs(key - query).astype(F32)


def biased_scores(keys, query_pair, distances, slope_one, slope_two):
    bias = jnp.concatenate((distances * slope_one, distances * slope_two), axis=1)
    return dot_nt(keys, query_pair) - bias


def untwine(both):
    mine = jnp.concatenate(
        (both[:HEAD_DIM, :BLOCK], both[HEAD_DIM:, BLOCK:]), axis=0
    )
    return mine.T


def attend_kernel(first_own, n_own, ids_ref, slopes_ref, q_ref, k_ref, v_ref, ctx_ref, lse_ref, table_ref):
    pair = pl.program_id(0)
    count = q_ref.shape[1] // BLOCK

    @pl.when(pair == 0)
    def _():
        fill_distances(table_ref)

    slope_one = slopes_ref[2 * pair]
    slope_two = slopes_ref[2 * pair + 1]

    def one_block(block, carry):
        start, length = run_of(ids_ref, block, count)
        own = jnp.logical_and(block >= first_own, block < first_own + n_own)
        active = jnp.logical_and(start < first_own + n_own, start + length > first_own)
        rows = pl.ds(pl.multiple_of(block * BLOCK, BLOCK), BLOCK)
        shift = pl.multiple_of((3 - (block - start)) * BLOCK, BLOCK)

        def variant(blocks):
            width = blocks * BLOCK
            span = pl.ds(pl.multiple_of(start * BLOCK, BLOCK), width)
            queries = halves_of(q_ref[0, rows, :] * jnp.asarray(HEAD_DIM**-0.5, BF16))
            scores = biased_scores(
                k_ref[0, span, :], queries, table_ref[pl.ds(shift, width), :], slope_one, slope_two
            )
            peak = jnp.max(scores, axis=0, keepdims=True)
            terms = jnp.exp(scores - peak)
            total = jnp.sum(terms, axis=0, keepdims=True)
            lse_ref[0, pl.ds(block, 1), :] = peak + jnp.log(total)

            @pl.when(own)
            def _():
                probs = (terms * (1.0 / total)).astype(BF16)
                both = dot_tn(v_ref[0, span, :], probs)
                place = pl.multiple_of((block - first_own) * BLOCK, BLOCK)
                ctx_ref[pl.ds(place, BLOCK), :] = untwine(both).astype(BF16)

        for blocks in (1, 2, 4):
            @pl.when(jnp.logical_and(active, length == blocks))
            def _(blocks=blocks):
                variant(blocks)

        return carry

    lax.fori_loop(0, count, one_block, 0)


def attend_call(ids, slopes, pairs, own_rows):
    rows = pairs.shape[1]
    count = rows // BLOCK
    width = HEADS * HEAD_DIM
    part = lambda third: pl.BlockSpec((1, rows, BLOCK), lambda p: (third * 6 + p, 0, 0))
    smem = pl.BlockSpec(memory_space=pltpu.SMEM)
    return pl.pallas_call(
        functools.partial(attend_kernel, HALO // BLOCK, own_rows // BLOCK),
        grid=(6,),
        in_specs=[smem, smem, part(0), part(1), part(2)],
        out_specs=[
            pl.BlockSpec((own_rows, BLOCK), lambda p: (0, p)),
            pl.BlockSpec((1, count, 2 * BLOCK), lambda p: (p, 0, 0)),
        ],
        out_shape=[
            jax.ShapeDtypeStruct((own_rows, width), BF16),
            jax.ShapeDtypeStruct((6, count, 2 * BLOCK), F32),
        ],
        scratch_shapes=[pltpu.VMEM((7 * BLOCK, BLOCK), F32)],
        compiler_params=pltpu.CompilerParams(
            dimension_semantics=("arbitrary",), vmem_limit_bytes=32 * MIB
        ),
        cost_estimate=pl.CostEstimate(
            flops=8 * 10**9, bytes_accessed=10 * 10**6, transcendentals=5 * 10**6
        ),
        name="attend",
    )(ids, slopes, pairs, pairs, pairs)


def attend_back_kernel(
    first_own, n_own, ids_ref, slopes_ref, q_ref, k_ref, v_ref, lse_ref, dctx_ref,
    dq_ref, dk_ref, dv_ref, table_ref, dk_sum, dv_sum,
):
    pair = pl.program_id(0)
    count = q_ref.shape[1] // BLOCK

    @pl.when(pair == 0)
    def _():
        fill_distances(table_ref)

    dk_sum[...] = jnp.zeros_like(dk_sum)
    dv_sum[...] = jnp.zeros_like(dv_sum)
    slope_one = slopes_ref[2 * pair]
    slope_two = slopes_ref[2 * pair + 1]

    def one_block(block, carry):
        start, length = run_of(ids_ref, block, count)
        own = jnp.logical_and(block >= first_own, block < first_own + n_own)
        active = jnp.logical_and(start < first_own + n_own, start + length > first_own)
        rows = pl.ds(pl.multiple_of(block * BLOCK, BLOCK), BLOCK)
        shift = pl.multiple_of((3 - (block - start)) * BLOCK, BLOCK)

        def variant(blocks):
            width = blocks * BLOCK
            span = pl.ds(pl.multiple_of(start * BLOCK, BLOCK), width)
            keys = k_ref[0, span, :]
            queries = halves_of(q_ref[0, rows, :] * jnp.asarray(HEAD_DIM**-0.5, BF16))
            scores = biased_scores(
                keys, queries, table_ref[pl.ds(shift, width), :], slope_one, slope_two
            )
            soft = jnp.exp(scores - lse_ref[0, pl.ds(block, 1), :])
            dctx = halves_of(dctx_ref[rows, :])
            dsoft = dot_nt(v_ref[0, span, :], dctx)
            dv_sum[span, :] += dot_nn(soft.astype(BF16), dctx)
            inner = jnp.sum(soft * dsoft, axis=0, keepdims=True)
            dscores = (soft * (dsoft - inner)).astype(BF16)
            dk_sum[span, :] += dot_nn(dscores, queries)

            @pl.when(own)
            def _():
                both = dot_tn(keys, dscores)
                place = pl.multiple_of((block - first_own) * BLOCK, BLOCK)
                dq_ref[pl.ds(place, BLOCK), :] = (untwine(both) * HEAD_DIM**-0.5).astype(BF16)

        for blocks in (1, 2, 4):
            @pl.when(jnp.logical_and(active, length == blocks))
            def _(blocks=blocks):
                variant(blocks)

        return carry

    lax.fori_loop(0, count, one_block, 0)
    mine = pl.ds(first_own * BLOCK, n_own * BLOCK)
    dk_ref[...] = dk_sum[mine, :].astype(BF16)
    dv_ref[...] = dv_sum[mine, :].astype(BF16)


def attend_back_call(ids, slopes, pairs, lse, dctx, own_rows):
    rows = pairs.shape[1]
    count = rows // BLOCK
    width = HEADS * HEAD_DIM
    part = lambda third: pl.BlockSpec((1, rows, BLOCK), lambda p: (third * 6 + p, 0, 0))
    smem = pl.BlockSpec(memory_space=pltpu.SMEM)
    return pl.pallas_call(
        functools.partial(attend_back_kernel, HALO // BLOCK, own_rows // BLOCK),
        grid=(6,),
        in_specs=[
            smem, smem, part(0), part(1), part(2),
            pl.BlockSpec((1, count, 2 * BLOCK), lambda p: (p, 0, 0)),
            pl.BlockSpec((rows, BLOCK), lambda p: (0, p)),
        ],
        out_specs=[pl.BlockSpec((own_rows, BLOCK), lambda p: (0, p))] * 3,
        out_shape=[jax.ShapeDtypeStruct((own_rows, width), BF16)] * 3,
        scratch_shapes=[
            pltpu.VMEM((7 * BLOCK, BLOCK), F32),
            pltpu.VMEM((rows, BLOCK), F32),
            pltpu.VMEM((rows, BLOCK), F32),
        ],
        compiler_params=pltpu.CompilerParams(
            dimension_semantics=("arbitrary",), vmem_limit_bytes=32 * MIB
        ),
        cost_estimate=pl.CostEstimate(
            flops=20 * 10**9, bytes_accessed=14 * 10**6, transcendentals=5 * 10**6
        ),
        name="attend_back",
    )(ids, slopes, pairs, pairs, pairs, lse, dctx)


FF_TILE = 512


def row_mean(values):
    return jnp.mean(values, axis=1, keepdims=True)


def norm_parts(values):
    center = values - row_mean(values)
    scale = lax.rsqrt(row_mean(center * center) + LN_EPS)
    return center * scale, scale


def norm_back(grad_unit, unit, scale):
    return scale * (grad_unit - row_mean(grad_unit) - unit * row_mean(grad_unit * unit))


def column_sum(values):
    return jnp.sum(values, axis=0, keepdims=True)


def middle_kernel(places_of, counts, ctx_ref, tok_ref, cot_ref, vec_ref, *refs):
    n_out, n_gu, n_down = counts
    n_pieces = sum(counts)
    pieces = refs[:n_pieces]
    (result_ref, hidden_ref, dgu_ref, dffn_ref, low_ref, dattn_ref, dfirst_ref, dctx_ref,
     sums_ref, w_out, w_gu, w_down, gate_grad, up_grad, sems) = refs[n_pieces:]
    step = pl.program_id(0)
    width = tok_ref.shape[1]
    ff = w_down.shape[0]

    def copies_of(which):
        place_out, place_gu, place_down = places_of()
        if which == 0:
            return piece_copies(pieces[:n_out], place_out, w_out, sems, 0)
        if which == 1:
            return piece_copies(pieces[n_out : n_out + n_gu], place_gu, w_gu, sems, n_out)
        return piece_copies(pieces[n_out + n_gu :], place_down, w_down, sems, n_out + n_gu)

    def wait_for(which):
        @pl.when(step == 0)
        def _():
            for copy in copies_of(which):
                copy.wait()

    @pl.when(step == 0)
    def _():
        sums_ref[...] = jnp.zeros_like(sums_ref)
        for which in range(3):
            for copy in copies_of(which):
                copy.start()

    gain_one, shift_one = vec_ref[0:1, :], vec_ref[1:2, :]
    gain_two, shift_two = vec_ref[2:3, :], vec_ref[3:4, :]
    wait_for(0)
    attn = dot_nn(ctx_ref[...], w_out[...])
    unit_one, scale_one = norm_parts(tok_ref[...].astype(F32) + attn + vec_ref[4:5, :])
    normed = unit_one * gain_one + shift_one
    low = normed.astype(BF16)
    low_ref[...] = low
    wait_for(1)
    wait_for(2)
    ffn = jnp.zeros((low.shape[0], width), F32)
    for tile in range(ff // FF_TILE):
        cols = slice(tile * FF_TILE, (tile + 1) * FF_TILE)
        gate = dot_nn(low, w_gu[:, cols])
        up = dot_nn(low, w_gu[:, ff + tile * FF_TILE : ff + (tile + 1) * FF_TILE])
        below = 0.5 + 0.5 * lax.erf(gate * np.float32(0.5**0.5))
        gelu = gate * below
        slope = below + gate * (jnp.exp(-0.5 * gate * gate) * np.float32((2.0 * np.pi) ** -0.5))
        hidden = (gelu * up).astype(BF16)
        hidden_ref[:, cols] = hidden
        gate_grad[:, cols] = up * slope
        up_grad[:, cols] = gelu
        ffn = ffn + dot_nn(hidden, w_down[cols, :])
    unit_two, scale_two = norm_parts(normed + ffn + vec_ref[5:6, :])
    result_ref[...] = (unit_two * gain_two + shift_two).astype(BF16)
    grad = cot_ref[...].astype(F32)
    sums_ref[2:3, :] += column_sum(grad * unit_two)
    sums_ref[3:4, :] += column_sum(grad)
    dsecond = norm_back(grad * gain_two, unit_two, scale_two)
    sums_ref[5:6, :] += column_sum(dsecond)
    dffn = dsecond.astype(BF16)
    dffn_ref[...] = dffn
    dnormed = dsecond
    for tile in range(ff // FF_TILE):
        cols = slice(tile * FF_TILE, (tile + 1) * FF_TILE)
        ups = slice(ff + tile * FF_TILE, ff + (tile + 1) * FF_TILE)
        dhidden = dot_nt(dffn, w_down[cols, :])
        dgate = (dhidden * gate_grad[:, cols]).astype(BF16)
        dup = (dhidden * up_grad[:, cols]).astype(BF16)
        dgu_ref[:, cols] = dgate
        dgu_ref[:, ups] = dup
        dnormed = dnormed + dot_nt(dgate, w_gu[:, cols]) + dot_nt(dup, w_gu[:, ups])
    sums_ref[0:1, :] += column_sum(dnormed * unit_one)
    sums_ref[1:2, :] += column_sum(dnormed)
    dfirst = norm_back(dnormed * gain_one, unit_one, scale_one)
    sums_ref[4:5, :] += column_sum(dfirst)
    dfirst_ref[...] = dfirst
    dattn = dfirst.astype(BF16)
    dattn_ref[...] = dattn
    dctx_ref[...] = dot_nt(dattn, w_out[...]).astype(BF16)


def middle_call(ctx, tokens, cotangent, vectors, pieces, places_of):
    rows, width = tokens.shape
    ff = 4 * width
    tile = 256
    by_rows = lambda cols: pl.BlockSpec((tile, cols), lambda i: (i, 0))
    counts = tuple(len(group) for group in pieces)
    flat = [piece for group in pieces for piece in group]
    shaped = lambda cols, dtype: jax.ShapeDtypeStruct((rows, cols), dtype)
    return pl.pallas_call(
        functools.partial(middle_kernel, places_of, counts),
        grid=(rows // tile,),
        in_specs=[by_rows(width)] * 3
        + [pl.BlockSpec((8, width), lambda i: (0, 0))]
        + [pl.BlockSpec(memory_space=pl.ANY)] * len(flat),
        out_specs=[
            by_rows(width), by_rows(ff), by_rows(2 * ff), by_rows(width), by_rows(width),
            by_rows(width), by_rows(width), by_rows(width),
            pl.BlockSpec((8, width), lambda i: (0, 0)),
        ],
        out_shape=[
            shaped(width, BF16), shaped(ff, BF16), shaped(2 * ff, BF16), shaped(width, BF16),
            shaped(width, BF16), shaped(width, BF16), shaped(width, F32), shaped(width, BF16),
            jax.ShapeDtypeStruct((8, width), F32),
        ],
        scratch_shapes=[
            pltpu.VMEM((width, width), BF16),
            pltpu.VMEM((width, 2 * ff), BF16),
            pltpu.VMEM((ff, width), BF16),
            pltpu.VMEM((tile, ff), F32),
            pltpu.VMEM((tile, ff), F32),
            pltpu.SemaphoreType.DMA((len(flat),)),
        ],
        compiler_params=pltpu.CompilerParams(
            dimension_semantics=("arbitrary",), vmem_limit_bytes=56 * MIB
        ),
        cost_estimate=pl.CostEstimate(
            flops=2 * 2 * rows * (width * width + 3 * ff * width),
            bytes_accessed=2 * (width * width + 3 * ff * width + 3 * rows * ff + 8 * rows * width),
            transcendentals=2 * rows * ff,
        ),
        name="middle",
    )(ctx, tokens, cotangent, vectors, *flat)


def adam_update(master, first_mom, second, grad_term, factor, step_rate, decay_rate):
    clipped = grad_term * factor
    first_new = BETA_ONE * first_mom + (1.0 - BETA_ONE) * clipped
    second_new = BETA_TWO * second + (1.0 - BETA_TWO) * clipped * clipped
    direction = first_new / CORR_ONE / (jnp.sqrt(second_new / CORR_TWO) + ADAM_EPS)
    master_new = master - step_rate * (direction + decay_rate * master)
    return (master_new, first_new, second_new, master_new.astype(jnp.bfloat16))


def halo_window(rows, groups):
    left = lax.ppermute(rows[-HALO:], "head", [(i, i + 1) for i in range(groups - 1)])
    right = lax.ppermute(rows[:HALO], "head", [(i + 1, i) for i in range(groups - 1)])
    return jnp.concatenate((left, rows, right), axis=0)


def whole_place():
    return [(0, 0)]


def body(
    tokens, segment_ids, cotangent, clip_norm,
    master_qkv, master_out, master_gu, master_down, master_vec,
    first_qkv, first_out, first_gu, first_down, first_vec,
    second_qkv, second_out, second_gu, second_down, second_vec,
):
    groups = lax.axis_size("head")
    own_rows, width = tokens.shape
    low = [w.astype(BF16) for w in (master_qkv, master_out, master_gu, master_down)]
    window = halo_window(tokens, groups)
    full = [lax.all_gather(w, "dp", axis=0, tiled=True) for w in low]
    full_vec = lax.all_gather(master_vec.astype(BF16), "dp", axis=1, tiled=True)
    vectors = jnp.pad(full_vec.astype(F32), ((0, 2), (0, 0)))
    slopes = jnp.asarray(np.array(SLOPES), F32)

    block_ids = segment_ids.reshape(-1, BLOCK)[:, 0]
    edge = HALO // BLOCK
    padded = jnp.pad(block_ids, (edge, edge), constant_values=-1)
    own_blocks = own_rows // BLOCK
    ids = lax.dynamic_slice_in_dim(
        padded, lax.axis_index("head") * own_blocks, own_blocks + 2 * edge
    )

    pairs, whole_qkv = qkv_call(window, [full[0]], whole_place)
    ctx, lse = attend_call(ids, slopes, pairs, own_rows)
    result, hidden, dgu, dffn, normed_low, dattn, dfirst, dctx, sums = middle_call(
        ctx, tokens, cotangent, vectors, [[full[1]], [full[2]], [full[3]]],
        lambda: [[(0, 0)], [(0, 0)], [(0, 0)]],
    )
    grad_down = dot_tn(hidden, dffn).astype(BF16)
    grad_gu = dot_tn(normed_low, dgu).astype(BF16)
    grad_out = dot_tn(ctx, dattn).astype(BF16)
    dctx_window = halo_window(dctx, groups)
    dq, dk, dv = attend_back_call(ids, slopes, pairs, lse, dctx_window, own_rows)
    djoined = jnp.concatenate((dq, dk, dv), axis=1)
    grad_qkv = dot_tn(tokens, djoined).astype(BF16)
    grad_input = dfirst + dot_nt(djoined, whole_qkv)

    def reduced(grad, axis):
        share = lax.psum_scatter(grad, "dp", scatter_dimension=axis, tiled=True)
        return lax.psum(share, "head").astype(F32)

    shards = [
        reduced(grad_qkv, 0), reduced(grad_out, 0), reduced(grad_gu, 0), reduced(grad_down, 0)
    ]
    vec_sum = lax.psum(sums[:6], ("dp", "head"))
    vec_cols = master_vec.shape[1]
    shards.append(
        lax.dynamic_slice_in_dim(vec_sum, lax.axis_index("dp") * vec_cols, vec_cols, axis=1)
    )
    squares = jnp.float32(0.0)
    for shard_piece in shards:
        squares = squares + jnp.sum(shard_piece * shard_piece)
    grad_norm = jnp.sqrt(lax.psum(squares, "dp"))
    factor = jnp.minimum(1.0, clip_norm[0] / grad_norm)
    masters = (master_qkv, master_out, master_gu, master_down, master_vec)
    firsts = (first_qkv, first_out, first_gu, first_down, first_vec)
    seconds = (second_qkv, second_out, second_gu, second_down, second_vec)
    updates = []
    for index in range(5):
        rate, decay = (RATE_MAT, DECAY_MAT) if index < 4 else (RATE_VEC, 0.0)
        updates.extend(
            adam_update(
                masters[index], firsts[index], seconds[index], shards[index], factor, rate, decay
            )
        )
    return (result, grad_input, *updates, grad_norm.reshape(1))


def solution(mesh):
    rows_split = P(("dp", "head"), None)
    mats, vecs = P("dp", None), P(None, "dp")
    state = (mats,) * 4 + (vecs,)
    in_specs = (rows_split, P("dp"), rows_split, P()) + state * 3
    out_specs = (rows_split, rows_split) + (mats,) * 16 + (vecs,) * 4 + (P(),)
    return jax.shard_map(body, mesh=mesh, in_specs=in_specs, out_specs=out_specs, check_vma=False)
```

```python
import functools

import jax
import jax.numpy as jnp
import numpy as np
from jax import lax
from jax.experimental import pallas as pl
from jax.experimental.pallas import tpu as pltpu
from jax.sharding import PartitionSpec as P

HEADS = 12
HEAD_DIM = 64
BLOCK = 128
HALO = 384
MIB = 1024 * 1024

SLOPES = [2.0 ** (-(level + 1)) for level in range(8)] + [
    2.0 ** (-(level + 0.5)) for level in range(4)
]
LN_EPS = 1e-05
BETA_ONE = 0.9
BETA_TWO = 0.999
ADAM_EPS = 1e-08
CORR_ONE = 1.0 - 0.9**10
CORR_TWO = 1.0 - 0.999**10
RATE_MAT = 0.05
RATE_VEC = 0.5
DECAY_MAT = 0.01

BF16 = jnp.bfloat16
F32 = jnp.float32


def dot_nn(left, right):
    return lax.dot_general(left, right, (((1,), (0,)), ((), ())), preferred_element_type=F32)


def dot_nt(left, right):
    return lax.dot_general(left, right, (((1,), (1,)), ((), ())), preferred_element_type=F32)


def dot_tn(left, right):
    return lax.dot_general(left, right, (((0,), (0,)), ((), ())), preferred_element_type=F32)


def part_copies(parts, plan, whole, sems, first):
    copies = []
    for number, (part, lead, row, rows, to_row, to_col) in enumerate(plan):
        source = parts[part] if lead is None else parts[part].at[lead]
        cols = source.shape[1]
        copies.append(
            pltpu.make_async_copy(
                source.at[pl.ds(row, rows), :],
                whole.at[pl.ds(to_row, rows), pl.ds(to_col, cols)],
                sems.at[first + number],
            )
        )
    return copies


def aligned(value, unit):
    return value if isinstance(value, int) else pl.multiple_of(value, unit)


def qkv_kernel(plan_of, n_pieces, window_ref, *refs):
    pieces = refs[:n_pieces]
    pairs_ref, whole_ref, sems = refs[n_pieces:]

    @pl.when(pl.program_id(0) == 0)
    def _():
        copies = part_copies(pieces, plan_of(), whole_ref, sems, 0)
        for copy in copies:
            copy.start()
        for copy in copies:
            copy.wait()

    rows = window_ref[...]
    for third in range(3):
        width = 6 * BLOCK
        part = dot_nn(rows, whole_ref[:, third * width : (third + 1) * width]).astype(BF16)
        for pair in range(6):
            pairs_ref[third * 6 + pair] = part[:, pair * BLOCK : (pair + 1) * BLOCK]


def qkv_call(window, pieces, plan_of, n_copies):
    rows, width = window.shape
    tile = HALO
    return pl.pallas_call(
        functools.partial(qkv_kernel, plan_of, len(pieces)),
        grid=(rows // tile,),
        in_specs=[pl.BlockSpec((tile, width), lambda i: (i, 0))]
        + [pl.BlockSpec(memory_space=pl.ANY)] * len(pieces),
        out_specs=[
            pl.BlockSpec((18, tile, BLOCK), lambda i: (0, i, 0)),
            pl.BlockSpec((width, 3 * width), lambda i: (0, 0)),
        ],
        out_shape=[
            jax.ShapeDtypeStruct((18, rows, BLOCK), BF16),
            jax.ShapeDtypeStruct((width, 3 * width), BF16),
        ],
        scratch_shapes=[pltpu.SemaphoreType.DMA((n_copies,))],
        compiler_params=pltpu.CompilerParams(
            dimension_semantics=("arbitrary",), vmem_limit_bytes=32 * MIB
        ),
        cost_estimate=pl.CostEstimate(
            flops=2 * rows * width * 3 * width,
            bytes_accessed=2 * (rows * width * 4 + 6 * width * width),
            transcendentals=0,
        ),
        name="qkv",
    )(window, *pieces)


def run_of(ids_ref, block, count):
    own = ids_ref[block]

    def same(other):
        inside = jnp.logical_and(other >= 0, other < count)
        return jnp.logical_and(inside, ids_ref[jnp.clip(other, 0, count - 1)] == own)

    before = sum(same(block - step).astype(jnp.int32) for step in (1, 2, 3))
    after = sum(same(block + step).astype(jnp.int32) for step in (1, 2, 3))
    return block - before, before + after + 1


def halves_of(rows):
    lane = lax.broadcasted_iota(jnp.int32, rows.shape, 1)
    zero = jnp.zeros_like(rows)
    return jnp.concatenate(
        (jnp.where(lane < HEAD_DIM, rows, zero), jnp.where(lane < HEAD_DIM, zero, rows)), axis=0
    )


def fill_distances(table_ref):
    shape = table_ref.shape
    key = lax.broadcasted_iota(jnp.int32, shape, 0) - 3 * BLOCK
    query = lax.broadcasted_iota(jnp.int32, shape, 1)
    table_ref[...] = jnp.abs(key - query).astype(F32)


def biased_scores(keys, query_pair, distances, slope_one, slope_two):
    bias = jnp.concatenate((distances * slope_one, distances * slope_two), axis=1)
    return dot_nt(keys, query_pair) - bias


def untwine(both):
    mine = jnp.concatenate(
        (both[:HEAD_DIM, :BLOCK], both[HEAD_DIM:, BLOCK:]), axis=0
    )
    return mine.T


def attend_kernel(first_own, n_own, ids_ref, slopes_ref, q_ref, k_ref, v_ref, ctx_ref, lse_ref, table_ref):
    pair = pl.program_id(0)
    count = q_ref.shape[1] // BLOCK

    @pl.when(pair == 0)
    def _():
        fill_distances(table_ref)

    slope_one = slopes_ref[2 * pair]
    slope_two = slopes_ref[2 * pair + 1]

    def one_block(block, carry):
        start, length = run_of(ids_ref, block, count)
        own = jnp.logical_and(block >= first_own, block < first_own + n_own)
        active = jnp.logical_and(start < first_own + n_own, start + length > first_own)
        rows = pl.ds(pl.multiple_of(block * BLOCK, BLOCK), BLOCK)
        shift = pl.multiple_of((3 - (block - start)) * BLOCK, BLOCK)

        def variant(blocks):
            width = blocks * BLOCK
            span = pl.ds(pl.multiple_of(start * BLOCK, BLOCK), width)
            queries = halves_of(q_ref[0, rows, :] * jnp.asarray(HEAD_DIM**-0.5, BF16))
            scores = biased_scores(
                k_ref[0, span, :], queries, table_ref[pl.ds(shift, width), :], slope_one, slope_two
            )
            peak = jnp.max(scores, axis=0, keepdims=True)
            terms = jnp.exp(scores - peak)
            total = jnp.sum(terms, axis=0, keepdims=True)
            lse_ref[0, pl.ds(block, 1), :] = peak + jnp.log(total)

            @pl.when(own)
            def _():
                probs = (terms * (1.0 / total)).astype(BF16)
                both = dot_tn(v_ref[0, span, :], probs)
                place = pl.multiple_of((block - first_own) * BLOCK, BLOCK)
                ctx_ref[pl.ds(place, BLOCK), :] = untwine(both).astype(BF16)

        for blocks in (1, 2, 4):
            @pl.when(jnp.logical_and(active, length == blocks))
            def _(blocks=blocks):
                variant(blocks)

        return carry

    lax.fori_loop(0, count, one_block, 0)


def attend_call(ids, slopes, pairs, own_rows):
    rows = pairs.shape[1]
    count = rows // BLOCK
    width = HEADS * HEAD_DIM
    part = lambda third: pl.BlockSpec((1, rows, BLOCK), lambda p: (third * 6 + p, 0, 0))
    smem = pl.BlockSpec(memory_space=pltpu.SMEM)
    return pl.pallas_call(
        functools.partial(attend_kernel, HALO // BLOCK, own_rows // BLOCK),
        grid=(6,),
        in_specs=[smem, smem, part(0), part(1), part(2)],
        out_specs=[
            pl.BlockSpec((own_rows, BLOCK), lambda p: (0, p)),
            pl.BlockSpec((1, count, 2 * BLOCK), lambda p: (p, 0, 0)),
        ],
        out_shape=[
            jax.ShapeDtypeStruct((own_rows, width), BF16),
            jax.ShapeDtypeStruct((6, count, 2 * BLOCK), F32),
        ],
        scratch_shapes=[pltpu.VMEM((7 * BLOCK, BLOCK), F32)],
        compiler_params=pltpu.CompilerParams(
            dimension_semantics=("arbitrary",), vmem_limit_bytes=32 * MIB
        ),
        cost_estimate=pl.CostEstimate(
            flops=8 * 10**9, bytes_accessed=10 * 10**6, transcendentals=5 * 10**6
        ),
        name="attend",
    )(ids, slopes, pairs, pairs, pairs)


def attend_back_kernel(
    first_own, n_own, first_pair, ids_ref, slopes_ref, q_ref, k_ref, v_ref, lse_ref, dctx_ref,
    dq_ref, dk_ref, dv_ref, table_ref, dk_sum, dv_sum,
):
    pair = first_pair + pl.program_id(0)
    count = q_ref.shape[1] // BLOCK

    @pl.when(pl.program_id(0) == 0)
    def _():
        fill_distances(table_ref)

    dk_sum[...] = jnp.zeros_like(dk_sum)
    dv_sum[...] = jnp.zeros_like(dv_sum)
    slope_one = slopes_ref[2 * pair]
    slope_two = slopes_ref[2 * pair + 1]

    def one_block(block, carry):
        start, length = run_of(ids_ref, block, count)
        own = jnp.logical_and(block >= first_own, block < first_own + n_own)
        active = jnp.logical_and(start < first_own + n_own, start + length > first_own)
        rows = pl.ds(pl.multiple_of(block * BLOCK, BLOCK), BLOCK)
        shift = pl.multiple_of((3 - (block - start)) * BLOCK, BLOCK)

        def variant(blocks):
            width = blocks * BLOCK
            span = pl.ds(pl.multiple_of(start * BLOCK, BLOCK), width)
            keys = k_ref[0, span, :]
            queries = halves_of(q_ref[0, rows, :] * jnp.asarray(HEAD_DIM**-0.5, BF16))
            scores = biased_scores(
                keys, queries, table_ref[pl.ds(shift, width), :], slope_one, slope_two
            )
            soft = jnp.exp(scores - lse_ref[0, pl.ds(block, 1), :])
            dctx = halves_of(dctx_ref[rows, :])
            dsoft = dot_nt(v_ref[0, span, :], dctx)
            dv_sum[span, :] += dot_nn(soft.astype(BF16), dctx)
            inner = jnp.sum(soft * dsoft, axis=0, keepdims=True)
            dscores = (soft * (dsoft - inner)).astype(BF16)
            dk_sum[span, :] += dot_nn(dscores, queries)

            @pl.when(own)
            def _():
                both = dot_tn(keys, dscores)
                place = pl.multiple_of((block - first_own) * BLOCK, BLOCK)
                dq_ref[pl.ds(place, BLOCK), :] = (untwine(both) * HEAD_DIM**-0.5).astype(BF16)

        for blocks in (1, 2, 4):
            @pl.when(jnp.logical_and(active, length == blocks))
            def _(blocks=blocks):
                variant(blocks)

        return carry

    lax.fori_loop(0, count, one_block, 0)
    mine = pl.ds(first_own * BLOCK, n_own * BLOCK)
    dk_ref[...] = dk_sum[mine, :].astype(BF16)
    dv_ref[...] = dv_sum[mine, :].astype(BF16)


def attend_back_call(ids, slopes, pairs, lse, dctx, own_rows, first_pair, n_pairs):
    rows = pairs.shape[1]
    count = rows // BLOCK
    part = lambda third: pl.BlockSpec(
        (1, rows, BLOCK), lambda p: (third * 6 + first_pair + p, 0, 0)
    )
    smem = pl.BlockSpec(memory_space=pltpu.SMEM)
    return pl.pallas_call(
        functools.partial(attend_back_kernel, HALO // BLOCK, own_rows // BLOCK, first_pair),
        grid=(n_pairs,),
        in_specs=[
            smem, smem, part(0), part(1), part(2),
            pl.BlockSpec((1, count, 2 * BLOCK), lambda p: (first_pair + p, 0, 0)),
            pl.BlockSpec((rows, BLOCK), lambda p: (0, first_pair + p)),
        ],
        out_specs=[pl.BlockSpec((own_rows, BLOCK), lambda p: (0, p))] * 3,
        out_shape=[jax.ShapeDtypeStruct((own_rows, n_pairs * BLOCK), BF16)] * 3,
        scratch_shapes=[
            pltpu.VMEM((7 * BLOCK, BLOCK), F32),
            pltpu.VMEM((rows, BLOCK), F32),
            pltpu.VMEM((rows, BLOCK), F32),
        ],
        compiler_params=pltpu.CompilerParams(
            dimension_semantics=("arbitrary",), vmem_limit_bytes=32 * MIB
        ),
        cost_estimate=pl.CostEstimate(
            flops=n_pairs * 4 * 10**9, bytes_accessed=n_pairs * 2 * 10**6,
            transcendentals=n_pairs * 10**6,
        ),
        name="attend_back",
    )(ids, slopes, pairs, pairs, pairs, lse, dctx)


FF_TILE = 512


def row_mean(values):
    return jnp.mean(values, axis=1, keepdims=True)


def norm_parts(values):
    center = values - row_mean(values)
    scale = lax.rsqrt(row_mean(center * center) + LN_EPS)
    return center * scale, scale


def norm_back(grad_unit, unit, scale):
    return scale * (grad_unit - row_mean(grad_unit) - unit * row_mean(grad_unit * unit))


def column_sum(values):
    return jnp.sum(values, axis=0, keepdims=True)


def middle_kernel(plans_of, slot_of, counts, n_pieces, ctx_ref, tok_ref, cot_ref, vec_ref, *refs):
    pieces = refs[:n_pieces]
    (result_ref, hidden_ref, dgu_ref, dffn_ref, low_ref, dattn_ref, dfirst_ref, dctx_ref,
     sums_ref, w_out, w_gu, w_down, gate_grad, up_grad, sems) = refs[n_pieces:]
    step = pl.program_id(0)
    width = tok_ref.shape[1]
    half = width // 2
    ff = w_down.shape[0]
    slot = slot_of()

    def copies_of(which):
        target = (w_out, w_gu, w_down)[which]
        return part_copies(pieces, plans_of()[which], target, sems, sum(counts[:which]))

    def wait_for(which):
        @pl.when(step == 0)
        def _():
            for copy in copies_of(which):
                copy.wait()

    @pl.when(step == 0)
    def _():
        sums_ref[...] = jnp.zeros_like(sums_ref)
        for which in range(3):
            for copy in copies_of(which):
                copy.start()

    gain_one, shift_one = vec_ref[0:1, :], vec_ref[1:2, :]
    gain_two, shift_two = vec_ref[2:3, :], vec_ref[3:4, :]
    wait_for(0)
    attn = dot_nn(ctx_ref[...], w_out[...])
    unit_one, scale_one = norm_parts(tok_ref[...].astype(F32) + attn + vec_ref[4:5, :])
    normed = unit_one * gain_one + shift_one
    low = normed.astype(BF16)
    low_ref[...] = low
    wait_for(1)
    wait_for(2)
    ffn = jnp.zeros((low.shape[0], width), F32)
    for tile in range(ff // FF_TILE):
        cols = slice(tile * FF_TILE, (tile + 1) * FF_TILE)
        gate = dot_nn(low, w_gu[:, cols])
        up = dot_nn(low, w_gu[:, ff + tile * FF_TILE : ff + (tile + 1) * FF_TILE])
        below = 0.5 + 0.5 * lax.erf(gate * np.float32(0.5**0.5))
        gelu = gate * below
        slope = below + gate * (jnp.exp(-0.5 * gate * gate) * np.float32((2.0 * np.pi) ** -0.5))
        hidden = (gelu * up).astype(BF16)
        hidden_ref[:, cols] = hidden
        gate_grad[:, cols] = up * slope
        up_grad[:, cols] = gelu
        ffn = ffn + dot_nn(hidden, w_down[cols, :])
    unit_two, scale_two = norm_parts(normed + ffn + vec_ref[5:6, :])
    result_ref[...] = (unit_two * gain_two + shift_two).astype(BF16)
    grad = cot_ref[...].astype(F32)
    sums_ref[2:3, :] += column_sum(grad * unit_two)
    sums_ref[3:4, :] += column_sum(grad)
    dsecond = norm_back(grad * gain_two, unit_two, scale_two)
    sums_ref[5:6, :] += column_sum(dsecond)
    dffn = dsecond.astype(BF16)
    dffn_ref[slot] = dffn[:, :half]
    dffn_ref[1 - slot] = dffn[:, half:]
    dnormed = dsecond
    for tile in range(ff // FF_TILE):
        cols = slice(tile * FF_TILE, (tile + 1) * FF_TILE)
        ups = slice(ff + tile * FF_TILE, ff + (tile + 1) * FF_TILE)
        dhidden = dot_nt(dffn, w_down[cols, :])
        dgate = (dhidden * gate_grad[:, cols]).astype(BF16)
        dup = (dhidden * up_grad[:, cols]).astype(BF16)
        dgu_ref[slot, :, cols] = dgate
        dgu_ref[1 - slot, :, cols] = dup
        dnormed = dnormed + dot_nt(dgate, w_gu[:, cols]) + dot_nt(dup, w_gu[:, ups])
    sums_ref[0:1, :] += column_sum(dnormed * unit_one)
    sums_ref[1:2, :] += column_sum(dnormed)
    dfirst = norm_back(dnormed * gain_one, unit_one, scale_one)
    sums_ref[4:5, :] += column_sum(dfirst)
    dfirst_ref[...] = dfirst
    dattn = dfirst.astype(BF16)
    dattn_ref[slot] = dattn[:, :half]
    dattn_ref[1 - slot] = dattn[:, half:]
    dctx_ref[...] = dot_nt(dattn, w_out[...]).astype(BF16)


def middle_call(ctx, tokens, cotangent, vectors, pieces, plans_of, slot_of, counts):
    rows, width = tokens.shape
    ff = 4 * width
    tile = 256
    by_rows = lambda cols: pl.BlockSpec((tile, cols), lambda i: (i, 0))
    paired = lambda cols: pl.BlockSpec((2, tile, cols), lambda i: (0, i, 0))
    shaped = lambda cols, dtype: jax.ShapeDtypeStruct((rows, cols), dtype)
    return pl.pallas_call(
        functools.partial(middle_kernel, plans_of, slot_of, counts, len(pieces)),
        grid=(rows // tile,),
        in_specs=[by_rows(width)] * 3
        + [pl.BlockSpec((8, width), lambda i: (0, 0))]
        + [pl.BlockSpec(memory_space=pl.ANY)] * len(pieces),
        out_specs=[
            by_rows(width), by_rows(ff), paired(ff), paired(width // 2), by_rows(width),
            paired(width // 2), by_rows(width), by_rows(width),
            pl.BlockSpec((8, width), lambda i: (0, 0)),
        ],
        out_shape=[
            shaped(width, BF16), shaped(ff, BF16), jax.ShapeDtypeStruct((2, rows, ff), BF16),
            jax.ShapeDtypeStruct((2, rows, width // 2), BF16), shaped(width, BF16),
            jax.ShapeDtypeStruct((2, rows, width // 2), BF16), shaped(width, F32),
            shaped(width, BF16),
            jax.ShapeDtypeStruct((8, width), F32),
        ],
        scratch_shapes=[
            pltpu.VMEM((width, width), BF16),
            pltpu.VMEM((width, 2 * ff), BF16),
            pltpu.VMEM((ff, width), BF16),
            pltpu.VMEM((tile, ff), F32),
            pltpu.VMEM((tile, ff), F32),
            pltpu.SemaphoreType.DMA((sum(counts),)),
        ],
        compiler_params=pltpu.CompilerParams(
            dimension_semantics=("arbitrary",), vmem_limit_bytes=56 * MIB
        ),
        cost_estimate=pl.CostEstimate(
            flops=2 * 2 * rows * (width * width + 3 * ff * width),
            bytes_accessed=2 * (width * width + 3 * ff * width + 3 * rows * ff + 8 * rows * width),
            transcendentals=2 * rows * ff,
        ),
        name="middle",
    )(ctx, tokens, cotangent, vectors, *pieces)


def adam_kernel(factor_ref, *refs):
    masters, firsts, seconds, grads, outs = (
        refs[:5], refs[5:10], refs[10:15], refs[15:20], refs[20:]
    )
    factor = factor_ref[0]
    for index in range(5):
        rate, decay = (RATE_MAT, DECAY_MAT) if index < 4 else (RATE_VEC, 0.0)
        new_ref, first_ref, second_ref, copy_ref = outs[4 * index : 4 * index + 4]
        master = masters[index][...]
        clipped = grads[index][...].astype(F32) * factor
        first = BETA_ONE * firsts[index][...] + (1.0 - BETA_ONE) * clipped
        second = BETA_TWO * seconds[index][...] + (1.0 - BETA_TWO) * clipped * clipped
        direction = first / CORR_ONE / (jnp.sqrt(second / CORR_TWO) + ADAM_EPS)
        new = master - rate * (direction + decay * master)
        new_ref[...] = new
        first_ref[...] = first
        second_ref[...] = second
        copy_ref[...] = new.astype(BF16)


def adam_call(masters, firsts, seconds, grads, factor):
    steps = 6

    def spec(array, index):
        rows, cols = array.shape
        if index == 4:
            return pl.BlockSpec((rows, cols), lambda i: (0, 0))
        return pl.BlockSpec((rows, cols // steps), lambda i: (0, i))

    specs = [spec(array, index) for index, array in enumerate(masters)]
    return pl.pallas_call(
        adam_kernel,
        grid=(steps,),
        in_specs=[pl.BlockSpec(memory_space=pltpu.SMEM)] + specs * 4,
        out_specs=[one for one in specs for _ in range(4)],
        out_shape=[
            jax.ShapeDtypeStruct(array.shape, dtype)
            for array in masters
            for dtype in (F32, F32, F32, BF16)
        ],
        compiler_params=pltpu.CompilerParams(
            dimension_semantics=("arbitrary",), vmem_limit_bytes=40 * MIB
        ),
        cost_estimate=pl.CostEstimate(
            flops=20 * sum(array.size for array in masters),
            bytes_accessed=28 * sum(array.size for array in masters),
            transcendentals=2 * sum(array.size for array in masters),
        ),
        name="adam",
    )(factor, *masters, *firsts, *seconds, *grads)


def halo_window(rows, groups):
    left = lax.ppermute(rows[-HALO:], "head", [(i, i + 1) for i in range(groups - 1)])
    right = lax.ppermute(rows[:HALO], "head", [(i + 1, i) for i in range(groups - 1)])
    return jnp.concatenate((left, rows, right), axis=0)


def slope_table():
    return jnp.asarray(np.array(SLOPES), F32)


def window_ids(segment_ids, own_rows):
    block_ids = segment_ids.reshape(-1, BLOCK)[:, 0]
    edge = HALO // BLOCK
    padded = jnp.pad(block_ids, (edge, edge), constant_values=-1)
    own_blocks = own_rows // BLOCK
    return lax.dynamic_slice_in_dim(
        padded, lax.axis_index("head") * own_blocks, own_blocks + 2 * edge
    )


def updated(masters, firsts, seconds, shards, grad_norm, clip_norm):
    factor = jnp.minimum(1.0, clip_norm / grad_norm)
    return adam_call(masters, firsts, seconds, shards, factor)


def plain_body(tokens, segment_ids, cotangent, clip_norm, *state):
    masters, firsts, seconds = state[:5], state[5:10], state[10:]
    groups = lax.axis_size("head")
    own_rows, width = tokens.shape
    low = [w.astype(BF16) for w in masters]
    window = halo_window(tokens, groups)
    full = [lax.all_gather(w, "dp", axis=0, tiled=True) for w in low[:4]]
    full_vec = lax.all_gather(low[4], "dp", axis=1, tiled=True)
    vectors = jnp.pad(full_vec.astype(F32), ((0, 2), (0, 0)))
    slopes = slope_table()
    ids = window_ids(segment_ids, own_rows)

    def whole_plan(part, rows):
        return [(part, None, 0, rows, 0, 0)]

    pairs, whole_qkv = qkv_call(window, [full[0]], lambda: whole_plan(0, width), 1)
    ctx, lse = attend_call(ids, slopes, pairs, own_rows)
    result, hidden, dgu, dffn, normed_low, dattn, dfirst, dctx, sums = middle_call(
        ctx, tokens, cotangent, vectors, full[1:],
        lambda: (whole_plan(0, width), whole_plan(1, width), whole_plan(2, 4 * width)),
        lambda: 0, (1, 1, 1),
    )
    joined_back = lambda two: jnp.concatenate((two[0], two[1]), axis=1)
    grad_down = dot_tn(hidden, joined_back(dffn)).astype(BF16)
    grad_gu = dot_tn(normed_low, joined_back(dgu)).astype(BF16)
    grad_out = dot_tn(ctx, joined_back(dattn)).astype(BF16)
    dctx_window = halo_window(dctx, groups)
    dq, dk, dv = attend_back_call(ids, slopes, pairs, lse, dctx_window, own_rows, 0, 6)
    djoined = jnp.concatenate((dq, dk, dv), axis=1)
    grad_qkv = dot_tn(tokens, djoined).astype(BF16)
    grad_input = dfirst + dot_nt(djoined, whole_qkv)

    def reduced(grad):
        share = lax.psum_scatter(grad, "dp", scatter_dimension=0, tiled=True)
        return lax.psum(share, "head").astype(F32)

    shards = [reduced(grad) for grad in (grad_qkv, grad_out, grad_gu, grad_down)]
    vec_sum = lax.psum(sums[:6], ("dp", "head"))
    vec_cols = masters[4].shape[1]
    shards.append(
        lax.dynamic_slice_in_dim(vec_sum, lax.axis_index("dp") * vec_cols, vec_cols, axis=1)
    )
    squares = sum(jnp.sum(piece * piece) for piece in shards)
    grad_norm = jnp.sqrt(lax.psum(squares, "dp")).reshape(1)
    updates = updated(masters, firsts, seconds, shards, grad_norm, clip_norm)
    return (result, grad_input, *updates, grad_norm)


SWAP_CORE = ("head", [(i, i ^ 1) for i in range(4)])
SWAP_X = ("head", [(i, i ^ 2) for i in range(4)])
SWAP_Y = ("dp", [(i, i ^ 1) for i in range(8)])
SWAP_Z = [None] + [("dp", [(i, i ^ (2 * step)) for i in range(8)]) for step in (1, 2, 3)]


def swap(values, how):
    return lax.ppermute(values, *how)


def position():
    dp, head = lax.axis_index("dp"), lax.axis_index("head")
    return dp // 2, dp % 2, head // 2, head % 2


def z_others(z):
    return (z + 1 - 2 * (z % 2), (z + 2) % 4, 3 - z)


def dp_order(z, y):
    others = z_others(z)
    first = [z * 2 + y, z * 2 + 1 - y]
    return first + [other * 2 + y for other in others] + [other * 2 + 1 - y for other in others]


def half_of(values, which, axis):
    size = values.shape[axis] // 2
    return lax.dynamic_slice_in_dim(values, which * size, size, axis)


def spread_z(mine):
    return [swap(mine, SWAP_Z[step]) for step in (1, 2, 3)]


def tied(values, after):
    return lax.optimization_barrier((values, *after))[0]


def together(*values):
    return lax.optimization_barrier(values)


def slab_sum(mine, other):
    return (mine.astype(F32) + other.astype(F32)).astype(BF16)


def pick(values, index):
    return lax.dynamic_index_in_dim(values, index, 0, keepdims=False)


def ordered(mine, other, which, axis):
    return jnp.where(
        which == 0,
        jnp.concatenate((mine, other), axis=axis),
        jnp.concatenate((other, mine), axis=axis),
    )


def cube_body(tokens, segment_ids, cotangent, clip_norm, *state):
    masters, firsts, seconds = state[:5], state[5:10], state[10:]
    groups = lax.axis_size("head")
    own_rows, width = tokens.shape
    ff = 4 * width
    half = width // 2
    shard = width // 8
    z, y, x, core = position()
    low = [w.astype(BF16) for w in masters]

    mine_qkv = half_of(low[0], core, 1)
    all_qkv = lax.all_gather(mine_qkv, "dp", axis=0, tiled=False)

    mine_gu = half_of(half_of(low[2], core, 1), x, 0)
    z_gu = spread_z(mine_gu)
    y_gu = swap(mine_gu, SWAP_Y)
    x_gu = swap(mine_gu, SWAP_X)
    mine_gu, y_gu, x_gu, *z_gu = together(mine_gu, y_gu, x_gu, *z_gu)

    vec_rows = jnp.pad(low[4], ((0, 10), (0, half - shard)))
    mine_rest = jnp.concatenate((half_of(low[3], core, 1), half_of(low[1], core, 1), vec_rows), axis=0)
    rest_rows = mine_rest.shape[0]
    mine_rest = tied(mine_rest, (y_gu,))
    all_rest = lax.all_gather(mine_rest, "dp", axis=0, tiled=False)

    near_gu = jnp.concatenate((y_gu, *z_gu), axis=0)
    far_gu = swap(near_gu[shard // 2 :], SWAP_Y)
    near_x_gu = swap(near_gu, SWAP_X)
    window = halo_window(tokens, groups)
    far_gu, all_qkv, window = together(far_gu, all_qkv, window)
    other_qkv = swap(all_qkv, SWAP_CORE)

    def qkv_plan():
        core = position()[3]
        plan = []
        for swapped in (0, 1):
            col = aligned((core + swapped * (1 - 2 * core)) * (3 * half), BLOCK)
            plan += [(swapped, dp, 0, shard, dp * shard, col) for dp in range(8)]
        return plan

    def middle_plans():
        z, y, x, core = position()
        order = dp_order(z, y)
        out_plan, gu_plan, down_plan = [], [], []
        for swapped in (0, 1):
            side = core + swapped * (1 - 2 * core)
            for dp in range(8):
                col = aligned(side * half, BLOCK)
                out_plan.append((12 + swapped, dp, ff // 8, shard, dp * shard, col))
                down_plan.append((12 + swapped, dp, 0, ff // 8, dp * (ff // 8), col))
            for flipped in (0, 1):
                rows_half = x + flipped * (1 - 2 * x)
                for number, dp in enumerate(order):
                    places = ((0, 0), (1, 0), (1, 1), (1, 2), (1, 3), (2, 0), (2, 1), (2, 2))
                    part, index = places[number]
                    row = aligned(dp * shard + rows_half * (shard // 2), 16)
                    gu_plan.append(
                        (6 * swapped + 3 * flipped + part, None, index * (shard // 2), shard // 2, row,
                         aligned(side * ff, BLOCK))
                    )
        return out_plan, gu_plan, down_plan

    slopes = slope_table()
    ids = window_ids(segment_ids, own_rows)
    pairs, whole_qkv = qkv_call(window, [all_qkv, other_qkv], qkv_plan, 16)
    pairs, near_x_gu = together(pairs, near_x_gu)
    ctx, lse = attend_call(ids, slopes, pairs, own_rows)
    far_x_gu = swap(far_gu, SWAP_X)
    parts_gu = [mine_gu, near_gu, far_gu, x_gu, near_x_gu]
    swapped_gu = [swap(part, SWAP_CORE) for part in parts_gu]
    ctx, lse, far_x_gu, all_rest, *swapped_gu = together(ctx, lse, far_x_gu, all_rest, *swapped_gu)
    parts_gu = parts_gu + [far_x_gu] + swapped_gu + [swap(far_x_gu, SWAP_CORE)]
    other_rest = swap(all_rest, SWAP_CORE)
    vec_all = all_rest[:, rest_rows - 16 : rest_rows - 8, :shard].astype(F32)
    vectors = vec_all.transpose(1, 0, 2).reshape(8, width)
    result, hidden, dgu, dffn, normed_low, dattn, dfirst, dctx, sums = middle_call(
        ctx, tokens, cotangent, vectors, parts_gu + [all_rest, other_rest],
        middle_plans, lambda: position()[3], (16, 32, 16),
    )

    def core_send(left, right):
        return swap(dot_tn(left, right[1]).astype(BF16), SWAP_CORE)

    def core_keep(left, right, theirs):
        return (dot_tn(left, right[0]) + theirs.astype(F32)).astype(BF16)

    their_gu = core_send(normed_low, dgu)
    dctx_window = halo_window(dctx, groups)
    their_down = core_send(hidden, dffn)
    their_out = core_send(ctx, dattn)
    vec_low = sums.astype(BF16)
    their_vec = swap(vec_low, SWAP_CORE)
    their_gu, their_down, their_out, their_vec, dctx_window = together(
        their_gu, their_down, their_out, their_vec, dctx_window
    )
    vec_cols = jnp.pad(slab_sum(vec_low, their_vec).T, ((0, 0), (0, BLOCK - 8)))
    sum_down = core_keep(hidden, dffn, their_down)
    sum_gu = core_keep(normed_low, dgu, their_gu)
    sum_out = core_keep(ctx, dattn, their_out)

    first_cols = ff // 2
    by_x = sum_gu[:, :first_cols].reshape(8, 2, shard // 2, first_cols)
    one_x = lax.dynamic_index_in_dim(by_x, x, 1, keepdims=False)
    one_away = lax.dynamic_index_in_dim(by_x, 1 - x, 1, keepdims=False)
    two = jnp.concatenate((sum_gu[:, first_cols:], sum_out, vec_cols), axis=1)
    two = two.reshape(4, 2, shard, two.shape[1])
    two_y = lax.dynamic_index_in_dim(two, y, 1, keepdims=False)
    two_away = lax.dynamic_index_in_dim(two, 1 - y, 1, keepdims=False)
    share_down = lax.psum_scatter(sum_down, "dp", scatter_dimension=0, tiled=True)

    def z_send(values, z):
        return [swap(pick(values, place), SWAP_Z[step]) for step, place in zip((1, 2, 3), z_others(z))]

    def z_keep(values, theirs, z):
        total = pick(values, z).astype(F32)
        for other in theirs:
            total = total + other.astype(F32)
        return total.astype(BF16)

    def split_y(values):
        values = values.reshape(4, 2, *values.shape[1:])
        return (
            lax.dynamic_index_in_dim(values, y, 1, keepdims=False),
            lax.dynamic_index_in_dim(values, 1 - y, 1, keepdims=False),
        )

    def back_part(first_pair, wait_for):
        return attend_back_call(
            ids, slopes, tied(pairs, wait_for), lse, dctx_window, own_rows, first_pair, 3
        )

    def qkv_sum(back):
        grad = dot_tn(tokens, jnp.concatenate(back, axis=1)).astype(BF16)
        grad = grad.reshape(8, 2, shard // 2, grad.shape[1])
        theirs = swap(lax.dynamic_index_in_dim(grad, 1 - core, 1, keepdims=False), SWAP_CORE)
        return slab_sum(lax.dynamic_index_in_dim(grad, core, 1, keepdims=False), theirs)

    one_their = swap(one_away, SWAP_X)
    two_their = swap(two_away, SWAP_Y)
    back_a = back_part(0, (one_away, two_away, sum_down))
    one_their, two_their, *back_a = together(one_their, two_their, *back_a)
    a_y, a_away = split_y(qkv_sum(back_a))
    one_y, one_away = split_y(slab_sum(one_x, one_their))
    two_y = slab_sum(two_y, two_their)
    one_their = swap(one_away, SWAP_Y)
    two_their = z_send(two_y, z)
    a_their = swap(a_away, SWAP_Y)
    back_b = back_part(3, (a_away, one_away, two_y))
    one_their, a_their, *rest = together(one_their, a_their, *two_their, *back_b)
    two_their, back_b = rest[:3], rest[3:]
    b_y, b_away = split_y(qkv_sum(back_b))
    one_y = slab_sum(one_y, one_their)
    a_y = slab_sum(a_y, a_their)
    two_z = z_keep(two_y, two_their, z)
    b_their = swap(b_away, SWAP_Y)
    one_their = z_send(one_y, z)
    a_their = z_send(a_y, z)
    two_their = swap(two_z, SWAP_X)
    djoined = jnp.concatenate([piece for pair in zip(back_a, back_b) for piece in pair], axis=1)
    grad_input = dfirst + dot_nt(djoined, whole_qkv)
    b_their, two_their, share_down, grad_input, *rest = together(
        b_their, two_their, share_down, grad_input, *one_their, *a_their
    )
    one_their, a_their = rest[:3], rest[3:]
    b_y = slab_sum(b_y, b_their)
    one_z = z_keep(one_y, one_their, z)
    a_z = z_keep(a_y, a_their, z)
    b_their = z_send(b_y, z)
    one_their = swap(one_z, SWAP_X)
    a_their = swap(a_z, SWAP_X)
    down_their = swap(share_down, SWAP_X)
    one_their, a_their, down_their, *b_their = together(one_their, a_their, down_their, *b_their)
    b_z = z_keep(b_y, b_their, z)
    b_their = swap(b_z, SWAP_X)
    share_down = slab_sum(share_down, down_their)
    ab = jnp.concatenate((slab_sum(a_z, a_their), slab_sum(b_z, b_their)), axis=1)
    share_qkv = ordered(ab, swap(ab, SWAP_CORE), core, 0)
    share_qkv = share_qkv.reshape(shard, 2, 3, half).transpose(0, 2, 1, 3).reshape(shard, 3 * width)
    two_sum = slab_sum(two_z, two_their)
    gu_two, share_out, share_vec = (
        two_sum[:, :first_cols], two_sum[:, first_cols : first_cols + half], two_sum[:, first_cols + half :]
    )
    gu_one = ordered(one_z, one_their, x, 0)

    def both_cores(mine):
        return ordered(mine, swap(mine, SWAP_CORE), core, 1)

    shards = [
        share_qkv,
        both_cores(share_out),
        both_cores(jnp.concatenate((gu_one, gu_two), axis=1)),
        both_cores(share_down),
        share_vec[:, :6].T,
    ]
    squares = sum(jnp.sum(jnp.square(piece.astype(F32))) for piece in shards).reshape(1, 1)
    for how in (SWAP_Y, SWAP_Z[1], SWAP_Z[2]):
        squares = squares + swap(squares, how)
    grad_norm = jnp.sqrt(squares[0])
    updates = updated(masters, firsts, seconds, shards, grad_norm, clip_norm)
    return (result, grad_input, *updates, grad_norm)


def solution(mesh):
    rows_split = P(("dp", "head"), None)
    mats, vecs = P("dp", None), P(None, "dp")
    state = (mats,) * 4 + (vecs,)
    in_specs = (rows_split, P("dp"), rows_split, P()) + state * 3
    out_specs = (rows_split, rows_split) + (mats,) * 16 + (vecs,) * 4 + (P(),)
    cube = mesh.shape["dp"] == 8 and mesh.shape["head"] == 4
    body = cube_body if cube else plain_body
    return jax.shard_map(body, mesh=mesh, in_specs=in_specs, out_specs=out_specs, check_vma=False)
```

```python
import functools

import jax
import jax.numpy as jnp
import numpy as np
from jax import lax
from jax.experimental import pallas as pl
from jax.experimental.pallas import tpu as pltpu
from jax.sharding import PartitionSpec as P

HEADS = 12
HEAD_DIM = 64
BLOCK = 128
HALO = 384
VMEM_GRANT = 60 * 1024 * 1024

SLOPES = [2.0 ** (-(level + 1)) for level in range(8)] + [
    2.0 ** (-(level + 0.5)) for level in range(4)
]
LN_EPS = 1e-05
BETA_ONE = 0.9
BETA_TWO = 0.999
ADAM_EPS = 1e-08
CORR_ONE = 1.0 - 0.9**10
CORR_TWO = 1.0 - 0.999**10
RATE_MAT = 0.05
RATE_VEC = 0.5
DECAY_MAT = 0.01

SHORT = pl.CostEstimate(flops=1000, bytes_accessed=1000, transcendentals=0)

BF16 = jnp.bfloat16
F32 = jnp.float32


def dot_nn(left, right):
    return lax.dot_general(left, right, (((1,), (0,)), ((), ())), preferred_element_type=F32)


def dot_nt(left, right):
    return lax.dot_general(left, right, (((1,), (1,)), ((), ())), preferred_element_type=F32)


def dot_tn(left, right):
    return lax.dot_general(left, right, (((0,), (0,)), ((), ())), preferred_element_type=F32)


def part_copies(parts, plan, whole, sems, first):
    copies = []
    for number, (part, lead, row, rows, to_row, to_col) in enumerate(plan):
        source = parts[part] if lead is None else parts[part].at[lead]
        cols = source.shape[1]
        copies.append(
            pltpu.make_async_copy(
                source.at[pl.ds(row, rows), :],
                whole.at[pl.ds(to_row, rows), pl.ds(to_col, cols)],
                sems.at[first + number],
            )
        )
    return copies


def aligned(value, unit):
    return value if isinstance(value, int) else pl.multiple_of(value, unit)


def qkv_kernel(plan_of, n_pieces, window_ref, *refs):
    pieces = refs[:n_pieces]
    pairs_ref, whole_ref, sems = refs[n_pieces:]

    @pl.when(pl.program_id(0) == 0)
    def _():
        copies = part_copies(pieces, plan_of(), whole_ref, sems, 0)
        for copy in copies:
            copy.start()
        for copy in copies:
            copy.wait()

    rows = window_ref[...]
    for third in range(3):
        width = 6 * BLOCK
        part = dot_nn(rows, whole_ref[:, third * width : (third + 1) * width]).astype(BF16)
        for pair in range(6):
            pairs_ref[third * 6 + pair] = part[:, pair * BLOCK : (pair + 1) * BLOCK]


def qkv_call(window, pieces, plan_of, n_copies):
    rows, width = window.shape
    tile = HALO
    return pl.pallas_call(
        functools.partial(qkv_kernel, plan_of, len(pieces)),
        grid=(rows // tile,),
        in_specs=[pl.BlockSpec((tile, width), lambda i: (i, 0))]
        + [pl.BlockSpec(memory_space=pl.ANY)] * len(pieces),
        out_specs=[
            pl.BlockSpec((18, tile, BLOCK), lambda i: (0, i, 0)),
            pl.BlockSpec((width, 3 * width), lambda i: (0, 0)),
        ],
        out_shape=[
            jax.ShapeDtypeStruct((18, rows, BLOCK), BF16),
            jax.ShapeDtypeStruct((width, 3 * width), BF16),
        ],
        scratch_shapes=[pltpu.SemaphoreType.DMA((n_copies,))],
        compiler_params=pltpu.CompilerParams(
            dimension_semantics=("arbitrary",), vmem_limit_bytes=VMEM_GRANT
        ),
        cost_estimate=SHORT,
        name="qkv",
    )(window, *pieces)


def run_of(ids_ref, block, count):
    own = ids_ref[block]

    def same(other):
        inside = jnp.logical_and(other >= 0, other < count)
        return jnp.logical_and(inside, ids_ref[jnp.clip(other, 0, count - 1)] == own)

    before = sum(same(block - step).astype(jnp.int32) for step in (1, 2, 3))
    after = sum(same(block + step).astype(jnp.int32) for step in (1, 2, 3))
    return block - before, before + after + 1


def halves_of(rows):
    lane = lax.broadcasted_iota(jnp.int32, rows.shape, 1)
    zero = jnp.zeros_like(rows)
    return jnp.concatenate(
        (jnp.where(lane < HEAD_DIM, rows, zero), jnp.where(lane < HEAD_DIM, zero, rows)), axis=0
    )


def fill_distances(table_ref):
    shape = table_ref.shape
    key = lax.broadcasted_iota(jnp.int32, shape, 0) - 3 * BLOCK
    query = lax.broadcasted_iota(jnp.int32, shape, 1)
    table_ref[...] = jnp.abs(key - query).astype(F32)


def biased_scores(keys, query_pair, distances, slope_one, slope_two):
    bias = jnp.concatenate((distances * slope_one, distances * slope_two), axis=1)
    return dot_nt(keys, query_pair) - bias


def untwine(both):
    mine = jnp.concatenate(
        (both[:HEAD_DIM, :BLOCK], both[HEAD_DIM:, BLOCK:]), axis=0
    )
    return mine.T


GROUP = 3


def attend_kernel(first_own, n_own, first_group, ids_ref, slopes_ref, q_ref, k_ref, v_ref, ctx_ref, lse_ref, table_ref):
    group = first_group + pl.program_id(0)
    count = q_ref.shape[1] // BLOCK

    @pl.when(pl.program_id(0) == 0)
    def _():
        fill_distances(table_ref)

    def one_block(number, carry):
        block = number + first_own
        start, length = run_of(ids_ref, block, count)
        rows = pl.ds(pl.multiple_of(block * BLOCK, BLOCK), BLOCK)
        place = pl.ds(pl.multiple_of(number * BLOCK, BLOCK), BLOCK)
        shift = pl.multiple_of((3 - (block - start)) * BLOCK, BLOCK)

        def variant(blocks):
            width = blocks * BLOCK
            span = pl.ds(pl.multiple_of(start * BLOCK, BLOCK), width)
            distances = table_ref[pl.ds(shift, width), :]
            for pair in range(GROUP):
                head = 2 * (group * GROUP + pair)
                queries = halves_of(q_ref[pair, rows, :] * jnp.asarray(HEAD_DIM**-0.5, BF16))
                scores = biased_scores(
                    k_ref[pair, span, :], queries, distances, slopes_ref[head], slopes_ref[head + 1]
                )
                peak = jnp.max(scores, axis=0, keepdims=True)
                terms = jnp.exp(scores - peak)
                total = jnp.sum(terms, axis=0, keepdims=True)
                lse = peak + jnp.log(total)
                lse_ref[pair, 0:1, place] = lse[:, :BLOCK]
                lse_ref[pair, 1:2, place] = lse[:, BLOCK:]
                probs = (terms * (1.0 / total)).astype(BF16)
                both = dot_tn(v_ref[pair, span, :], probs)
                ctx_ref[place, pair * BLOCK : (pair + 1) * BLOCK] = untwine(both).astype(BF16)

        for blocks in (1, 2, 4):
            @pl.when(length == blocks)
            def _(blocks=blocks):
                variant(blocks)

        return carry

    lax.fori_loop(0, n_own, one_block, 0)


def attend_call(ids, slopes, pairs, own_rows, first_group, n_groups):
    rows = pairs.shape[1]
    steps = 6 // GROUP
    wide = GROUP * BLOCK
    part = lambda third: pl.BlockSpec(
        (GROUP, rows, BLOCK), lambda g: (third * steps + first_group + g, 0, 0)
    )
    smem = pl.BlockSpec(memory_space=pltpu.SMEM)
    return pl.pallas_call(
        functools.partial(attend_kernel, HALO // BLOCK, own_rows // BLOCK, first_group),
        grid=(n_groups,),
        in_specs=[smem, smem, part(0), part(1), part(2)],
        out_specs=[
            pl.BlockSpec((own_rows, wide), lambda g: (0, g)),
            pl.BlockSpec((GROUP, 2, own_rows), lambda g: (g, 0, 0)),
        ],
        out_shape=[
            jax.ShapeDtypeStruct((own_rows, n_groups * wide), BF16),
            jax.ShapeDtypeStruct((n_groups * GROUP, 2, own_rows), F32),
        ],
        scratch_shapes=[pltpu.VMEM((7 * BLOCK, BLOCK), F32)],
        compiler_params=pltpu.CompilerParams(
            dimension_semantics=("arbitrary",), vmem_limit_bytes=VMEM_GRANT
        ),
        cost_estimate=SHORT,
        name="attend",
    )(ids, slopes, pairs, pairs, pairs)


def attend_back_kernel(
    first_own, n_own, first_group, ids_ref, slopes_ref, q_ref, k_ref, v_ref, stats_ref, dctx_ref,
    dq_ref, dk_ref, dv_ref, table_ref, dk_sum, dv_sum,
):
    group = first_group + pl.program_id(0)
    count = q_ref.shape[1] // BLOCK

    @pl.when(pl.program_id(0) == 0)
    def _():
        fill_distances(table_ref)

    dk_sum[...] = jnp.zeros_like(dk_sum)
    dv_sum[...] = jnp.zeros_like(dv_sum)
    end_own = first_own + n_own

    def one_block(block, carry):
        start, length = run_of(ids_ref, block, count)
        own = jnp.logical_and(block >= first_own, block < end_own)
        key_start = jnp.where(own, start, jnp.maximum(start, first_own))
        key_end = jnp.where(own, start + length, jnp.minimum(start + length, end_own))
        n_keys = key_end - key_start
        rows = pl.ds(pl.multiple_of(block * BLOCK, BLOCK), BLOCK)
        place = pl.ds(pl.multiple_of(block * BLOCK, BLOCK), BLOCK)
        shift = pl.multiple_of((3 - (block - key_start)) * BLOCK, BLOCK)

        def variant(blocks):
            width = blocks * BLOCK
            span = pl.ds(pl.multiple_of(key_start * BLOCK, BLOCK), width)
            distances = table_ref[pl.ds(shift, width), :]
            for pair in range(GROUP):
                head = 2 * (group * GROUP + pair)
                lanes = slice(pair * BLOCK, (pair + 1) * BLOCK)
                keys = k_ref[pair, span, :]
                queries = halves_of(q_ref[pair, rows, :] * jnp.asarray(HEAD_DIM**-0.5, BF16))
                scores = biased_scores(
                    keys, queries, distances, slopes_ref[head], slopes_ref[head + 1]
                )
                lse = jnp.concatenate(
                    (stats_ref[pair, 0:1, rows], stats_ref[pair, 1:2, rows]), axis=1
                )
                inner = jnp.concatenate(
                    (stats_ref[pair, 2:3, rows], stats_ref[pair, 3:4, rows]), axis=1
                )
                soft = jnp.exp(scores - lse)
                dctx = halves_of(dctx_ref[rows, lanes])
                dsoft = dot_nt(v_ref[pair, span, :], dctx)
                dv_sum[pair, span, :] += dot_nn(soft.astype(BF16), dctx)
                dscores = (soft * (dsoft - inner)).astype(BF16)
                dk_sum[pair, span, :] += dot_nn(dscores, queries)
                dq_ref[place, lanes] = (untwine(dot_tn(keys, dscores)) * HEAD_DIM**-0.5).astype(BF16)

        for blocks in (1, 2, 3, 4):
            @pl.when(n_keys == blocks)
            def _(blocks=blocks):
                variant(blocks)

        return carry

    lax.fori_loop(0, count, one_block, 0)
    mine = pl.ds(first_own * BLOCK, n_own * BLOCK)
    for pair in range(GROUP):
        lanes = slice(pair * BLOCK, (pair + 1) * BLOCK)
        dk_ref[:, lanes] = dk_sum[pair, mine, :].astype(BF16)
        dv_ref[:, lanes] = dv_sum[pair, mine, :].astype(BF16)


def attend_back_call(ids, slopes, pairs, stats, dctx, own_rows, first_group, n_groups):
    rows = pairs.shape[1]
    steps = 6 // GROUP
    wide = GROUP * BLOCK
    part = lambda third: pl.BlockSpec(
        (GROUP, rows, BLOCK), lambda g: (third * steps + first_group + g, 0, 0)
    )
    smem = pl.BlockSpec(memory_space=pltpu.SMEM)
    return pl.pallas_call(
        functools.partial(attend_back_kernel, HALO // BLOCK, own_rows // BLOCK, first_group),
        grid=(n_groups,),
        in_specs=[
            smem, smem, part(0), part(1), part(2),
            pl.BlockSpec((GROUP, 4, rows), lambda g: (first_group + g, 0, 0)),
            pl.BlockSpec((rows, wide), lambda g: (0, first_group + g)),
        ],
        out_specs=[pl.BlockSpec((rows, wide), lambda g: (0, g))]
        + [pl.BlockSpec((own_rows, wide), lambda g: (0, g))] * 2,
        out_shape=[jax.ShapeDtypeStruct((rows, n_groups * wide), BF16)]
        + [jax.ShapeDtypeStruct((own_rows, n_groups * wide), BF16)] * 2,
        scratch_shapes=[
            pltpu.VMEM((7 * BLOCK, BLOCK), F32),
            pltpu.VMEM((GROUP, rows, BLOCK), F32),
            pltpu.VMEM((GROUP, rows, BLOCK), F32),
        ],
        compiler_params=pltpu.CompilerParams(
            dimension_semantics=("arbitrary",), vmem_limit_bytes=VMEM_GRANT
        ),
        cost_estimate=SHORT,
        name="attend_back",
    )(ids, slopes, pairs, pairs, pairs, stats, dctx)


FF_TILE = 512


def row_mean(values):
    return jnp.mean(values, axis=1, keepdims=True)


def norm_parts(values):
    center = values - row_mean(values)
    scale = lax.rsqrt(row_mean(center * center) + LN_EPS)
    return center * scale, scale


def norm_back(grad_unit, unit, scale):
    return scale * (grad_unit - row_mean(grad_unit) - unit * row_mean(grad_unit * unit))


def column_sum(values):
    return jnp.sum(values, axis=0, keepdims=True)


def middle_kernel(plans_of, slot_of, counts, n_pieces, ctx_ref, tok_ref, cot_ref, vec_ref, *refs):
    pieces = refs[:n_pieces]
    (result_ref, hidden_ref, dgu_ref, dffn_ref, low_ref, dattn_ref, dfirst_ref, dctx_ref,
     inner_ref, sums_ref, w_out, w_gu, w_down, gate_grad, up_grad, sems) = refs[n_pieces:]
    step = pl.program_id(0)
    width = tok_ref.shape[1]
    half = width // 2
    ff = w_down.shape[0]
    slot = slot_of()

    def copies_of(which):
        target = (w_out, w_gu, w_down)[which]
        return part_copies(pieces, plans_of()[which], target, sems, sum(counts[:which]))

    def wait_for(which):
        @pl.when(step == 0)
        def _():
            for copy in copies_of(which):
                copy.wait()

    @pl.when(step == 0)
    def _():
        sums_ref[...] = jnp.zeros_like(sums_ref)
        for which in range(3):
            for copy in copies_of(which):
                copy.start()

    gain_one, shift_one = vec_ref[0:1, :], vec_ref[1:2, :]
    gain_two, shift_two = vec_ref[2:3, :], vec_ref[3:4, :]
    wait_for(0)
    attn = dot_nn(ctx_ref[...], w_out[...])
    unit_one, scale_one = norm_parts(tok_ref[...].astype(F32) + attn + vec_ref[4:5, :])
    normed = unit_one * gain_one + shift_one
    low = normed.astype(BF16)
    low_ref[...] = low
    wait_for(1)
    wait_for(2)
    ffn = jnp.zeros((low.shape[0], width), F32)
    for tile in range(ff // FF_TILE):
        cols = slice(tile * FF_TILE, (tile + 1) * FF_TILE)
        gate = dot_nn(low, w_gu[:, cols])
        up = dot_nn(low, w_gu[:, ff + tile * FF_TILE : ff + (tile + 1) * FF_TILE])
        below = 0.5 + 0.5 * lax.erf(gate * np.float32(0.5**0.5))
        gelu = gate * below
        slope = below + gate * (jnp.exp(-0.5 * gate * gate) * np.float32((2.0 * np.pi) ** -0.5))
        hidden = (gelu * up).astype(BF16)
        hidden_ref[:, cols] = hidden
        gate_grad[:, cols] = up * slope
        up_grad[:, cols] = gelu
        ffn = ffn + dot_nn(hidden, w_down[cols, :])
    unit_two, scale_two = norm_parts(normed + ffn + vec_ref[5:6, :])
    result_ref[...] = (unit_two * gain_two + shift_two).astype(BF16)
    grad = cot_ref[...].astype(F32)
    sums_ref[2:3, :] += column_sum(grad * unit_two)
    sums_ref[3:4, :] += column_sum(grad)
    dsecond = norm_back(grad * gain_two, unit_two, scale_two)
    sums_ref[5:6, :] += column_sum(dsecond)
    dffn = dsecond.astype(BF16)
    dffn_ref[slot] = dffn[:, :half]
    dffn_ref[1 - slot] = dffn[:, half:]
    dnormed = dsecond
    for tile in range(ff // FF_TILE):
        cols = slice(tile * FF_TILE, (tile + 1) * FF_TILE)
        ups = slice(ff + tile * FF_TILE, ff + (tile + 1) * FF_TILE)
        dhidden = dot_nt(dffn, w_down[cols, :])
        dgate = (dhidden * gate_grad[:, cols]).astype(BF16)
        dup = (dhidden * up_grad[:, cols]).astype(BF16)
        chunk, place = divmod(tile * FF_TILE, ff // 2)
        dgu_ref[slot, chunk, :, place : place + FF_TILE] = dgate
        dgu_ref[1 - slot, chunk, :, place : place + FF_TILE] = dup
        dnormed = dnormed + dot_nt(dgate, w_gu[:, cols]) + dot_nt(dup, w_gu[:, ups])
    sums_ref[0:1, :] += column_sum(dnormed * unit_one)
    sums_ref[1:2, :] += column_sum(dnormed)
    dfirst = norm_back(dnormed * gain_one, unit_one, scale_one)
    sums_ref[4:5, :] += column_sum(dfirst)
    dfirst_ref[...] = dfirst
    dattn = dfirst.astype(BF16)
    dattn_ref[...] = dattn
    dctx = dot_nt(dattn, w_out[...]).astype(BF16)
    dctx_ref[...] = dctx
    head = lax.broadcasted_iota(jnp.int32, (16, width), 0)
    column = lax.broadcasted_iota(jnp.int32, (16, width), 1)
    member = jnp.where(column // HEAD_DIM == head, 1.0, 0.0).astype(BF16)
    product = dctx.astype(F32) * ctx_ref[...].astype(F32)
    high = product.astype(BF16)
    rest = (product - high.astype(F32)).astype(BF16)
    inner_ref[...] = dot_nt(member, high) + dot_nt(member, rest)


def middle_call(ctx, tokens, cotangent, vectors, pieces, plans_of, slot_of, counts):
    rows, width = tokens.shape
    ff = 4 * width
    tile = 256
    by_rows = lambda cols: pl.BlockSpec((tile, cols), lambda i: (i, 0))
    paired = lambda cols: pl.BlockSpec((2, tile, cols), lambda i: (0, i, 0))
    shaped = lambda cols, dtype: jax.ShapeDtypeStruct((rows, cols), dtype)
    return pl.pallas_call(
        functools.partial(middle_kernel, plans_of, slot_of, counts, len(pieces)),
        grid=(rows // tile,),
        in_specs=[by_rows(width)] * 3
        + [pl.BlockSpec((8, width), lambda i: (0, 0))]
        + [pl.BlockSpec(memory_space=pl.ANY)] * len(pieces),
        out_specs=[
            by_rows(width), by_rows(ff),
            pl.BlockSpec((2, 2, tile, ff // 2), lambda i: (0, 0, i, 0)),
            paired(width // 2), by_rows(width),
            by_rows(width), by_rows(width), by_rows(width),
            pl.BlockSpec((16, tile), lambda i: (0, i)),
            pl.BlockSpec((8, width), lambda i: (0, 0)),
        ],
        out_shape=[
            shaped(width, BF16), shaped(ff, BF16), jax.ShapeDtypeStruct((2, 2, rows, ff // 2), BF16),
            jax.ShapeDtypeStruct((2, rows, width // 2), BF16), shaped(width, BF16),
            shaped(width, BF16), shaped(width, F32),
            shaped(width, BF16),
            jax.ShapeDtypeStruct((16, rows), F32),
            jax.ShapeDtypeStruct((8, width), F32),
        ],
        scratch_shapes=[
            pltpu.VMEM((width, width), BF16),
            pltpu.VMEM((width, 2 * ff), BF16),
            pltpu.VMEM((ff, width), BF16),
            pltpu.VMEM((tile, ff), F32),
            pltpu.VMEM((tile, ff), F32),
            pltpu.SemaphoreType.DMA((sum(counts),)),
        ],
        compiler_params=pltpu.CompilerParams(
            dimension_semantics=("arbitrary",), vmem_limit_bytes=VMEM_GRANT
        ),
        cost_estimate=SHORT,
        name="middle",
    )(ctx, tokens, cotangent, vectors, *pieces)


def collect_kernel(plan_of, n_parts, *refs):
    parts, wholes = refs[:n_parts], refs[n_parts : n_parts + 5]
    total_ref, sems = refs[n_parts + 5 :]
    copies = []
    for number, entry in enumerate(plan_of()):
        part, row, rows, col, cols, whole, to_row, to_col = entry
        copies.append(
            pltpu.make_async_copy(
                parts[part].at[pl.ds(row, rows), pl.ds(col, cols)],
                wholes[whole].at[pl.ds(to_row, rows), pl.ds(to_col, cols)],
                sems.at[number],
            )
        )
    for copy in copies:
        copy.start()
    for copy in copies:
        copy.wait()
    total = jnp.zeros((1, 1), F32)
    for whole in wholes:
        values = whole[...].astype(F32)
        total = total + jnp.sum(jnp.sum(values * values, axis=0, keepdims=True), axis=1, keepdims=True)
    total_ref[...] = jnp.broadcast_to(total, total_ref.shape)


def collect_call(parts, plan_of, n_copies, shapes):
    vmem = pl.BlockSpec(memory_space=pltpu.VMEM)
    return pl.pallas_call(
        functools.partial(collect_kernel, plan_of, len(parts)),
        in_specs=[pl.BlockSpec(memory_space=pl.ANY)] * len(parts),
        out_specs=[vmem] * 6,
        out_shape=[jax.ShapeDtypeStruct(shape, BF16) for shape in shapes]
        + [jax.ShapeDtypeStruct((8, BLOCK), F32)],
        scratch_shapes=[pltpu.SemaphoreType.DMA((n_copies,))],
        compiler_params=pltpu.CompilerParams(vmem_limit_bytes=VMEM_GRANT),
        cost_estimate=SHORT,
        name="collect",
    )(*parts)


def adam_kernel(factor_ref, *refs):
    masters, firsts, seconds, grads, outs = (
        refs[:5], refs[5:10], refs[10:15], refs[15:20], refs[20:]
    )
    factor = factor_ref[0]
    for index in range(5):
        rate, decay = (RATE_MAT, DECAY_MAT) if index < 4 else (RATE_VEC, 0.0)
        new_ref, first_ref, second_ref, copy_ref = outs[4 * index : 4 * index + 4]
        master = masters[index][...]
        clipped = grads[index][...].astype(F32) * factor
        first = BETA_ONE * firsts[index][...] + (1.0 - BETA_ONE) * clipped
        second = BETA_TWO * seconds[index][...] + (1.0 - BETA_TWO) * clipped * clipped
        direction = first / CORR_ONE / (jnp.sqrt(second / CORR_TWO) + ADAM_EPS)
        new = master - rate * (direction + decay * master)
        new_ref[...] = new
        first_ref[...] = first
        second_ref[...] = second
        copy_ref[...] = new.astype(BF16)


def adam_call(masters, firsts, seconds, grads, factor):
    steps = 6

    def spec(array, index):
        rows, cols = array.shape
        if index == 4:
            return pl.BlockSpec((rows, cols), lambda i: (0, 0))
        return pl.BlockSpec((rows, cols // steps), lambda i: (0, i))

    specs = [spec(array, index) for index, array in enumerate(masters)]
    return pl.pallas_call(
        adam_kernel,
        grid=(steps,),
        in_specs=[pl.BlockSpec(memory_space=pltpu.SMEM)] + specs * 4,
        out_specs=[one for one in specs for _ in range(4)],
        out_shape=[
            jax.ShapeDtypeStruct(array.shape, dtype)
            for array in masters
            for dtype in (F32, F32, F32, BF16)
        ],
        compiler_params=pltpu.CompilerParams(
            dimension_semantics=("arbitrary",), vmem_limit_bytes=VMEM_GRANT
        ),
        cost_estimate=SHORT,
        name="adam",
    )(factor, *masters, *firsts, *seconds, *grads)


def halo_window(rows, groups):
    left = lax.ppermute(rows[-HALO:], "head", [(i, i + 1) for i in range(groups - 1)])
    right = lax.ppermute(rows[:HALO], "head", [(i + 1, i) for i in range(groups - 1)])
    return jnp.concatenate((left, rows, right), axis=0)


def halo_stats(lse, inner, groups):
    stats = jnp.concatenate((lse, inner[:HEADS].reshape(6, 2, -1)), axis=1)
    left = lax.ppermute(stats[:, :, -HALO:], "head", [(i, i + 1) for i in range(groups - 1)])
    right = lax.ppermute(stats[:, :, :HALO], "head", [(i + 1, i) for i in range(groups - 1)])
    return jnp.concatenate((left, stats, right), axis=2)


def slope_table():
    return jnp.asarray(np.array(SLOPES), F32)


def window_ids(segment_ids, own_rows):
    block_ids = segment_ids.reshape(-1, BLOCK)[:, 0]
    edge = HALO // BLOCK
    padded = jnp.pad(block_ids, (edge, edge), constant_values=-1)
    own_blocks = own_rows // BLOCK
    return lax.dynamic_slice_in_dim(
        padded, lax.axis_index("head") * own_blocks, own_blocks + 2 * edge
    )


def updated(masters, firsts, seconds, shards, grad_norm, clip_norm):
    factor = jnp.minimum(1.0, clip_norm / grad_norm)
    return adam_call(masters, firsts, seconds, shards, factor)


def plain_body(tokens, segment_ids, cotangent, clip_norm, *state):
    masters, firsts, seconds = state[:5], state[5:10], state[10:]
    groups = lax.axis_size("head")
    own_rows, width = tokens.shape
    low = [w.astype(BF16) for w in masters]
    window = halo_window(tokens, groups)
    full = [lax.all_gather(w, "dp", axis=0, tiled=True) for w in low[:4]]
    full_vec = lax.all_gather(low[4], "dp", axis=1, tiled=True)
    vectors = jnp.pad(full_vec.astype(F32), ((0, 2), (0, 0)))
    slopes = slope_table()
    ids = window_ids(segment_ids, own_rows)

    def whole_plan(part, rows):
        return [(part, None, 0, rows, 0, 0)]

    pairs, whole_qkv = qkv_call(window, [full[0]], lambda: whole_plan(0, width), 1)
    ctx, lse = attend_call(ids, slopes, pairs, own_rows, 0, 6 // GROUP)
    result, hidden, dgu, dffn, normed_low, dattn, dfirst, dctx, inner, sums = middle_call(
        ctx, tokens, cotangent, vectors, full[1:],
        lambda: (whole_plan(0, width), whole_plan(1, width), whole_plan(2, 4 * width)),
        lambda: 0, (1, 1, 1),
    )
    joined_back = lambda two: jnp.concatenate((two[0], two[1]), axis=1)
    grad_down = dot_tn(hidden, joined_back(dffn)).astype(BF16)
    grad_gu = dot_tn(normed_low, jnp.concatenate((dgu[0, 0], dgu[0, 1], dgu[1, 0], dgu[1, 1]), axis=1)).astype(BF16)
    grad_out = dot_tn(ctx, dattn).astype(BF16)
    dctx_window = halo_window(dctx, groups)
    stats = halo_stats(lse, inner, groups)
    dq, dk, dv = attend_back_call(ids, slopes, pairs, stats, dctx_window, own_rows, 0, 6 // GROUP)
    dq = dq[HALO:-HALO]
    djoined = jnp.concatenate((dq, dk, dv), axis=1)
    grad_qkv = dot_tn(tokens, djoined).astype(BF16)
    grad_input = dfirst + dot_nt(djoined, whole_qkv)

    def reduced(grad):
        share = lax.psum_scatter(grad, "dp", scatter_dimension=0, tiled=True)
        return lax.psum(share, "head").astype(F32)

    shards = [reduced(grad) for grad in (grad_qkv, grad_out, grad_gu, grad_down)]
    vec_sum = lax.psum(sums[:6], ("dp", "head"))
    vec_cols = masters[4].shape[1]
    shards.append(
        lax.dynamic_slice_in_dim(vec_sum, lax.axis_index("dp") * vec_cols, vec_cols, axis=1)
    )
    squares = sum(jnp.sum(piece * piece) for piece in shards)
    grad_norm = jnp.sqrt(lax.psum(squares, "dp")).reshape(1)
    updates = updated(masters, firsts, seconds, shards, grad_norm, clip_norm)
    return (result, grad_input, *updates, grad_norm)


SWAP_CORE = ("head", [(i, i ^ 1) for i in range(4)])
SWAP_X = ("head", [(i, i ^ 2) for i in range(4)])
SWAP_Y = ("dp", [(i, i ^ 1) for i in range(8)])
SWAP_Z = [None] + [("dp", [(i, i ^ (2 * step)) for i in range(8)]) for step in (1, 2, 3)]


MIDDLE_Z = ("dp", [(2, 4), (3, 5), (4, 2), (5, 3)])
OUTWARD_Z = ("dp", [(2, 0), (3, 1), (4, 6), (5, 7)])


def swap(values, how):
    return lax.ppermute(values, *how)


def position():
    dp, head = lax.axis_index("dp"), lax.axis_index("head")
    return dp // 2, dp % 2, head // 2, head % 2


def half_of(values, which, axis):
    size = values.shape[axis] // 2
    return lax.dynamic_slice_in_dim(values, which * size, size, axis)


def together(*values):
    return lax.optimization_barrier(values)


def slab_sum(mine, other):
    return (mine.astype(F32) + other.astype(F32)).astype(BF16)


def split(values, which, axis):
    return (
        lax.dynamic_index_in_dim(values, which, axis, keepdims=False),
        lax.dynamic_index_in_dim(values, 1 - which, axis, keepdims=False),
    )


def split_y(values, y):
    return split(values.reshape(4, 2, *values.shape[1:]), y, 1)


def trade(values, axis):
    return lax.all_to_all(values, axis, split_axis=0, concat_axis=0, tiled=True)


def cube_body(tokens, segment_ids, cotangent, clip_norm, *state):
    masters, firsts, seconds = state[:5], state[5:10], state[10:]
    groups = lax.axis_size("head")
    own_rows, width = tokens.shape
    ff = 4 * width
    half = width // 2
    shard = width // 8
    z, y, x, core = position()
    low = [w.astype(BF16) for w in masters]
    slopes = slope_table()
    ids = window_ids(segment_ids, own_rows)

    own_q = half_of(low[0], core, 1)
    own_g = half_of(half_of(low[2], core, 1), x, 0)
    vec_rows = jnp.pad(low[4], ((0, 10), (0, half - shard)))
    own_r = jnp.concatenate((half_of(low[3], core, 1), half_of(low[1], core, 1), vec_rows), axis=0)
    rest_rows = own_r.shape[0]

    def pair_of(own):
        return jnp.stack((own, swap(own, SWAP_Z[1])))

    pair_q, pair_r, own_g = together(pair_of(own_q), pair_of(own_r), own_g)

    mid_q = swap(pair_q, MIDDLE_Z)
    pair_y_q = swap(pair_q, SWAP_Y)
    pair_g = pair_of(own_g)
    window = halo_window(tokens, groups)
    mid_q, pair_y_q, pair_g, pair_r, window = together(mid_q, pair_y_q, pair_g, pair_r, window)

    end_q = swap(mid_q, OUTWARD_Z)
    mid_g = swap(pair_g, MIDDLE_Z)
    pair_y_g = swap(pair_g, SWAP_Y)
    xpair_g = swap(pair_g, SWAP_X)
    near_q = [pair_q, pair_y_q]
    across_q = [swap(part, SWAP_CORE) for part in near_q]
    end_q, mid_g, pair_y_g, pair_g, xpair_g, pair_r, *rest = together(
        end_q, mid_g, pair_y_g, pair_g, xpair_g, pair_r, *near_q, *across_q
    )
    near_q, across_q = rest[:2], rest[2:]

    other_q = mid_q + end_q
    other_y_q = swap(other_q, SWAP_Y)
    end_g = swap(mid_g, OUTWARD_Z)
    mid_r = swap(pair_r, MIDDLE_Z)
    xpair_y_g = swap(pair_y_g, SWAP_X)
    other_q, other_y_q, end_g, xpair_y_g, mid_r, pair_r = together(
        other_q, other_y_q, end_g, xpair_y_g, mid_r, pair_r
    )

    other_g = mid_g + end_g
    other_y_g = swap(other_g, SWAP_Y)
    end_r = swap(mid_r, OUTWARD_Z)
    xother_g = swap(other_g, SWAP_X)
    late_q = [other_q, other_y_q]
    late_across_q = [swap(part, SWAP_CORE) for part in late_q]

    def pair_rows(z, y):
        near = z + 1 - 2 * (z % 2)
        far_one, far_two = 2 - z // 2, 3 - 3 * (z // 2)
        first = [[z * 2 + y, near * 2 + y], [z * 2 + 1 - y, near * 2 + 1 - y]]
        return first + [
            [far_one * 2 + y, far_two * 2 + y], [far_one * 2 + 1 - y, far_two * 2 + 1 - y]
        ]

    def qkv_plan():
        z, y, _, core = position()
        plan = []
        for swapped in (0, 1):
            col = aligned((core + swapped * (1 - 2 * core)) * (3 * half), BLOCK)
            for part, rows in enumerate(pair_rows(z, y)):
                for index, dp in enumerate(rows):
                    plan.append((part + 4 * swapped, index, 0, shard, aligned(dp * shard, 32), col))
        return plan

    pairs, whole_qkv = qkv_call(window, near_q + late_q + across_q + late_across_q, qkv_plan, 16)
    pairs, other_g, other_y_g, end_r = together(pairs, other_g, other_y_g, end_r)

    xother_y_g = swap(other_y_g, SWAP_X)
    other_r = mid_r + end_r
    pair_y_r, other_y_r = swap(pair_r, SWAP_Y), swap(other_r, SWAP_Y)
    near_r = [pair_r, other_r]
    across_r = [swap(part, SWAP_CORE) for part in near_r]
    near_g = [pair_g, pair_y_g, other_g, other_y_g, xpair_g, xpair_y_g]
    across_g = [swap(part, SWAP_CORE) for part in near_g]
    ctx, lse = attend_call(ids, slopes, pairs, own_rows, 0, 2)
    ctx, lse, xother_g, xother_y_g, pair_y_r, other_y_r, *rest = together(
        ctx, lse, xother_g, xother_y_g, pair_y_r, other_y_r, *near_r, *across_r, *across_g
    )
    near_r, across_r, across_g = rest[:2], rest[2:4], rest[4:]
    late_g = [xother_g, xother_y_g]
    parts_g = near_g + late_g + across_g + [swap(part, SWAP_CORE) for part in late_g]
    parts_r = [near_r[0], pair_y_r, near_r[1], other_y_r]
    order = jnp.stack([index for indices in pair_rows(z, y) for index in indices])
    vec_all = jnp.concatenate([part[:, rest_rows - 16 : rest_rows - 8, :shard] for part in parts_r])
    vec_all = vec_all.astype(F32)
    parts_r = parts_r + [
        across_r[0], swap(pair_y_r, SWAP_CORE), across_r[1], swap(other_y_r, SWAP_CORE)
    ]
    vectors = jnp.zeros_like(vec_all).at[order].set(vec_all).transpose(1, 0, 2).reshape(8, width)

    def middle_plans():
        z, y, x, core = position()
        rows_of = pair_rows(z, y)
        out_plan, gu_plan, down_plan = [], [], []
        for swapped in (0, 1):
            side = core + swapped * (1 - 2 * core)
            for part in range(4):
                for index, dp in enumerate(rows_of[part]):
                    col = aligned(side * half, BLOCK)
                    place = (16 + 4 * swapped + part, index)
                    out_plan.append((*place, ff // 8, shard, aligned(dp * shard, 32), col))
                    down_plan.append((*place, 0, ff // 8, aligned(dp * (ff // 8), BLOCK), col))
            for flipped in (0, 1):
                rows_half = x + flipped * (1 - 2 * x)
                for part in range(4):
                    for index, dp in enumerate(rows_of[part]):
                        place = (4 * flipped + part, index)
                        row = aligned(dp * shard + rows_half * (shard // 2), 16)
                        gu_plan.append(
                            (8 * swapped + place[0], place[1], 0, shard // 2, row, aligned(side * ff, BLOCK))
                        )
        return out_plan, gu_plan, down_plan

    result, hidden, dgu, dffn, normed_low, dattn, dfirst, dctx, inner, sums = middle_call(
        ctx, tokens, cotangent, vectors, parts_g + parts_r,
        middle_plans, lambda: position()[3], (16, 32, 16),
    )

    def core_keep(left, right, theirs):
        return (dot_tn(left, right) + theirs.astype(F32)).astype(BF16)

    their_down = swap(dot_tn(hidden, dffn[1]).astype(BF16), SWAP_CORE)
    one_theirs = swap(dot_tn(normed_low, dgu[1, 0]).astype(BF16), SWAP_CORE)
    two_theirs = dot_tn(normed_low, dgu[1, 1]).astype(BF16)
    their_down, one_theirs, two_theirs, hidden, normed_low = together(
        their_down, one_theirs, two_theirs, hidden, normed_low
    )
    two_theirs = swap(two_theirs, SWAP_CORE)
    sum_down = core_keep(hidden, dffn[0], their_down)
    sum_one = core_keep(normed_low, dgu[0, 0], one_theirs).reshape(8, 2, shard // 2, ff // 2)
    sum_down, sum_one, two_theirs, normed_low = together(sum_down, sum_one, two_theirs, normed_low)
    share_down = lax.psum_scatter(sum_down, "dp", scatter_dimension=0, tiled=True)

    def core_rows(grad):
        mine, away = split(grad.reshape(8, 2, shard // 2, grad.shape[1]), core, 1)
        return slab_sum(mine, swap(away, SWAP_CORE))

    def z_send(values):
        others = (z + 1 - 2 * (z % 2), (z + 2) % 4, 3 - z)
        return [
            swap(lax.dynamic_index_in_dim(values, other, 0, keepdims=False), SWAP_Z[step])
            for step, other in zip((1, 2, 3), others)
        ]

    def z_sum(values, theirs):
        total = lax.dynamic_index_in_dim(values, z, 0, keepdims=False).astype(F32)
        for other in theirs:
            total = total + other.astype(F32)
        return total.astype(BF16)

    def qkv_grad(back):
        joined = jnp.concatenate((back[0][HALO:-HALO], back[1], back[2]), axis=1)
        return core_rows(dot_tn(tokens, joined).astype(BF16))

    cut = ff // 2
    one, one_away = split(sum_one, x, 1)
    two, two_away = split_y(core_keep(normed_low, dgu[0, 1], two_theirs).reshape(8, shard, cut), y)
    dctx_window = halo_window(dctx, groups)
    stats = halo_stats(lse, inner, groups)
    one, one_away, two, two_away, dctx_window, stats = together(
        one, one_away, two, two_away, dctx_window, stats
    )
    one_their = swap(one_away, SWAP_X)
    two_their = swap(two_away, SWAP_Y)
    vec_cols = jnp.pad(sums.astype(BF16).T, ((0, 0), (0, BLOCK - 8)))
    sum_ov = core_rows(jnp.concatenate((dot_tn(ctx, dattn).astype(BF16), vec_cols), axis=1))
    back_a = attend_back_call(ids, slopes, pairs, stats, dctx_window, own_rows, 0, 1)
    one_their, two_their, dctx_window, sum_ov, *back_a = together(
        one_their, two_their, dctx_window, sum_ov, *back_a
    )
    two = slab_sum(two, two_their)
    two_their = z_send(two)
    one = jnp.concatenate((slab_sum(one, one_their), qkv_grad(back_a), sum_ov), axis=2)
    one, one_away = split_y(one, y)
    one_their = swap(one_away, SWAP_Y)
    back_b = attend_back_call(ids, slopes, pairs, stats, dctx_window, own_rows, 1, 1)
    one_their, share_down, *rest = together(one_their, share_down, *two_their, *back_b)
    two_their, back_b = rest[:3], rest[3:]

    one = slab_sum(one, one_their)
    one_their = z_send(one)
    grad_b = trade(qkv_grad(back_b), "dp")
    two_mine = z_sum(two, two_their)
    two_other = swap(two_mine, SWAP_X)
    down_other = swap(share_down, SWAP_X)
    djoined = jnp.concatenate(
        (back_a[0][HALO:-HALO], back_b[0][HALO:-HALO], back_a[1], back_b[1], back_a[2], back_b[2]), axis=1
    )
    grad_input = dfirst + dot_nt(djoined, whole_qkv)
    grad_b, two_other, down_other, grad_input, *one_their = together(
        grad_b, two_other, down_other, grad_input, *one_their
    )
    b_mine = jnp.sum(grad_b.astype(F32), axis=0).astype(BF16)
    one_mine = jnp.concatenate((z_sum(one, one_their), b_mine), axis=1)
    one_other = swap(one_mine, SWAP_X)
    two_sum, down_sum = slab_sum(two_mine, two_other), slab_sum(share_down, down_other)
    two_across, down_across = swap(two_sum, SWAP_CORE), swap(down_sum, SWAP_CORE)
    rest_sum = slab_sum(one_mine[:, cut:], one_other[:, cut:])
    parts = [
        one_mine, one_other, rest_sum, two_sum, down_sum,
        swap(one_mine, SWAP_CORE), swap(one_other, SWAP_CORE), swap(rest_sum, SWAP_CORE),
        two_across, down_across,
    ]

    def collect_plan():
        _, _, x, core = position()
        rows = shard // 2
        plan = []
        for swapped in (0, 1):
            side = core + swapped * (1 - 2 * core)
            first = 5 * swapped
            for flipped in (0, 1):
                to_row = aligned((x + flipped * (1 - 2 * x)) * rows, 16)
                plan.append((first + flipped, 0, rows, 0, cut, 2, to_row, aligned(side * ff, BLOCK)))
            plan.append((first + 3, 0, shard, 0, cut, 2, 0, aligned(side * ff + cut, BLOCK)))
            plan.append((first + 4, 0, ff // 8, 0, half, 3, 0, aligned(side * half, BLOCK)))
            to_row = aligned(side * rows, 16)
            later = 3 * half + width + BLOCK
            for third in range(3):
                for part in (0, 1):
                    plan.append(
                        (first + 2, 0, rows, part * later + third * half, half, 0, to_row,
                         third * width + part * half)
                    )
            plan.append((first + 2, 0, rows, 3 * half, width, 1, to_row, 0))
            plan.append((first + 2, 0, rows, 3 * half + width, BLOCK, 4, to_row, 0))
        return plan

    *shards, squares = collect_call(
        parts, collect_plan, 24,
        [(shard, 3 * width), (shard, width), (shard, 2 * ff), (ff // 8, width), (shard, BLOCK)],
    )
    shards[4] = shards[4][:, :6].T
    squares = squares[:1]
    for how in (SWAP_Y, SWAP_Z[1], SWAP_Z[2]):
        squares = squares + swap(squares, how)
    grad_norm = jnp.sqrt(squares[0, :1])
    updates = updated(masters, firsts, seconds, shards, grad_norm, clip_norm)
    return (result, grad_input, *updates, grad_norm)


def solution(mesh):
    rows_split = P(("dp", "head"), None)
    mats, vecs = P("dp", None), P(None, "dp")
    state = (mats,) * 4 + (vecs,)
    in_specs = (rows_split, P("dp"), rows_split, P()) + state * 3
    out_specs = (rows_split, rows_split) + (mats,) * 16 + (vecs,) * 4 + (P(),)
    cube = mesh.shape["dp"] == 8 and mesh.shape["head"] == 4
    body = cube_body if cube else plain_body
    return jax.shard_map(body, mesh=mesh, in_specs=in_specs, out_specs=out_specs, check_vma=False)
```

```python
import functools

import jax
import jax.numpy as jnp
import numpy as np
from jax import lax
from jax.experimental import pallas as pl
from jax.experimental.pallas import tpu as pltpu
from jax.sharding import PartitionSpec as P

HEADS = 12
HEAD_DIM = 64
BLOCK = 128
HALO = 384
VMEM_GRANT = 60 * 1024 * 1024

SLOPES = [2.0 ** (-(level + 1)) for level in range(8)] + [
    2.0 ** (-(level + 0.5)) for level in range(4)
]
LN_EPS = 1e-05
BETA_ONE = 0.9
BETA_TWO = 0.999
ADAM_EPS = 1e-08
CORR_ONE = 1.0 - 0.9**10
CORR_TWO = 1.0 - 0.999**10
RATE_MAT = 0.05
RATE_VEC = 0.5
DECAY_MAT = 0.01

SHORT = pl.CostEstimate(flops=1000, bytes_accessed=1000, transcendentals=0)

BF16 = jnp.bfloat16
F32 = jnp.float32


def dot_nn(left, right):
    return lax.dot_general(left, right, (((1,), (0,)), ((), ())), preferred_element_type=F32)


def dot_nt(left, right):
    return lax.dot_general(left, right, (((1,), (1,)), ((), ())), preferred_element_type=F32)


def dot_tn(left, right):
    return lax.dot_general(left, right, (((0,), (0,)), ((), ())), preferred_element_type=F32)


def part_copies(parts, plan, whole, sems, first):
    copies = []
    for number, (part, lead, row, rows, to_row, to_col) in enumerate(plan):
        source = parts[part] if lead is None else parts[part].at[lead]
        cols = source.shape[1]
        copies.append(
            pltpu.make_async_copy(
                source.at[pl.ds(row, rows), :],
                whole.at[pl.ds(to_row, rows), pl.ds(to_col, cols)],
                sems.at[first + number],
            )
        )
    return copies


def aligned(value, unit):
    return value if isinstance(value, int) else pl.multiple_of(value, unit)


def qkv_kernel(plan_of, n_pieces, window_ref, *refs):
    pieces = refs[:n_pieces]
    pairs_ref, whole_ref, sems = refs[n_pieces:]

    @pl.when(pl.program_id(0) == 0)
    def _():
        copies = part_copies(pieces, plan_of(), whole_ref, sems, 0)
        for copy in copies:
            copy.start()
        for copy in copies:
            copy.wait()

    rows = window_ref[...]
    for third in range(3):
        width = 6 * BLOCK
        part = dot_nn(rows, whole_ref[:, third * width : (third + 1) * width]).astype(BF16)
        for pair in range(6):
            pairs_ref[third * 6 + pair] = part[:, pair * BLOCK : (pair + 1) * BLOCK]


def qkv_call(window, pieces, plan_of, n_copies):
    rows, width = window.shape
    tile = HALO
    return pl.pallas_call(
        functools.partial(qkv_kernel, plan_of, len(pieces)),
        grid=(rows // tile,),
        in_specs=[pl.BlockSpec((tile, width), lambda i: (i, 0))]
        + [pl.BlockSpec(memory_space=pl.ANY)] * len(pieces),
        out_specs=[
            pl.BlockSpec((18, tile, BLOCK), lambda i: (0, i, 0)),
            pl.BlockSpec((width, 3 * width), lambda i: (0, 0)),
        ],
        out_shape=[
            jax.ShapeDtypeStruct((18, rows, BLOCK), BF16),
            jax.ShapeDtypeStruct((width, 3 * width), BF16),
        ],
        scratch_shapes=[pltpu.SemaphoreType.DMA((n_copies,))],
        compiler_params=pltpu.CompilerParams(
            dimension_semantics=("arbitrary",), vmem_limit_bytes=VMEM_GRANT
        ),
        cost_estimate=SHORT,
        name="qkv",
    )(window, *pieces)


def run_of(ids_ref, block, count):
    own = ids_ref[block]

    def same(other):
        inside = jnp.logical_and(other >= 0, other < count)
        return jnp.logical_and(inside, ids_ref[jnp.clip(other, 0, count - 1)] == own)

    before = sum(same(block - step).astype(jnp.int32) for step in (1, 2, 3))
    after = sum(same(block + step).astype(jnp.int32) for step in (1, 2, 3))
    return block - before, before + after + 1


def halves_of(rows):
    lane = lax.broadcasted_iota(jnp.int32, rows.shape, 1)
    zero = jnp.zeros_like(rows)
    return jnp.concatenate(
        (jnp.where(lane < HEAD_DIM, rows, zero), jnp.where(lane < HEAD_DIM, zero, rows)), axis=0
    )


def fill_distances(table_ref):
    shape = table_ref.shape
    key = lax.broadcasted_iota(jnp.int32, shape, 0) - 3 * BLOCK
    query = lax.broadcasted_iota(jnp.int32, shape, 1)
    table_ref[...] = jnp.abs(key - query).astype(F32)


def biased_scores(keys, query_pair, distances, slope_one, slope_two):
    bias = jnp.concatenate((distances * slope_one, distances * slope_two), axis=1)
    return dot_nt(keys, query_pair) - bias


def untwine(both):
    mine = jnp.concatenate(
        (both[:HEAD_DIM, :BLOCK], both[HEAD_DIM:, BLOCK:]), axis=0
    )
    return mine.T


GROUP = 3


def attend_kernel(first_own, n_own, first_group, ids_ref, slopes_ref, q_ref, k_ref, v_ref, ctx_ref, lse_ref, table_ref):
    group = first_group + pl.program_id(0)
    count = q_ref.shape[1] // BLOCK

    @pl.when(pl.program_id(0) == 0)
    def _():
        fill_distances(table_ref)

    def one_block(number, carry):
        block = number + first_own
        start, length = run_of(ids_ref, block, count)
        rows = pl.ds(pl.multiple_of(block * BLOCK, BLOCK), BLOCK)
        place = pl.ds(pl.multiple_of(number * BLOCK, BLOCK), BLOCK)
        shift = pl.multiple_of((3 - (block - start)) * BLOCK, BLOCK)

        def variant(blocks):
            width = blocks * BLOCK
            span = pl.ds(pl.multiple_of(start * BLOCK, BLOCK), width)
            distances = table_ref[pl.ds(shift, width), :]
            for pair in range(GROUP):
                head = 2 * (group * GROUP + pair)
                queries = halves_of(q_ref[pair, rows, :] * jnp.asarray(HEAD_DIM**-0.5, BF16))
                scores = biased_scores(
                    k_ref[pair, span, :], queries, distances, slopes_ref[head], slopes_ref[head + 1]
                )
                peak = jnp.max(scores, axis=0, keepdims=True)
                terms = jnp.exp(scores - peak)
                total = jnp.sum(terms, axis=0, keepdims=True)
                lse = peak + jnp.log(total)
                lse_ref[pair, 0:1, place] = lse[:, :BLOCK]
                lse_ref[pair, 1:2, place] = lse[:, BLOCK:]
                probs = (terms * (1.0 / total)).astype(BF16)
                both = dot_tn(v_ref[pair, span, :], probs)
                ctx_ref[place, pair * BLOCK : (pair + 1) * BLOCK] = untwine(both).astype(BF16)

        for blocks in (1, 2, 4):
            @pl.when(length == blocks)
            def _(blocks=blocks):
                variant(blocks)

        return carry

    lax.fori_loop(0, n_own, one_block, 0)


def attend_call(ids, slopes, pairs, own_rows, first_group, n_groups):
    rows = pairs.shape[1]
    steps = 6 // GROUP
    wide = GROUP * BLOCK
    part = lambda third: pl.BlockSpec(
        (GROUP, rows, BLOCK), lambda g: (third * steps + first_group + g, 0, 0)
    )
    smem = pl.BlockSpec(memory_space=pltpu.SMEM)
    return pl.pallas_call(
        functools.partial(attend_kernel, HALO // BLOCK, own_rows // BLOCK, first_group),
        grid=(n_groups,),
        in_specs=[smem, smem, part(0), part(1), part(2)],
        out_specs=[
            pl.BlockSpec((own_rows, wide), lambda g: (0, g)),
            pl.BlockSpec((GROUP, 2, own_rows), lambda g: (g, 0, 0)),
        ],
        out_shape=[
            jax.ShapeDtypeStruct((own_rows, n_groups * wide), BF16),
            jax.ShapeDtypeStruct((n_groups * GROUP, 2, own_rows), F32),
        ],
        scratch_shapes=[pltpu.VMEM((7 * BLOCK, BLOCK), F32)],
        compiler_params=pltpu.CompilerParams(
            dimension_semantics=("arbitrary",), vmem_limit_bytes=VMEM_GRANT
        ),
        cost_estimate=SHORT,
        name="attend",
    )(ids, slopes, pairs, pairs, pairs)


def attend_back_kernel(
    first_own, n_own, first_group, ids_ref, slopes_ref, q_ref, k_ref, v_ref, stats_ref, dctx_ref,
    dq_ref, dk_ref, dv_ref, table_ref, dk_sum, dv_sum,
):
    group = first_group + pl.program_id(0)
    count = q_ref.shape[1] // BLOCK

    @pl.when(pl.program_id(0) == 0)
    def _():
        fill_distances(table_ref)

    dk_sum[...] = jnp.zeros_like(dk_sum)
    dv_sum[...] = jnp.zeros_like(dv_sum)
    end_own = first_own + n_own

    def one_block(block, carry):
        start, length = run_of(ids_ref, block, count)
        own = jnp.logical_and(block >= first_own, block < end_own)
        key_start = jnp.where(own, start, jnp.maximum(start, first_own))
        key_end = jnp.where(own, start + length, jnp.minimum(start + length, end_own))
        whole = key_end - key_start == 3
        key_start = jnp.where(whole, start, key_start)
        n_keys = jnp.where(whole, length, key_end - key_start)
        rows = pl.ds(pl.multiple_of(block * BLOCK, BLOCK), BLOCK)
        place = pl.ds(pl.multiple_of(block * BLOCK, BLOCK), BLOCK)
        shift = pl.multiple_of((3 - (block - key_start)) * BLOCK, BLOCK)

        def variant(blocks):
            width = blocks * BLOCK
            span = pl.ds(pl.multiple_of(key_start * BLOCK, BLOCK), width)
            distances = table_ref[pl.ds(shift, width), :]
            for pair in range(GROUP):
                head = 2 * (group * GROUP + pair)
                lanes = slice(pair * BLOCK, (pair + 1) * BLOCK)
                keys = k_ref[pair, span, :]
                queries = halves_of(q_ref[pair, rows, :] * jnp.asarray(HEAD_DIM**-0.5, BF16))
                scores = biased_scores(
                    keys, queries, distances, slopes_ref[head], slopes_ref[head + 1]
                )
                lse = jnp.concatenate(
                    (stats_ref[pair, 0:1, rows], stats_ref[pair, 1:2, rows]), axis=1
                )
                inner = jnp.concatenate(
                    (stats_ref[pair, 2:3, rows], stats_ref[pair, 3:4, rows]), axis=1
                )
                soft = jnp.exp(scores - lse)
                dctx = halves_of(dctx_ref[rows, lanes])
                dsoft = dot_nt(v_ref[pair, span, :], dctx)
                dv_sum[pair, span, :] += dot_nn(soft.astype(BF16), dctx)
                dscores = (soft * (dsoft - inner)).astype(BF16)
                dk_sum[pair, span, :] += dot_nn(dscores, queries)
                dq_ref[place, lanes] = (untwine(dot_tn(keys, dscores)) * HEAD_DIM**-0.5).astype(BF16)

        for blocks in (1, 2, 4):
            @pl.when(n_keys == blocks)
            def _(blocks=blocks):
                variant(blocks)

        return carry

    lax.fori_loop(0, count, one_block, 0)
    mine = pl.ds(first_own * BLOCK, n_own * BLOCK)
    for pair in range(GROUP):
        lanes = slice(pair * BLOCK, (pair + 1) * BLOCK)
        dk_ref[:, lanes] = dk_sum[pair, mine, :].astype(BF16)
        dv_ref[:, lanes] = dv_sum[pair, mine, :].astype(BF16)


def attend_back_call(ids, slopes, pairs, stats, dctx, own_rows, first_group, n_groups):
    rows = pairs.shape[1]
    steps = 6 // GROUP
    wide = GROUP * BLOCK
    part = lambda third: pl.BlockSpec(
        (GROUP, rows, BLOCK), lambda g: (third * steps + first_group + g, 0, 0)
    )
    smem = pl.BlockSpec(memory_space=pltpu.SMEM)
    return pl.pallas_call(
        functools.partial(attend_back_kernel, HALO // BLOCK, own_rows // BLOCK, first_group),
        grid=(n_groups,),
        in_specs=[
            smem, smem, part(0), part(1), part(2),
            pl.BlockSpec((GROUP, 4, rows), lambda g: (first_group + g, 0, 0)),
            pl.BlockSpec((rows, wide), lambda g: (0, first_group + g)),
        ],
        out_specs=[pl.BlockSpec((rows, wide), lambda g: (0, g))]
        + [pl.BlockSpec((own_rows, wide), lambda g: (0, g))] * 2,
        out_shape=[jax.ShapeDtypeStruct((rows, n_groups * wide), BF16)]
        + [jax.ShapeDtypeStruct((own_rows, n_groups * wide), BF16)] * 2,
        scratch_shapes=[
            pltpu.VMEM((7 * BLOCK, BLOCK), F32),
            pltpu.VMEM((GROUP, rows, BLOCK), F32),
            pltpu.VMEM((GROUP, rows, BLOCK), F32),
        ],
        compiler_params=pltpu.CompilerParams(
            dimension_semantics=("arbitrary",), vmem_limit_bytes=VMEM_GRANT
        ),
        cost_estimate=SHORT,
        name="attend_back",
    )(ids, slopes, pairs, pairs, pairs, stats, dctx)


FF_TILE = 512


def row_mean(values):
    return jnp.mean(values, axis=1, keepdims=True)


def norm_parts(values):
    center = values - row_mean(values)
    scale = lax.rsqrt(row_mean(center * center) + LN_EPS)
    return center * scale, scale


def norm_back(grad_unit, unit, scale):
    return scale * (grad_unit - row_mean(grad_unit) - unit * row_mean(grad_unit * unit))


def column_sum(values):
    return jnp.sum(values, axis=0, keepdims=True)


def middle_kernel(plans_of, slot_of, counts, n_pieces, ctx_ref, tok_ref, cot_ref, vec_ref, *refs):
    pieces = refs[:n_pieces]
    (result_ref, hidden_ref, dgu_ref, dffn_ref, low_ref, dattn_ref, dfirst_ref, dctx_ref,
     inner_ref, sums_ref, w_out, w_gu, w_down, gate_grad, up_grad, sems) = refs[n_pieces:]
    step = pl.program_id(0)
    width = tok_ref.shape[1]
    half = width // 2
    ff = w_down.shape[0]
    slot = slot_of()

    def copies_of(which):
        target = (w_out, w_gu, w_down)[which]
        return part_copies(pieces, plans_of()[which], target, sems, sum(counts[:which]))

    def wait_for(which):
        @pl.when(step == 0)
        def _():
            for copy in copies_of(which):
                copy.wait()

    @pl.when(step == 0)
    def _():
        sums_ref[...] = jnp.zeros_like(sums_ref)
        for which in range(3):
            for copy in copies_of(which):
                copy.start()

    gain_one, shift_one = vec_ref[0:1, :], vec_ref[1:2, :]
    gain_two, shift_two = vec_ref[2:3, :], vec_ref[3:4, :]
    wait_for(0)
    attn = dot_nn(ctx_ref[...], w_out[...])
    unit_one, scale_one = norm_parts(tok_ref[...].astype(F32) + attn + vec_ref[4:5, :])
    normed = unit_one * gain_one + shift_one
    low = normed.astype(BF16)
    low_ref[...] = low
    wait_for(1)
    for tile in range(ff // FF_TILE):
        cols = slice(tile * FF_TILE, (tile + 1) * FF_TILE)
        gate = dot_nn(low, w_gu[:, cols])
        up = dot_nn(low, w_gu[:, ff + tile * FF_TILE : ff + (tile + 1) * FF_TILE])
        below = 0.5 + 0.5 * lax.erf(gate * np.float32(0.5**0.5))
        gelu = gate * below
        slope = below + gate * (jnp.exp(-0.5 * gate * gate) * np.float32((2.0 * np.pi) ** -0.5))
        hidden = (gelu * up).astype(BF16)
        hidden_ref[:, cols] = hidden
        gate_grad[:, cols] = up * slope
        up_grad[:, cols] = gelu
    wait_for(2)
    ffn = dot_nn(hidden_ref[...], w_down[...])
    unit_two, scale_two = norm_parts(normed + ffn + vec_ref[5:6, :])
    result_ref[...] = (unit_two * gain_two + shift_two).astype(BF16)
    grad = cot_ref[...].astype(F32)
    sums_ref[2:3, :] += column_sum(grad * unit_two)
    sums_ref[3:4, :] += column_sum(grad)
    dsecond = norm_back(grad * gain_two, unit_two, scale_two)
    sums_ref[5:6, :] += column_sum(dsecond)
    dffn = dsecond.astype(BF16)
    dffn_ref[slot] = dffn[:, :half]
    dffn_ref[1 - slot] = dffn[:, half:]
    dnormed = dsecond
    for tile in range(ff // FF_TILE):
        cols = slice(tile * FF_TILE, (tile + 1) * FF_TILE)
        ups = slice(ff + tile * FF_TILE, ff + (tile + 1) * FF_TILE)
        dhidden = dot_nt(dffn, w_down[cols, :])
        dgate = (dhidden * gate_grad[:, cols]).astype(BF16)
        dup = (dhidden * up_grad[:, cols]).astype(BF16)
        chunk, place = divmod(tile * FF_TILE, ff // 2)
        dgu_ref[slot, chunk, :, place : place + FF_TILE] = dgate
        dgu_ref[1 - slot, chunk, :, place : place + FF_TILE] = dup
        dnormed = dnormed + dot_nt(dgate, w_gu[:, cols]) + dot_nt(dup, w_gu[:, ups])
    sums_ref[0:1, :] += column_sum(dnormed * unit_one)
    sums_ref[1:2, :] += column_sum(dnormed)
    dfirst = norm_back(dnormed * gain_one, unit_one, scale_one)
    sums_ref[4:5, :] += column_sum(dfirst)
    dfirst_ref[...] = dfirst
    dattn = dfirst.astype(BF16)
    dattn_ref[...] = dattn
    dctx = dot_nt(dattn, w_out[...]).astype(BF16)
    dctx_ref[...] = dctx
    head = lax.broadcasted_iota(jnp.int32, (16, width), 0)
    column = lax.broadcasted_iota(jnp.int32, (16, width), 1)
    member = jnp.where(column // HEAD_DIM == head, 1.0, 0.0).astype(BF16)
    product = dctx.astype(F32) * ctx_ref[...].astype(F32)
    high = product.astype(BF16)
    rest = (product - high.astype(F32)).astype(BF16)
    inner_ref[...] = dot_nt(member, high) + dot_nt(member, rest)


def middle_call(ctx, tokens, cotangent, vectors, pieces, plans_of, slot_of, counts):
    rows, width = tokens.shape
    ff = 4 * width
    tile = 384
    by_rows = lambda cols: pl.BlockSpec((tile, cols), lambda i: (i, 0))
    paired = lambda cols: pl.BlockSpec((2, tile, cols), lambda i: (0, i, 0))
    shaped = lambda cols, dtype: jax.ShapeDtypeStruct((rows, cols), dtype)
    return pl.pallas_call(
        functools.partial(middle_kernel, plans_of, slot_of, counts, len(pieces)),
        grid=(rows // tile,),
        in_specs=[by_rows(width)] * 3
        + [pl.BlockSpec((8, width), lambda i: (0, 0))]
        + [pl.BlockSpec(memory_space=pl.ANY)] * len(pieces),
        out_specs=[
            by_rows(width), by_rows(ff),
            pl.BlockSpec((2, 2, tile, ff // 2), lambda i: (0, 0, i, 0)),
            paired(width // 2), by_rows(width),
            by_rows(width), by_rows(width), by_rows(width),
            pl.BlockSpec((16, tile), lambda i: (0, i)),
            pl.BlockSpec((8, width), lambda i: (0, 0)),
        ],
        out_shape=[
            shaped(width, BF16), shaped(ff, BF16), jax.ShapeDtypeStruct((2, 2, rows, ff // 2), BF16),
            jax.ShapeDtypeStruct((2, rows, width // 2), BF16), shaped(width, BF16),
            shaped(width, BF16), shaped(width, F32),
            shaped(width, BF16),
            jax.ShapeDtypeStruct((16, rows), F32),
            jax.ShapeDtypeStruct((8, width), F32),
        ],
        scratch_shapes=[
            pltpu.VMEM((width, width), BF16),
            pltpu.VMEM((width, 2 * ff), BF16),
            pltpu.VMEM((ff, width), BF16),
            pltpu.VMEM((tile, ff), F32),
            pltpu.VMEM((tile, ff), F32),
            pltpu.SemaphoreType.DMA((sum(counts),)),
        ],
        compiler_params=pltpu.CompilerParams(
            dimension_semantics=("arbitrary",), vmem_limit_bytes=VMEM_GRANT
        ),
        cost_estimate=SHORT,
        name="middle",
    )(ctx, tokens, cotangent, vectors, *pieces)


def group_grad_kernel(tokens_ref, dq_ref, dk_ref, dv_ref, mine_ref, away_ref):
    own_rows = tokens_ref.shape[0]
    lower = lax.axis_index("head") % 2 == 0
    for third, ref in enumerate((dq_ref, dk_ref, dv_ref)):
        skip = HALO if third == 0 else 0
        cols = slice(third * ref.shape[1], (third + 1) * ref.shape[1])
        values = dot_tn(tokens_ref[...], ref[skip : skip + own_rows, :]).astype(BF16)
        halves = values.reshape(8, 2, values.shape[0] // 16, values.shape[1])
        mine_ref[:, :, cols] = jnp.where(lower, halves[:, 0], halves[:, 1])
        away_ref[:, :, cols] = jnp.where(lower, halves[:, 1], halves[:, 0])


def group_grad_call(tokens, back):
    width = tokens.shape[1]
    half = jax.ShapeDtypeStruct((8, width // 16, 3 * back[1].shape[1]), BF16)
    vmem = pl.BlockSpec(memory_space=pltpu.VMEM)
    return pl.pallas_call(
        group_grad_kernel,
        in_specs=[vmem] * 4,
        out_specs=[vmem] * 2,
        out_shape=[half] * 2,
        compiler_params=pltpu.CompilerParams(vmem_limit_bytes=VMEM_GRANT),
        cost_estimate=SHORT,
        name="group_grad",
    )(tokens, *back)


def collect_kernel(plan_of, n_parts, *refs):
    parts, wholes = refs[:n_parts], refs[n_parts : n_parts + 5]
    total_ref, sems = refs[n_parts + 5 :]
    copies = []
    for number, entry in enumerate(plan_of()):
        part, row, rows, col, cols, whole, to_row, to_col = entry
        copies.append(
            pltpu.make_async_copy(
                parts[part].at[pl.ds(row, rows), pl.ds(col, cols)],
                wholes[whole].at[pl.ds(to_row, rows), pl.ds(to_col, cols)],
                sems.at[number],
            )
        )
    for copy in copies:
        copy.start()
    for copy in copies:
        copy.wait()
    total = jnp.zeros((1, 1), F32)
    for whole in wholes:
        values = whole[...].astype(F32)
        total = total + jnp.sum(jnp.sum(values * values, axis=0, keepdims=True), axis=1, keepdims=True)
    total_ref[...] = jnp.broadcast_to(total, total_ref.shape)


def collect_call(parts, plan_of, n_copies, shapes):
    vmem = pl.BlockSpec(memory_space=pltpu.VMEM)
    return pl.pallas_call(
        functools.partial(collect_kernel, plan_of, len(parts)),
        in_specs=[pl.BlockSpec(memory_space=pl.ANY)] * len(parts),
        out_specs=[vmem] * 6,
        out_shape=[jax.ShapeDtypeStruct(shape, BF16) for shape in shapes]
        + [jax.ShapeDtypeStruct((8, BLOCK), F32)],
        scratch_shapes=[pltpu.SemaphoreType.DMA((n_copies,))],
        compiler_params=pltpu.CompilerParams(vmem_limit_bytes=VMEM_GRANT),
        cost_estimate=SHORT,
        name="collect",
    )(*parts)


def adam_kernel(factor_ref, *refs):
    masters, firsts, seconds, grads, outs = (
        refs[:5], refs[5:10], refs[10:15], refs[15:20], refs[20:]
    )
    factor = factor_ref[0]
    for index in range(5):
        rate, decay = (RATE_MAT, DECAY_MAT) if index < 4 else (RATE_VEC, 0.0)
        new_ref, first_ref, second_ref, copy_ref = outs[4 * index : 4 * index + 4]
        master = masters[index][...]
        clipped = grads[index][...].astype(F32) * factor
        first = BETA_ONE * firsts[index][...] + (1.0 - BETA_ONE) * clipped
        second = BETA_TWO * seconds[index][...] + (1.0 - BETA_TWO) * clipped * clipped
        direction = first / CORR_ONE / (jnp.sqrt(second / CORR_TWO) + ADAM_EPS)
        new = master - rate * (direction + decay * master)
        new_ref[...] = new
        first_ref[...] = first
        second_ref[...] = second
        copy_ref[...] = new.astype(BF16)


def adam_call(masters, firsts, seconds, grads, factor):
    steps = 6

    def spec(array, index):
        rows, cols = array.shape
        if index == 4:
            return pl.BlockSpec((rows, cols), lambda i: (0, 0))
        return pl.BlockSpec((rows, cols // steps), lambda i: (0, i))

    specs = [spec(array, index) for index, array in enumerate(masters)]
    return pl.pallas_call(
        adam_kernel,
        grid=(steps,),
        in_specs=[pl.BlockSpec(memory_space=pltpu.SMEM)] + specs * 4,
        out_specs=[one for one in specs for _ in range(4)],
        out_shape=[
            jax.ShapeDtypeStruct(array.shape, dtype)
            for array in masters
            for dtype in (F32, F32, F32, BF16)
        ],
        compiler_params=pltpu.CompilerParams(
            dimension_semantics=("arbitrary",), vmem_limit_bytes=VMEM_GRANT
        ),
        cost_estimate=SHORT,
        name="adam",
    )(factor, *masters, *firsts, *seconds, *grads)


def halo_window(rows, groups):
    left = lax.ppermute(rows[-HALO:], "head", [(i, i + 1) for i in range(groups - 1)])
    right = lax.ppermute(rows[:HALO], "head", [(i + 1, i) for i in range(groups - 1)])
    return jnp.concatenate((left, rows, right), axis=0)


def halo_stats(lse, inner, groups):
    stats = jnp.concatenate((lse, inner[:HEADS].reshape(6, 2, -1)), axis=1)
    left = lax.ppermute(stats[:, :, -HALO:], "head", [(i, i + 1) for i in range(groups - 1)])
    right = lax.ppermute(stats[:, :, :HALO], "head", [(i + 1, i) for i in range(groups - 1)])
    return jnp.concatenate((left, stats, right), axis=2)


def slope_table():
    return jnp.asarray(np.array(SLOPES), F32)


def window_ids(segment_ids, own_rows):
    block_ids = segment_ids.reshape(-1, BLOCK)[:, 0]
    edge = HALO // BLOCK
    padded = jnp.pad(block_ids, (edge, edge), constant_values=-1)
    own_blocks = own_rows // BLOCK
    return lax.dynamic_slice_in_dim(
        padded, lax.axis_index("head") * own_blocks, own_blocks + 2 * edge
    )


def updated(masters, firsts, seconds, shards, grad_norm, clip_norm):
    factor = jnp.minimum(1.0, clip_norm / grad_norm)
    return adam_call(masters, firsts, seconds, shards, factor)


def plain_body(tokens, segment_ids, cotangent, clip_norm, *state):
    masters, firsts, seconds = state[:5], state[5:10], state[10:]
    groups = lax.axis_size("head")
    own_rows, width = tokens.shape
    low = [w.astype(BF16) for w in masters]
    window = halo_window(tokens, groups)
    full = [lax.all_gather(w, "dp", axis=0, tiled=True) for w in low[:4]]
    full_vec = lax.all_gather(low[4], "dp", axis=1, tiled=True)
    vectors = jnp.pad(full_vec.astype(F32), ((0, 2), (0, 0)))
    slopes = slope_table()
    ids = window_ids(segment_ids, own_rows)

    def whole_plan(part, rows):
        return [(part, None, 0, rows, 0, 0)]

    pairs, whole_qkv = qkv_call(window, [full[0]], lambda: whole_plan(0, width), 1)
    ctx, lse = attend_call(ids, slopes, pairs, own_rows, 0, 6 // GROUP)
    result, hidden, dgu, dffn, normed_low, dattn, dfirst, dctx, inner, sums = middle_call(
        ctx, tokens, cotangent, vectors, full[1:],
        lambda: (whole_plan(0, width), whole_plan(1, width), whole_plan(2, 4 * width)),
        lambda: 0, (1, 1, 1),
    )
    joined_back = lambda two: jnp.concatenate((two[0], two[1]), axis=1)
    grad_down = dot_tn(hidden, joined_back(dffn)).astype(BF16)
    grad_gu = dot_tn(normed_low, jnp.concatenate((dgu[0, 0], dgu[0, 1], dgu[1, 0], dgu[1, 1]), axis=1)).astype(BF16)
    grad_out = dot_tn(ctx, dattn).astype(BF16)
    dctx_window = halo_window(dctx, groups)
    stats = halo_stats(lse, inner, groups)
    dq, dk, dv = attend_back_call(ids, slopes, pairs, stats, dctx_window, own_rows, 0, 6 // GROUP)
    dq = dq[HALO:-HALO]
    djoined = jnp.concatenate((dq, dk, dv), axis=1)
    grad_qkv = dot_tn(tokens, djoined).astype(BF16)
    grad_input = dfirst + dot_nt(djoined, whole_qkv)

    def reduced(grad):
        share = lax.psum_scatter(grad, "dp", scatter_dimension=0, tiled=True)
        return lax.psum(share, "head").astype(F32)

    shards = [reduced(grad) for grad in (grad_qkv, grad_out, grad_gu, grad_down)]
    vec_sum = lax.psum(sums[:6], ("dp", "head"))
    vec_cols = masters[4].shape[1]
    shards.append(
        lax.dynamic_slice_in_dim(vec_sum, lax.axis_index("dp") * vec_cols, vec_cols, axis=1)
    )
    squares = sum(jnp.sum(piece * piece) for piece in shards)
    grad_norm = jnp.sqrt(lax.psum(squares, "dp")).reshape(1)
    updates = updated(masters, firsts, seconds, shards, grad_norm, clip_norm)
    return (result, grad_input, *updates, grad_norm)


SWAP_CORE = ("head", [(i, i ^ 1) for i in range(4)])
SWAP_X = ("head", [(i, i ^ 2) for i in range(4)])
SWAP_Y = ("dp", [(i, i ^ 1) for i in range(8)])
SWAP_Z = [None] + [("dp", [(i, i ^ (2 * step)) for i in range(8)]) for step in (1, 2, 3)]


MIDDLE_Z = ("dp", [(2, 4), (3, 5), (4, 2), (5, 3)])
OUTWARD_Z = ("dp", [(2, 0), (3, 1), (4, 6), (5, 7)])


def swap(values, how):
    return lax.ppermute(values, *how)


def position():
    dp, head = lax.axis_index("dp"), lax.axis_index("head")
    return dp // 2, dp % 2, head // 2, head % 2


def half_of(values, which, axis):
    size = values.shape[axis] // 2
    return lax.dynamic_slice_in_dim(values, which * size, size, axis)


def together(*values):
    return lax.optimization_barrier(values)


def slab_sum(mine, other):
    return (mine.astype(F32) + other.astype(F32)).astype(BF16)


def split(values, which, axis):
    return (
        lax.dynamic_index_in_dim(values, which, axis, keepdims=False),
        lax.dynamic_index_in_dim(values, 1 - which, axis, keepdims=False),
    )


def split_y(values, y):
    return split(values.reshape(4, 2, *values.shape[1:]), y, 1)


def trade(values, axis):
    return lax.all_to_all(values, axis, split_axis=0, concat_axis=0, tiled=True)


def cube_body(tokens, segment_ids, cotangent, clip_norm, *state):
    masters, firsts, seconds = state[:5], state[5:10], state[10:]
    groups = lax.axis_size("head")
    own_rows, width = tokens.shape
    ff = 4 * width
    half = width // 2
    shard = width // 8
    z, y, x, core = position()
    low = [w.astype(BF16) for w in masters]
    slopes = slope_table()
    ids = window_ids(segment_ids, own_rows)

    own_q = half_of(low[0], core, 1)
    own_g = half_of(half_of(low[2], core, 1), x, 0)
    vec_rows = jnp.pad(low[4], ((0, 10), (0, half - shard)))
    own_r = jnp.concatenate((half_of(low[3], core, 1), half_of(low[1], core, 1), vec_rows), axis=0)
    rest_rows = own_r.shape[0]

    def pair_of(own):
        return jnp.stack((own, swap(own, SWAP_Z[1])))

    pair_q, pair_r, own_g = together(pair_of(own_q), pair_of(own_r), own_g)

    mid_q = swap(pair_q, MIDDLE_Z)
    pair_y_q = swap(pair_q, SWAP_Y)
    pair_g = pair_of(own_g)
    window = halo_window(tokens, groups)
    mid_q, pair_y_q, pair_g, pair_r, window = together(mid_q, pair_y_q, pair_g, pair_r, window)

    end_q = swap(mid_q, OUTWARD_Z)
    mid_g = swap(pair_g, MIDDLE_Z)
    pair_y_g = swap(pair_g, SWAP_Y)
    xpair_g = swap(pair_g, SWAP_X)
    near_q = [pair_q, pair_y_q]
    across_q = [swap(part, SWAP_CORE) for part in near_q]
    end_q, mid_g, pair_y_g, pair_g, xpair_g, pair_r, *rest = together(
        end_q, mid_g, pair_y_g, pair_g, xpair_g, pair_r, *near_q, *across_q
    )
    near_q, across_q = rest[:2], rest[2:]

    other_q = mid_q + end_q
    other_y_q = swap(other_q, SWAP_Y)
    end_g = swap(mid_g, OUTWARD_Z)
    mid_r = swap(pair_r, MIDDLE_Z)
    xpair_y_g = swap(pair_y_g, SWAP_X)
    other_q, other_y_q, end_g, xpair_y_g, mid_r, pair_r = together(
        other_q, other_y_q, end_g, xpair_y_g, mid_r, pair_r
    )

    other_g = mid_g + end_g
    other_y_g = swap(other_g, SWAP_Y)
    end_r = swap(mid_r, OUTWARD_Z)
    xother_g = swap(other_g, SWAP_X)
    late_q = [other_q, other_y_q]
    late_across_q = [swap(part, SWAP_CORE) for part in late_q]

    def pair_rows(z, y):
        near = z + 1 - 2 * (z % 2)
        far_one, far_two = 2 - z // 2, 3 - 3 * (z // 2)
        first = [[z * 2 + y, near * 2 + y], [z * 2 + 1 - y, near * 2 + 1 - y]]
        return first + [
            [far_one * 2 + y, far_two * 2 + y], [far_one * 2 + 1 - y, far_two * 2 + 1 - y]
        ]

    def qkv_plan():
        z, y, _, core = position()
        plan = []
        for swapped in (0, 1):
            col = aligned((core + swapped * (1 - 2 * core)) * (3 * half), BLOCK)
            for part, rows in enumerate(pair_rows(z, y)):
                for index, dp in enumerate(rows):
                    plan.append((part + 4 * swapped, index, 0, shard, aligned(dp * shard, 32), col))
        return plan

    pairs, whole_qkv = qkv_call(window, near_q + late_q + across_q + late_across_q, qkv_plan, 16)
    pairs, other_g, other_y_g, end_r = together(pairs, other_g, other_y_g, end_r)

    xother_y_g = swap(other_y_g, SWAP_X)
    other_r = mid_r + end_r
    pair_y_r, other_y_r = swap(pair_r, SWAP_Y), swap(other_r, SWAP_Y)
    near_r = [pair_r, other_r]
    across_r = [swap(part, SWAP_CORE) for part in near_r]
    near_g = [pair_g, pair_y_g, other_g, other_y_g, xpair_g, xpair_y_g]
    across_g = [swap(part, SWAP_CORE) for part in near_g]
    ctx, lse = attend_call(ids, slopes, pairs, own_rows, 0, 2)
    ctx, lse, xother_g, xother_y_g, pair_y_r, other_y_r, *rest = together(
        ctx, lse, xother_g, xother_y_g, pair_y_r, other_y_r, *near_r, *across_r, *across_g
    )
    near_r, across_r, across_g = rest[:2], rest[2:4], rest[4:]
    late_g = [xother_g, xother_y_g]
    parts_g = near_g + late_g + across_g + [swap(part, SWAP_CORE) for part in late_g]
    parts_r = [near_r[0], pair_y_r, near_r[1], other_y_r]
    order = jnp.stack([index for indices in pair_rows(z, y) for index in indices])
    vec_all = jnp.concatenate([part[:, rest_rows - 16 : rest_rows - 8, :shard] for part in parts_r])
    vec_all = vec_all.astype(F32)
    parts_r = parts_r + [
        across_r[0], swap(pair_y_r, SWAP_CORE), across_r[1], swap(other_y_r, SWAP_CORE)
    ]
    vectors = jnp.zeros_like(vec_all).at[order].set(vec_all).transpose(1, 0, 2).reshape(8, width)

    def middle_plans():
        z, y, x, core = position()
        rows_of = pair_rows(z, y)
        out_plan, gu_plan, down_plan = [], [], []
        for swapped in (0, 1):
            side = core + swapped * (1 - 2 * core)
            for part in range(4):
                for index, dp in enumerate(rows_of[part]):
                    col = aligned(side * half, BLOCK)
                    place = (16 + 4 * swapped + part, index)
                    out_plan.append((*place, ff // 8, shard, aligned(dp * shard, 32), col))
                    down_plan.append((*place, 0, ff // 8, aligned(dp * (ff // 8), BLOCK), col))
            for flipped in (0, 1):
                rows_half = x + flipped * (1 - 2 * x)
                for part in range(4):
                    for index, dp in enumerate(rows_of[part]):
                        place = (4 * flipped + part, index)
                        row = aligned(dp * shard + rows_half * (shard // 2), 16)
                        gu_plan.append(
                            (8 * swapped + place[0], place[1], 0, shard // 2, row, aligned(side * ff, BLOCK))
                        )
        return out_plan, gu_plan, down_plan

    result, hidden, dgu, dffn, normed_low, dattn, dfirst, dctx, inner, sums = middle_call(
        ctx, tokens, cotangent, vectors, parts_g + parts_r,
        middle_plans, lambda: position()[3], (16, 32, 16),
    )

    def core_keep(left, right, theirs):
        return (dot_tn(left, right) + theirs.astype(F32)).astype(BF16)

    their_down = swap(dot_tn(hidden, dffn[1]).astype(BF16), SWAP_CORE)
    one_theirs = swap(dot_tn(normed_low, dgu[1, 0]).astype(BF16), SWAP_CORE)
    two_theirs = dot_tn(normed_low, dgu[1, 1]).astype(BF16)
    their_down, one_theirs, two_theirs, hidden, normed_low = together(
        their_down, one_theirs, two_theirs, hidden, normed_low
    )
    two_theirs = swap(two_theirs, SWAP_CORE)
    sum_down = core_keep(hidden, dffn[0], their_down)
    sum_one = core_keep(normed_low, dgu[0, 0], one_theirs).reshape(8, 2, shard // 2, ff // 2)
    sum_down, sum_one, two_theirs, normed_low = together(sum_down, sum_one, two_theirs, normed_low)
    share_down = lax.psum_scatter(sum_down, "dp", scatter_dimension=0, tiled=True)

    def core_rows(grad):
        mine, away = split(grad.reshape(8, 2, shard // 2, grad.shape[1]), core, 1)
        return slab_sum(mine, swap(away, SWAP_CORE))

    def z_send(values):
        others = (z + 1 - 2 * (z % 2), (z + 2) % 4, 3 - z)
        return [
            swap(lax.dynamic_index_in_dim(values, other, 0, keepdims=False), SWAP_Z[step])
            for step, other in zip((1, 2, 3), others)
        ]

    def z_sum(values, theirs):
        total = lax.dynamic_index_in_dim(values, z, 0, keepdims=False).astype(F32)
        for other in theirs:
            total = total + other.astype(F32)
        return total.astype(BF16)

    cut = ff // 2
    one, one_away = split(sum_one, x, 1)
    two, two_away = split_y(core_keep(normed_low, dgu[0, 1], two_theirs).reshape(8, shard, cut), y)
    dctx_window = halo_window(dctx, groups)
    stats = halo_stats(lse, inner, groups)
    one, one_away, two, two_away, dctx_window, stats = together(
        one, one_away, two, two_away, dctx_window, stats
    )
    one_their = swap(one_away, SWAP_X)
    two_their = swap(two_away, SWAP_Y)
    vec_cols = jnp.pad(sums.astype(BF16).T, ((0, 0), (0, BLOCK - 8)))
    sum_ov = core_rows(jnp.concatenate((dot_tn(ctx, dattn).astype(BF16), vec_cols), axis=1))
    back_a = attend_back_call(ids, slopes, pairs, stats, dctx_window, own_rows, 0, 1)
    grad_a, grad_away = group_grad_call(tokens, back_a)
    one_their, two_their, dctx_window, sum_ov, grad_a, grad_away, *back_a = together(
        one_their, two_their, dctx_window, sum_ov, grad_a, grad_away, *back_a
    )
    grad_a = slab_sum(grad_a, swap(grad_away, SWAP_CORE))
    two = slab_sum(two, two_their)
    two_their = z_send(two)
    one = jnp.concatenate((slab_sum(one, one_their), grad_a, sum_ov), axis=2)
    one, one_away = split_y(one, y)
    one_their = swap(one_away, SWAP_Y)
    back_b = attend_back_call(ids, slopes, pairs, stats, dctx_window, own_rows, 1, 1)
    grad_b, grad_away = group_grad_call(tokens, back_b)
    one_their, share_down, grad_b, grad_away, *rest = together(
        one_their, share_down, grad_b, grad_away, *two_their, *back_b
    )
    two_their, back_b = rest[:3], rest[3:]

    one = slab_sum(one, one_their)
    one_their = z_send(one)
    grad_b = trade(slab_sum(grad_b, swap(grad_away, SWAP_CORE)), "dp")
    two_mine = z_sum(two, two_their)
    two_other = swap(two_mine, SWAP_X)
    down_other = swap(share_down, SWAP_X)
    djoined = jnp.concatenate(
        (back_a[0][HALO:-HALO], back_b[0][HALO:-HALO], back_a[1], back_b[1], back_a[2], back_b[2]), axis=1
    )
    grad_input = dfirst + dot_nt(djoined, whole_qkv)
    grad_b, two_other, down_other, grad_input, *one_their = together(
        grad_b, two_other, down_other, grad_input, *one_their
    )
    b_mine = jnp.sum(grad_b.astype(F32), axis=0).astype(BF16)
    one_mine = jnp.concatenate((z_sum(one, one_their), b_mine), axis=1)
    one_other = swap(one_mine, SWAP_X)
    two_sum, down_sum = slab_sum(two_mine, two_other), slab_sum(share_down, down_other)
    two_across, down_across = swap(two_sum, SWAP_CORE), swap(down_sum, SWAP_CORE)
    rest_sum = slab_sum(one_mine[:, cut:], one_other[:, cut:])
    parts = [
        one_mine, one_other, rest_sum, two_sum, down_sum,
        swap(one_mine, SWAP_CORE), swap(one_other, SWAP_CORE), swap(rest_sum, SWAP_CORE),
        two_across, down_across,
    ]

    def collect_plan():
        _, _, x, core = position()
        rows = shard // 2
        plan = []
        for swapped in (0, 1):
            side = core + swapped * (1 - 2 * core)
            first = 5 * swapped
            for flipped in (0, 1):
                to_row = aligned((x + flipped * (1 - 2 * x)) * rows, 16)
                plan.append((first + flipped, 0, rows, 0, cut, 2, to_row, aligned(side * ff, BLOCK)))
            plan.append((first + 3, 0, shard, 0, cut, 2, 0, aligned(side * ff + cut, BLOCK)))
            plan.append((first + 4, 0, ff // 8, 0, half, 3, 0, aligned(side * half, BLOCK)))
            to_row = aligned(side * rows, 16)
            later = 3 * half + width + BLOCK
            for third in range(3):
                for part in (0, 1):
                    plan.append(
                        (first + 2, 0, rows, part * later + third * half, half, 0, to_row,
                         third * width + part * half)
                    )
            plan.append((first + 2, 0, rows, 3 * half, width, 1, to_row, 0))
            plan.append((first + 2, 0, rows, 3 * half + width, BLOCK, 4, to_row, 0))
        return plan

    *shards, squares = collect_call(
        parts, collect_plan, 24,
        [(shard, 3 * width), (shard, width), (shard, 2 * ff), (ff // 8, width), (shard, BLOCK)],
    )
    shards[4] = shards[4][:, :6].T
    squares = squares[:1]
    for how in (SWAP_Y, SWAP_Z[1], SWAP_Z[2]):
        squares = squares + swap(squares, how)
    grad_norm = jnp.sqrt(squares[0, :1])
    updates = updated(masters, firsts, seconds, shards, grad_norm, clip_norm)
    return (result, grad_input, *updates, grad_norm)


def solution(mesh):
    rows_split = P(("dp", "head"), None)
    mats, vecs = P("dp", None), P(None, "dp")
    state = (mats,) * 4 + (vecs,)
    in_specs = (rows_split, P("dp"), rows_split, P()) + state * 3
    out_specs = (rows_split, rows_split) + (mats,) * 16 + (vecs,) * 4 + (P(),)
    cube = mesh.shape["dp"] == 8 and mesh.shape["head"] == 4
    body = cube_body if cube else plain_body
    return jax.shard_map(body, mesh=mesh, in_specs=in_specs, out_specs=out_specs, check_vma=False)
```

```python
import functools

import jax
import jax.numpy as jnp
import numpy as np
from jax import lax
from jax.experimental import pallas as pl
from jax.experimental.pallas import tpu as pltpu
from jax.sharding import PartitionSpec as P

HEADS = 12
HEAD_DIM = 64
BLOCK = 128
HALO = 384
VMEM_GRANT = 60 * 1024 * 1024

SLOPES = [2.0 ** (-(level + 1)) for level in range(8)] + [
    2.0 ** (-(level + 0.5)) for level in range(4)
]
LN_EPS = 1e-05
BETA_ONE = 0.9
BETA_TWO = 0.999
ADAM_EPS = 1e-08
CORR_ONE = 1.0 - 0.9**10
CORR_TWO = 1.0 - 0.999**10
RATE_MAT = 0.05
RATE_VEC = 0.5
DECAY_MAT = 0.01

SHORT = pl.CostEstimate(flops=1000, bytes_accessed=1000, transcendentals=0)

BF16 = jnp.bfloat16
F32 = jnp.float32


def dot_nn(left, right):
    return lax.dot_general(left, right, (((1,), (0,)), ((), ())), preferred_element_type=F32)


def dot_nt(left, right):
    return lax.dot_general(left, right, (((1,), (1,)), ((), ())), preferred_element_type=F32)


def dot_tn(left, right):
    return lax.dot_general(left, right, (((0,), (0,)), ((), ())), preferred_element_type=F32)


def part_copies(parts, plan, whole, sems, first):
    copies = []
    for number, (part, lead, row, rows, to_row, to_col) in enumerate(plan):
        source = parts[part] if lead is None else parts[part].at[lead]
        cols = source.shape[1]
        copies.append(
            pltpu.make_async_copy(
                source.at[pl.ds(row, rows), :],
                whole.at[pl.ds(to_row, rows), pl.ds(to_col, cols)],
                sems.at[first + number],
            )
        )
    return copies


def aligned(value, unit):
    return value if isinstance(value, int) else pl.multiple_of(value, unit)


def qkv_kernel(plan_of, n_pieces, window_ref, *refs):
    pieces = refs[:n_pieces]
    pairs_ref, whole_ref, sems = refs[n_pieces:]

    @pl.when(pl.program_id(0) == 0)
    def _():
        copies = part_copies(pieces, plan_of(), whole_ref, sems, 0)
        for copy in copies:
            copy.start()
        for copy in copies:
            copy.wait()

    rows = window_ref[...]
    for third in range(3):
        width = 6 * BLOCK
        part = dot_nn(rows, whole_ref[:, third * width : (third + 1) * width]).astype(BF16)
        for pair in range(6):
            pairs_ref[third * 6 + pair] = part[:, pair * BLOCK : (pair + 1) * BLOCK]


def qkv_call(window, pieces, plan_of, n_copies):
    rows, width = window.shape
    tile = HALO
    return pl.pallas_call(
        functools.partial(qkv_kernel, plan_of, len(pieces)),
        grid=(rows // tile,),
        in_specs=[pl.BlockSpec((tile, width), lambda i: (i, 0))]
        + [pl.BlockSpec(memory_space=pl.ANY)] * len(pieces),
        out_specs=[
            pl.BlockSpec((18, tile, BLOCK), lambda i: (0, i, 0)),
            pl.BlockSpec((width, 3 * width), lambda i: (0, 0)),
        ],
        out_shape=[
            jax.ShapeDtypeStruct((18, rows, BLOCK), BF16),
            jax.ShapeDtypeStruct((width, 3 * width), BF16),
        ],
        scratch_shapes=[pltpu.SemaphoreType.DMA((n_copies,))],
        compiler_params=pltpu.CompilerParams(
            dimension_semantics=("arbitrary",), vmem_limit_bytes=VMEM_GRANT
        ),
        cost_estimate=SHORT,
        name="qkv",
    )(window, *pieces)


def run_of(ids_ref, block, count):
    own = ids_ref[block]

    def same(other):
        inside = jnp.logical_and(other >= 0, other < count)
        return jnp.logical_and(inside, ids_ref[jnp.clip(other, 0, count - 1)] == own)

    before = sum(same(block - step).astype(jnp.int32) for step in (1, 2, 3))
    after = sum(same(block + step).astype(jnp.int32) for step in (1, 2, 3))
    return block - before, before + after + 1


def halves_of(rows):
    lane = lax.broadcasted_iota(jnp.int32, rows.shape, 1)
    zero = jnp.zeros_like(rows)
    return jnp.concatenate(
        (jnp.where(lane < HEAD_DIM, rows, zero), jnp.where(lane < HEAD_DIM, zero, rows)), axis=0
    )


def fill_distances(table_ref):
    shape = table_ref.shape
    key = lax.broadcasted_iota(jnp.int32, shape, 0) - 3 * BLOCK
    query = lax.broadcasted_iota(jnp.int32, shape, 1)
    table_ref[...] = jnp.abs(key - query).astype(F32)


def biased_scores(keys, query_pair, distances, slope_one, slope_two):
    bias = jnp.concatenate((distances * slope_one, distances * slope_two), axis=1)
    return dot_nt(keys, query_pair) - bias


def untwine(both):
    mine = jnp.concatenate(
        (both[:HEAD_DIM, :BLOCK], both[HEAD_DIM:, BLOCK:]), axis=0
    )
    return mine.T


GROUP = 3


def attend_kernel(first_own, n_own, first_group, ids_ref, slopes_ref, q_ref, k_ref, v_ref, ctx_ref, lse_ref, table_ref):
    group = first_group + pl.program_id(0)
    count = q_ref.shape[1] // BLOCK

    @pl.when(pl.program_id(0) == 0)
    def _():
        fill_distances(table_ref)

    def one_block(number, carry):
        block = number + first_own
        start, length = run_of(ids_ref, block, count)
        rows = pl.ds(pl.multiple_of(block * BLOCK, BLOCK), BLOCK)
        place = pl.ds(pl.multiple_of(number * BLOCK, BLOCK), BLOCK)
        shift = pl.multiple_of((3 - (block - start)) * BLOCK, BLOCK)

        def variant(blocks):
            width = blocks * BLOCK
            span = pl.ds(pl.multiple_of(start * BLOCK, BLOCK), width)
            distances = table_ref[pl.ds(shift, width), :]
            for pair in range(GROUP):
                head = 2 * (group * GROUP + pair)
                queries = halves_of(q_ref[pair, rows, :] * jnp.asarray(HEAD_DIM**-0.5, BF16))
                scores = biased_scores(
                    k_ref[pair, span, :], queries, distances, slopes_ref[head], slopes_ref[head + 1]
                )
                peak = jnp.max(scores, axis=0, keepdims=True)
                terms = jnp.exp(scores - peak)
                total = jnp.sum(terms, axis=0, keepdims=True)
                lse = peak + jnp.log(total)
                lse_ref[pair, 0:1, place] = lse[:, :BLOCK]
                lse_ref[pair, 1:2, place] = lse[:, BLOCK:]
                probs = (terms * (1.0 / total)).astype(BF16)
                both = dot_tn(v_ref[pair, span, :], probs)
                ctx_ref[place, pair * BLOCK : (pair + 1) * BLOCK] = untwine(both).astype(BF16)

        for blocks in (1, 2, 4):
            @pl.when(length == blocks)
            def _(blocks=blocks):
                variant(blocks)

        return carry

    lax.fori_loop(0, n_own, one_block, 0)


def attend_call(ids, slopes, pairs, own_rows, first_group, n_groups):
    rows = pairs.shape[1]
    steps = 6 // GROUP
    wide = GROUP * BLOCK
    part = lambda third: pl.BlockSpec(
        (GROUP, rows, BLOCK), lambda g: (third * steps + first_group + g, 0, 0)
    )
    smem = pl.BlockSpec(memory_space=pltpu.SMEM)
    return pl.pallas_call(
        functools.partial(attend_kernel, HALO // BLOCK, own_rows // BLOCK, first_group),
        grid=(n_groups,),
        in_specs=[smem, smem, part(0), part(1), part(2)],
        out_specs=[
            pl.BlockSpec((own_rows, wide), lambda g: (0, g)),
            pl.BlockSpec((GROUP, 2, own_rows), lambda g: (g, 0, 0)),
        ],
        out_shape=[
            jax.ShapeDtypeStruct((own_rows, n_groups * wide), BF16),
            jax.ShapeDtypeStruct((n_groups * GROUP, 2, own_rows), F32),
        ],
        scratch_shapes=[pltpu.VMEM((7 * BLOCK, BLOCK), F32)],
        compiler_params=pltpu.CompilerParams(
            dimension_semantics=("arbitrary",), vmem_limit_bytes=VMEM_GRANT
        ),
        cost_estimate=SHORT,
        name="attend",
    )(ids, slopes, pairs, pairs, pairs)


def attend_back_kernel(
    first_own, n_own, first_group, ids_ref, slopes_ref, q_ref, k_ref, v_ref, stats_ref, dctx_ref,
    dq_ref, dk_ref, dv_ref, table_ref, dk_sum, dv_sum,
):
    group = first_group + pl.program_id(0)
    count = q_ref.shape[1] // BLOCK

    @pl.when(pl.program_id(0) == 0)
    def _():
        fill_distances(table_ref)

    dk_sum[...] = jnp.zeros_like(dk_sum)
    dv_sum[...] = jnp.zeros_like(dv_sum)
    end_own = first_own + n_own

    def one_block(block, carry):
        start, length = run_of(ids_ref, block, count)
        own = jnp.logical_and(block >= first_own, block < end_own)
        key_start = jnp.where(own, start, jnp.maximum(start, first_own))
        key_end = jnp.where(own, start + length, jnp.minimum(start + length, end_own))
        whole = key_end - key_start == 3
        key_start = jnp.where(whole, start, key_start)
        n_keys = jnp.where(whole, length, key_end - key_start)
        rows = pl.ds(pl.multiple_of(block * BLOCK, BLOCK), BLOCK)
        place = pl.ds(pl.multiple_of(block * BLOCK, BLOCK), BLOCK)
        shift = pl.multiple_of((3 - (block - key_start)) * BLOCK, BLOCK)

        def variant(blocks):
            width = blocks * BLOCK
            span = pl.ds(pl.multiple_of(key_start * BLOCK, BLOCK), width)
            distances = table_ref[pl.ds(shift, width), :]
            for pair in range(GROUP):
                head = 2 * (group * GROUP + pair)
                lanes = slice(pair * BLOCK, (pair + 1) * BLOCK)
                keys = k_ref[pair, span, :]
                queries = halves_of(q_ref[pair, rows, :] * jnp.asarray(HEAD_DIM**-0.5, BF16))
                scores = biased_scores(
                    keys, queries, distances, slopes_ref[head], slopes_ref[head + 1]
                )
                lse = jnp.concatenate(
                    (stats_ref[pair, 0:1, rows], stats_ref[pair, 1:2, rows]), axis=1
                )
                inner = jnp.concatenate(
                    (stats_ref[pair, 2:3, rows], stats_ref[pair, 3:4, rows]), axis=1
                )
                soft = jnp.exp(scores - lse)
                dctx = halves_of(dctx_ref[rows, lanes])
                dsoft = dot_nt(v_ref[pair, span, :], dctx)
                dv_sum[pair, span, :] += dot_nn(soft.astype(BF16), dctx)
                dscores = (soft * (dsoft - inner)).astype(BF16)
                dk_sum[pair, span, :] += dot_nn(dscores, queries)
                dq_ref[place, lanes] = (untwine(dot_tn(keys, dscores)) * HEAD_DIM**-0.5).astype(BF16)

        for blocks in (1, 2, 4):
            @pl.when(n_keys == blocks)
            def _(blocks=blocks):
                variant(blocks)

        return carry

    lax.fori_loop(0, count, one_block, 0)
    mine = pl.ds(first_own * BLOCK, n_own * BLOCK)
    for pair in range(GROUP):
        lanes = slice(pair * BLOCK, (pair + 1) * BLOCK)
        dk_ref[:, lanes] = dk_sum[pair, mine, :].astype(BF16)
        dv_ref[:, lanes] = dv_sum[pair, mine, :].astype(BF16)


def attend_back_call(ids, slopes, pairs, stats, dctx, own_rows, first_group, n_groups):
    rows = pairs.shape[1]
    steps = 6 // GROUP
    wide = GROUP * BLOCK
    part = lambda third: pl.BlockSpec(
        (GROUP, rows, BLOCK), lambda g: (third * steps + first_group + g, 0, 0)
    )
    smem = pl.BlockSpec(memory_space=pltpu.SMEM)
    return pl.pallas_call(
        functools.partial(attend_back_kernel, HALO // BLOCK, own_rows // BLOCK, first_group),
        grid=(n_groups,),
        in_specs=[
            smem, smem, part(0), part(1), part(2),
            pl.BlockSpec((GROUP, 4, rows), lambda g: (first_group + g, 0, 0)),
            pl.BlockSpec((rows, wide), lambda g: (0, first_group + g)),
        ],
        out_specs=[pl.BlockSpec((rows, wide), lambda g: (0, g))]
        + [pl.BlockSpec((own_rows, wide), lambda g: (0, g))] * 2,
        out_shape=[jax.ShapeDtypeStruct((rows, n_groups * wide), BF16)]
        + [jax.ShapeDtypeStruct((own_rows, n_groups * wide), BF16)] * 2,
        scratch_shapes=[
            pltpu.VMEM((7 * BLOCK, BLOCK), F32),
            pltpu.VMEM((GROUP, rows, BLOCK), F32),
            pltpu.VMEM((GROUP, rows, BLOCK), F32),
        ],
        compiler_params=pltpu.CompilerParams(
            dimension_semantics=("arbitrary",), vmem_limit_bytes=VMEM_GRANT
        ),
        cost_estimate=SHORT,
        name="attend_back",
    )(ids, slopes, pairs, pairs, pairs, stats, dctx)


FF_TILE = 512


def row_mean(values):
    return jnp.mean(values, axis=1, keepdims=True)


def norm_parts(values):
    center = values - row_mean(values)
    scale = lax.rsqrt(row_mean(center * center) + LN_EPS)
    return center * scale, scale


def norm_back(grad_unit, unit, scale):
    return scale * (grad_unit - row_mean(grad_unit) - unit * row_mean(grad_unit * unit))


def column_sum(values):
    return jnp.sum(values, axis=0, keepdims=True)


def middle_kernel(plans_of, slot_of, counts, n_pieces, ctx_ref, tok_ref, cot_ref, vec_ref, *refs):
    pieces = refs[:n_pieces]
    (result_ref, hidden_ref, dgu_ref, dffn_ref, low_ref, dattn_ref, dfirst_ref, dctx_ref,
     inner_ref, sums_ref, w_out, w_gu, w_down, gate_grad, up_grad, sems) = refs[n_pieces:]
    step = pl.program_id(0)
    width = tok_ref.shape[1]
    half = width // 2
    ff = w_down.shape[0]
    slot = slot_of()

    def copies_of(which):
        target = (w_out, w_gu, w_down)[which]
        return part_copies(pieces, plans_of()[which], target, sems, sum(counts[:which]))

    def wait_for(which):
        @pl.when(step == 0)
        def _():
            for copy in copies_of(which):
                copy.wait()

    @pl.when(step == 0)
    def _():
        sums_ref[...] = jnp.zeros_like(sums_ref)
        for which in range(3):
            for copy in copies_of(which):
                copy.start()

    gain_one, shift_one = vec_ref[0:1, :], vec_ref[1:2, :]
    gain_two, shift_two = vec_ref[2:3, :], vec_ref[3:4, :]
    wait_for(0)
    attn = dot_nn(ctx_ref[...], w_out[...])
    unit_one, scale_one = norm_parts(tok_ref[...].astype(F32) + attn + vec_ref[4:5, :])
    normed = unit_one * gain_one + shift_one
    low = normed.astype(BF16)
    low_ref[...] = low
    wait_for(1)
    for tile in range(ff // FF_TILE):
        cols = slice(tile * FF_TILE, (tile + 1) * FF_TILE)
        gate = dot_nn(low, w_gu[:, cols])
        up = dot_nn(low, w_gu[:, ff + tile * FF_TILE : ff + (tile + 1) * FF_TILE])
        below = 0.5 + 0.5 * lax.erf(gate * np.float32(0.5**0.5))
        gelu = gate * below
        slope = below + gate * (jnp.exp(-0.5 * gate * gate) * np.float32((2.0 * np.pi) ** -0.5))
        hidden = (gelu * up).astype(BF16)
        hidden_ref[:, cols] = hidden
        gate_grad[:, cols] = up * slope
        up_grad[:, cols] = gelu
    wait_for(2)
    ffn = dot_nn(hidden_ref[...], w_down[...])
    unit_two, scale_two = norm_parts(normed + ffn + vec_ref[5:6, :])
    result_ref[...] = (unit_two * gain_two + shift_two).astype(BF16)
    grad = cot_ref[...].astype(F32)
    sums_ref[2:3, :] += column_sum(grad * unit_two)
    sums_ref[3:4, :] += column_sum(grad)
    dsecond = norm_back(grad * gain_two, unit_two, scale_two)
    sums_ref[5:6, :] += column_sum(dsecond)
    dffn = dsecond.astype(BF16)
    dffn_ref[slot] = dffn[:, :half]
    dffn_ref[1 - slot] = dffn[:, half:]
    dnormed = dsecond
    for tile in range(ff // FF_TILE):
        cols = slice(tile * FF_TILE, (tile + 1) * FF_TILE)
        ups = slice(ff + tile * FF_TILE, ff + (tile + 1) * FF_TILE)
        dhidden = dot_nt(dffn, w_down[cols, :])
        dgate = (dhidden * gate_grad[:, cols]).astype(BF16)
        dup = (dhidden * up_grad[:, cols]).astype(BF16)
        chunk, place = divmod(tile * FF_TILE, ff // 2)
        dgu_ref[slot, chunk, :, place : place + FF_TILE] = dgate
        dgu_ref[1 - slot, chunk, :, place : place + FF_TILE] = dup
        dnormed = dnormed + dot_nt(dgate, w_gu[:, cols]) + dot_nt(dup, w_gu[:, ups])
    sums_ref[0:1, :] += column_sum(dnormed * unit_one)
    sums_ref[1:2, :] += column_sum(dnormed)
    dfirst = norm_back(dnormed * gain_one, unit_one, scale_one)
    sums_ref[4:5, :] += column_sum(dfirst)
    dfirst_ref[...] = dfirst
    dattn = dfirst.astype(BF16)
    dattn_ref[...] = dattn
    dctx = dot_nt(dattn, w_out[...]).astype(BF16)
    dctx_ref[...] = dctx
    head = lax.broadcasted_iota(jnp.int32, (16, width), 0)
    column = lax.broadcasted_iota(jnp.int32, (16, width), 1)
    member = jnp.where(column // HEAD_DIM == head, 1.0, 0.0).astype(BF16)
    product = dctx.astype(F32) * ctx_ref[...].astype(F32)
    high = product.astype(BF16)
    rest = (product - high.astype(F32)).astype(BF16)
    inner_ref[...] = dot_nt(member, high) + dot_nt(member, rest)


def middle_call(ctx, tokens, cotangent, vectors, pieces, plans_of, slot_of, counts):
    rows, width = tokens.shape
    ff = 4 * width
    tile = 384
    by_rows = lambda cols: pl.BlockSpec((tile, cols), lambda i: (i, 0))
    paired = lambda cols: pl.BlockSpec((2, tile, cols), lambda i: (0, i, 0))
    shaped = lambda cols, dtype: jax.ShapeDtypeStruct((rows, cols), dtype)
    return pl.pallas_call(
        functools.partial(middle_kernel, plans_of, slot_of, counts, len(pieces)),
        grid=(rows // tile,),
        in_specs=[by_rows(width)] * 3
        + [pl.BlockSpec((8, width), lambda i: (0, 0))]
        + [pl.BlockSpec(memory_space=pl.ANY)] * len(pieces),
        out_specs=[
            by_rows(width), by_rows(ff),
            pl.BlockSpec((2, 2, tile, ff // 2), lambda i: (0, 0, i, 0)),
            paired(width // 2), by_rows(width),
            by_rows(width), by_rows(width), by_rows(width),
            pl.BlockSpec((16, tile), lambda i: (0, i)),
            pl.BlockSpec((8, width), lambda i: (0, 0)),
        ],
        out_shape=[
            shaped(width, BF16), shaped(ff, BF16), jax.ShapeDtypeStruct((2, 2, rows, ff // 2), BF16),
            jax.ShapeDtypeStruct((2, rows, width // 2), BF16), shaped(width, BF16),
            shaped(width, BF16), shaped(width, F32),
            shaped(width, BF16),
            jax.ShapeDtypeStruct((16, rows), F32),
            jax.ShapeDtypeStruct((8, width), F32),
        ],
        scratch_shapes=[
            pltpu.VMEM((width, width), BF16),
            pltpu.VMEM((width, 2 * ff), BF16),
            pltpu.VMEM((ff, width), BF16),
            pltpu.VMEM((tile, ff), F32),
            pltpu.VMEM((tile, ff), F32),
            pltpu.SemaphoreType.DMA((sum(counts),)),
        ],
        compiler_params=pltpu.CompilerParams(
            dimension_semantics=("arbitrary",), vmem_limit_bytes=VMEM_GRANT
        ),
        cost_estimate=SHORT,
        name="middle",
    )(ctx, tokens, cotangent, vectors, *pieces)


def group_grad_kernel(tokens_ref, dq_ref, dk_ref, dv_ref, mine_ref, away_ref):
    own_rows = tokens_ref.shape[0]
    lower = lax.axis_index("head") % 2 == 0
    for third, ref in enumerate((dq_ref, dk_ref, dv_ref)):
        skip = HALO if third == 0 else 0
        cols = slice(third * ref.shape[1], (third + 1) * ref.shape[1])
        values = dot_tn(tokens_ref[...], ref[skip : skip + own_rows, :]).astype(BF16)
        halves = values.reshape(8, 2, values.shape[0] // 16, values.shape[1])
        mine_ref[:, :, cols] = jnp.where(lower, halves[:, 0], halves[:, 1])
        away_ref[:, :, cols] = jnp.where(lower, halves[:, 1], halves[:, 0])


def group_grad_call(tokens, back):
    width = tokens.shape[1]
    half = jax.ShapeDtypeStruct((8, width // 16, 3 * back[1].shape[1]), BF16)
    vmem = pl.BlockSpec(memory_space=pltpu.VMEM)
    return pl.pallas_call(
        group_grad_kernel,
        in_specs=[vmem] * 4,
        out_specs=[vmem] * 2,
        out_shape=[half] * 2,
        compiler_params=pltpu.CompilerParams(vmem_limit_bytes=VMEM_GRANT),
        cost_estimate=SHORT,
        name="group_grad",
    )(tokens, *back)


def collect_kernel(plan_of, n_parts, *refs):
    parts, wholes = refs[:n_parts], refs[n_parts : n_parts + 5]
    total_ref, sems = refs[n_parts + 5 :]
    copies = []
    for number, entry in enumerate(plan_of()):
        part, row, rows, col, cols, whole, to_row, to_col = entry
        copies.append(
            pltpu.make_async_copy(
                parts[part].at[pl.ds(row, rows), pl.ds(col, cols)],
                wholes[whole].at[pl.ds(to_row, rows), pl.ds(to_col, cols)],
                sems.at[number],
            )
        )
    for copy in copies:
        copy.start()
    for copy in copies:
        copy.wait()
    total = jnp.zeros((1, 1), F32)
    for whole in wholes:
        values = whole[...].astype(F32)
        total = total + jnp.sum(jnp.sum(values * values, axis=0, keepdims=True), axis=1, keepdims=True)
    total_ref[...] = jnp.broadcast_to(total, total_ref.shape)


def collect_call(parts, plan_of, n_copies, shapes):
    vmem = pl.BlockSpec(memory_space=pltpu.VMEM)
    return pl.pallas_call(
        functools.partial(collect_kernel, plan_of, len(parts)),
        in_specs=[pl.BlockSpec(memory_space=pl.ANY)] * len(parts),
        out_specs=[vmem] * 6,
        out_shape=[jax.ShapeDtypeStruct(shape, BF16) for shape in shapes]
        + [jax.ShapeDtypeStruct((8, BLOCK), F32)],
        scratch_shapes=[pltpu.SemaphoreType.DMA((n_copies,))],
        compiler_params=pltpu.CompilerParams(vmem_limit_bytes=VMEM_GRANT),
        cost_estimate=SHORT,
        name="collect",
    )(*parts)


def adam_kernel(factor_ref, *refs):
    masters, firsts, seconds, grads, outs = (
        refs[:5], refs[5:10], refs[10:15], refs[15:20], refs[20:]
    )
    factor = factor_ref[0]
    for index in range(5):
        rate, decay = (RATE_MAT, DECAY_MAT) if index < 4 else (RATE_VEC, 0.0)
        new_ref, first_ref, second_ref, copy_ref = outs[4 * index : 4 * index + 4]
        master = masters[index][...]
        clipped = grads[index][...].astype(F32) * factor
        first = BETA_ONE * firsts[index][...] + (1.0 - BETA_ONE) * clipped
        second = BETA_TWO * seconds[index][...] + (1.0 - BETA_TWO) * clipped * clipped
        direction = first / CORR_ONE / (jnp.sqrt(second / CORR_TWO) + ADAM_EPS)
        new = master - rate * (direction + decay * master)
        new_ref[...] = new
        first_ref[...] = first
        second_ref[...] = second
        copy_ref[...] = new.astype(BF16)


def adam_call(masters, firsts, seconds, grads, factor):
    steps = 6

    def spec(array, index):
        rows, cols = array.shape
        if index == 4:
            return pl.BlockSpec((rows, cols), lambda i: (0, 0))
        return pl.BlockSpec((rows, cols // steps), lambda i: (0, i))

    specs = [spec(array, index) for index, array in enumerate(masters)]
    return pl.pallas_call(
        adam_kernel,
        grid=(steps,),
        in_specs=[pl.BlockSpec(memory_space=pltpu.SMEM)] + specs * 4,
        out_specs=[one for one in specs for _ in range(4)],
        out_shape=[
            jax.ShapeDtypeStruct(array.shape, dtype)
            for array in masters
            for dtype in (F32, F32, F32, BF16)
        ],
        compiler_params=pltpu.CompilerParams(
            dimension_semantics=("arbitrary",), vmem_limit_bytes=VMEM_GRANT
        ),
        cost_estimate=SHORT,
        name="adam",
    )(factor, *masters, *firsts, *seconds, *grads)


def halo_window(rows, groups):
    left = lax.ppermute(rows[-HALO:], "head", [(i, i + 1) for i in range(groups - 1)])
    right = lax.ppermute(rows[:HALO], "head", [(i + 1, i) for i in range(groups - 1)])
    return jnp.concatenate((left, rows, right), axis=0)


def halo_stats(lse, inner, groups):
    stats = jnp.concatenate((lse, inner[:HEADS].reshape(6, 2, -1)), axis=1)
    left = lax.ppermute(stats[:, :, -HALO:], "head", [(i, i + 1) for i in range(groups - 1)])
    right = lax.ppermute(stats[:, :, :HALO], "head", [(i + 1, i) for i in range(groups - 1)])
    return jnp.concatenate((left, stats, right), axis=2)


def slope_table():
    return jnp.asarray(np.array(SLOPES), F32)


def window_ids(segment_ids, own_rows):
    block_ids = segment_ids.reshape(-1, BLOCK)[:, 0]
    edge = HALO // BLOCK
    padded = jnp.pad(block_ids, (edge, edge), constant_values=-1)
    own_blocks = own_rows // BLOCK
    return lax.dynamic_slice_in_dim(
        padded, lax.axis_index("head") * own_blocks, own_blocks + 2 * edge
    )


def updated(masters, firsts, seconds, shards, grad_norm, clip_norm):
    factor = jnp.minimum(1.0, clip_norm / grad_norm)
    return adam_call(masters, firsts, seconds, shards, factor)


def plain_body(tokens, segment_ids, cotangent, clip_norm, *state):
    masters, firsts, seconds = state[:5], state[5:10], state[10:]
    groups = lax.axis_size("head")
    own_rows, width = tokens.shape
    low = [w.astype(BF16) for w in masters]
    window = halo_window(tokens, groups)
    full = [lax.all_gather(w, "dp", axis=0, tiled=True) for w in low[:4]]
    full_vec = lax.all_gather(low[4], "dp", axis=1, tiled=True)
    vectors = jnp.pad(full_vec.astype(F32), ((0, 2), (0, 0)))
    slopes = slope_table()
    ids = window_ids(segment_ids, own_rows)

    def whole_plan(part, rows):
        return [(part, None, 0, rows, 0, 0)]

    pairs, whole_qkv = qkv_call(window, [full[0]], lambda: whole_plan(0, width), 1)
    ctx, lse = attend_call(ids, slopes, pairs, own_rows, 0, 6 // GROUP)
    result, hidden, dgu, dffn, normed_low, dattn, dfirst, dctx, inner, sums = middle_call(
        ctx, tokens, cotangent, vectors, full[1:],
        lambda: (whole_plan(0, width), whole_plan(1, width), whole_plan(2, 4 * width)),
        lambda: 0, (1, 1, 1),
    )
    joined_back = lambda two: jnp.concatenate((two[0], two[1]), axis=1)
    grad_down = dot_tn(hidden, joined_back(dffn)).astype(BF16)
    grad_gu = dot_tn(normed_low, jnp.concatenate((dgu[0, 0], dgu[0, 1], dgu[1, 0], dgu[1, 1]), axis=1)).astype(BF16)
    grad_out = dot_tn(ctx, dattn).astype(BF16)
    dctx_window = halo_window(dctx, groups)
    stats = halo_stats(lse, inner, groups)
    dq, dk, dv = attend_back_call(ids, slopes, pairs, stats, dctx_window, own_rows, 0, 6 // GROUP)
    dq = dq[HALO:-HALO]
    djoined = jnp.concatenate((dq, dk, dv), axis=1)
    grad_qkv = dot_tn(tokens, djoined).astype(BF16)
    grad_input = dfirst + dot_nt(djoined, whole_qkv)

    def reduced(grad):
        share = lax.psum_scatter(grad, "dp", scatter_dimension=0, tiled=True)
        return lax.psum(share, "head").astype(F32)

    shards = [reduced(grad) for grad in (grad_qkv, grad_out, grad_gu, grad_down)]
    vec_sum = lax.psum(sums[:6], ("dp", "head"))
    vec_cols = masters[4].shape[1]
    shards.append(
        lax.dynamic_slice_in_dim(vec_sum, lax.axis_index("dp") * vec_cols, vec_cols, axis=1)
    )
    squares = sum(jnp.sum(piece * piece) for piece in shards)
    grad_norm = jnp.sqrt(lax.psum(squares, "dp")).reshape(1)
    updates = updated(masters, firsts, seconds, shards, grad_norm, clip_norm)
    return (result, grad_input, *updates, grad_norm)


SWAP_CORE = ("head", [(i, i ^ 1) for i in range(4)])
SWAP_X = ("head", [(i, i ^ 2) for i in range(4)])
SWAP_Y = ("dp", [(i, i ^ 1) for i in range(8)])
LINES_Z = [[0, 2, 4, 6], [1, 3, 5, 7]]
SWAP_Z = [None] + [("dp", [(i, i ^ (2 * step)) for i in range(8)]) for step in (1, 2, 3)]


MIDDLE_Z = ("dp", [(2, 4), (3, 5), (4, 2), (5, 3)])
OUTWARD_Z = ("dp", [(2, 0), (3, 1), (4, 6), (5, 7)])


def swap(values, how):
    return lax.ppermute(values, *how)


def position():
    dp, head = lax.axis_index("dp"), lax.axis_index("head")
    return dp // 2, dp % 2, head // 2, head % 2


def half_of(values, which, axis):
    size = values.shape[axis] // 2
    return lax.dynamic_slice_in_dim(values, which * size, size, axis)


def together(*values):
    return lax.optimization_barrier(values)


def slab_sum(mine, other):
    return (mine.astype(F32) + other.astype(F32)).astype(BF16)


def split(values, which, axis):
    return (
        lax.dynamic_index_in_dim(values, which, axis, keepdims=False),
        lax.dynamic_index_in_dim(values, 1 - which, axis, keepdims=False),
    )


def split_y(values, y):
    return split(values.reshape(4, 2, *values.shape[1:]), y, 1)


def trade_z(values):
    return lax.all_to_all(
        values, "dp", split_axis=0, concat_axis=0, tiled=True, axis_index_groups=LINES_Z
    )


def cube_body(tokens, segment_ids, cotangent, clip_norm, *state):
    masters, firsts, seconds = state[:5], state[5:10], state[10:]
    groups = lax.axis_size("head")
    own_rows, width = tokens.shape
    ff = 4 * width
    half = width // 2
    shard = width // 8
    z, y, x, core = position()
    low = [w.astype(BF16) for w in masters]
    slopes = slope_table()
    ids = window_ids(segment_ids, own_rows)

    own_q = half_of(low[0], core, 1)
    own_g = half_of(half_of(low[2], core, 1), x, 0)
    vec_rows = jnp.pad(low[4], ((0, 10), (0, half - shard)))
    own_r = jnp.concatenate((half_of(low[3], core, 1), half_of(low[1], core, 1), vec_rows), axis=0)
    rest_rows = own_r.shape[0]

    def pair_of(own):
        return jnp.stack((own, swap(own, SWAP_Z[1])))

    pair_q, pair_r, own_g = together(pair_of(own_q), pair_of(own_r), own_g)

    mid_q = swap(pair_q, MIDDLE_Z)
    pair_y_q = swap(pair_q, SWAP_Y)
    pair_g = pair_of(own_g)
    window = halo_window(tokens, groups)
    mid_q, pair_y_q, pair_g, pair_r, window = together(mid_q, pair_y_q, pair_g, pair_r, window)

    end_q = swap(mid_q, OUTWARD_Z)
    mid_g = swap(pair_g, MIDDLE_Z)
    pair_y_g = swap(pair_g, SWAP_Y)
    xpair_g = swap(pair_g, SWAP_X)
    near_q = [pair_q, pair_y_q]
    across_q = [swap(part, SWAP_CORE) for part in near_q]
    end_q, mid_g, pair_y_g, pair_g, xpair_g, pair_r, *rest = together(
        end_q, mid_g, pair_y_g, pair_g, xpair_g, pair_r, *near_q, *across_q
    )
    near_q, across_q = rest[:2], rest[2:]

    other_q = mid_q + end_q
    other_y_q = swap(other_q, SWAP_Y)
    end_g = swap(mid_g, OUTWARD_Z)
    mid_r = swap(pair_r, MIDDLE_Z)
    xpair_y_g = swap(pair_y_g, SWAP_X)
    other_q, other_y_q, end_g, xpair_y_g, mid_r, pair_r = together(
        other_q, other_y_q, end_g, xpair_y_g, mid_r, pair_r
    )

    other_g = mid_g + end_g
    other_y_g = swap(other_g, SWAP_Y)
    end_r = swap(mid_r, OUTWARD_Z)
    xother_g = swap(other_g, SWAP_X)
    late_q = [other_q, other_y_q]
    late_across_q = [swap(part, SWAP_CORE) for part in late_q]

    def pair_rows(z, y):
        near = z + 1 - 2 * (z % 2)
        far_one, far_two = 2 - z // 2, 3 - 3 * (z // 2)
        first = [[z * 2 + y, near * 2 + y], [z * 2 + 1 - y, near * 2 + 1 - y]]
        return first + [
            [far_one * 2 + y, far_two * 2 + y], [far_one * 2 + 1 - y, far_two * 2 + 1 - y]
        ]

    def qkv_plan():
        z, y, _, core = position()
        plan = []
        for swapped in (0, 1):
            col = aligned((core + swapped * (1 - 2 * core)) * (3 * half), BLOCK)
            for part, rows in enumerate(pair_rows(z, y)):
                for index, dp in enumerate(rows):
                    plan.append((part + 4 * swapped, index, 0, shard, aligned(dp * shard, 32), col))
        return plan

    pairs, whole_qkv = qkv_call(window, near_q + late_q + across_q + late_across_q, qkv_plan, 16)
    pairs, other_g, other_y_g, end_r = together(pairs, other_g, other_y_g, end_r)

    xother_y_g = swap(other_y_g, SWAP_X)
    other_r = mid_r + end_r
    pair_y_r, other_y_r = swap(pair_r, SWAP_Y), swap(other_r, SWAP_Y)
    near_r = [pair_r, other_r]
    across_r = [swap(part, SWAP_CORE) for part in near_r]
    near_g = [pair_g, pair_y_g, other_g, other_y_g, xpair_g, xpair_y_g]
    across_g = [swap(part, SWAP_CORE) for part in near_g]
    ctx, lse = attend_call(ids, slopes, pairs, own_rows, 0, 2)
    ctx, lse, xother_g, xother_y_g, pair_y_r, other_y_r, *rest = together(
        ctx, lse, xother_g, xother_y_g, pair_y_r, other_y_r, *near_r, *across_r, *across_g
    )
    near_r, across_r, across_g = rest[:2], rest[2:4], rest[4:]
    late_g = [xother_g, xother_y_g]
    parts_g = near_g + late_g + across_g + [swap(part, SWAP_CORE) for part in late_g]
    parts_r = [near_r[0], pair_y_r, near_r[1], other_y_r]
    order = jnp.stack([index for indices in pair_rows(z, y) for index in indices])
    vec_all = jnp.concatenate([part[:, rest_rows - 16 : rest_rows - 8, :shard] for part in parts_r])
    vec_all = vec_all.astype(F32)
    parts_r = parts_r + [
        across_r[0], swap(pair_y_r, SWAP_CORE), across_r[1], swap(other_y_r, SWAP_CORE)
    ]
    vectors = jnp.zeros_like(vec_all).at[order].set(vec_all).transpose(1, 0, 2).reshape(8, width)

    def middle_plans():
        z, y, x, core = position()
        rows_of = pair_rows(z, y)
        out_plan, gu_plan, down_plan = [], [], []
        for swapped in (0, 1):
            side = core + swapped * (1 - 2 * core)
            for part in range(4):
                for index, dp in enumerate(rows_of[part]):
                    col = aligned(side * half, BLOCK)
                    place = (16 + 4 * swapped + part, index)
                    out_plan.append((*place, ff // 8, shard, aligned(dp * shard, 32), col))
                    down_plan.append((*place, 0, ff // 8, aligned(dp * (ff // 8), BLOCK), col))
            for flipped in (0, 1):
                rows_half = x + flipped * (1 - 2 * x)
                for part in range(4):
                    for index, dp in enumerate(rows_of[part]):
                        place = (4 * flipped + part, index)
                        row = aligned(dp * shard + rows_half * (shard // 2), 16)
                        gu_plan.append(
                            (8 * swapped + place[0], place[1], 0, shard // 2, row, aligned(side * ff, BLOCK))
                        )
        return out_plan, gu_plan, down_plan

    result, hidden, dgu, dffn, normed_low, dattn, dfirst, dctx, inner, sums = middle_call(
        ctx, tokens, cotangent, vectors, parts_g + parts_r,
        middle_plans, lambda: position()[3], (16, 32, 16),
    )

    def core_keep(left, right, theirs):
        return (dot_tn(left, right) + theirs.astype(F32)).astype(BF16)

    their_down = swap(dot_tn(hidden, dffn[1]).astype(BF16), SWAP_CORE)
    one_theirs = swap(dot_tn(normed_low, dgu[1, 0]).astype(BF16), SWAP_CORE)
    two_theirs = dot_tn(normed_low, dgu[1, 1]).astype(BF16)
    their_down, one_theirs, two_theirs, hidden, normed_low = together(
        their_down, one_theirs, two_theirs, hidden, normed_low
    )
    two_theirs = swap(two_theirs, SWAP_CORE)
    sum_down = core_keep(hidden, dffn[0], their_down)
    sum_one = core_keep(normed_low, dgu[0, 0], one_theirs).reshape(8, 2, shard // 2, ff // 2)
    sum_down, sum_one, two_theirs, normed_low = together(sum_down, sum_one, two_theirs, normed_low)
    share_down = lax.psum_scatter(sum_down, "dp", scatter_dimension=0, tiled=True)

    def core_rows(grad):
        mine, away = split(grad.reshape(8, 2, shard // 2, grad.shape[1]), core, 1)
        return slab_sum(mine, swap(away, SWAP_CORE))

    def z_send(values):
        others = (z + 1 - 2 * (z % 2), (z + 2) % 4, 3 - z)
        return [
            swap(lax.dynamic_index_in_dim(values, other, 0, keepdims=False), SWAP_Z[step])
            for step, other in zip((1, 2, 3), others)
        ]

    def z_sum(values, theirs):
        total = lax.dynamic_index_in_dim(values, z, 0, keepdims=False).astype(F32)
        for other in theirs:
            total = total + other.astype(F32)
        return total.astype(BF16)

    cut = ff // 2
    one, one_away = split(sum_one, x, 1)
    two, two_away = split_y(core_keep(normed_low, dgu[0, 1], two_theirs).reshape(8, shard, cut), y)
    dctx_window = halo_window(dctx, groups)
    stats = halo_stats(lse, inner, groups)
    one, one_away, two, two_away, dctx_window, stats = together(
        one, one_away, two, two_away, dctx_window, stats
    )
    one_their = swap(one_away, SWAP_X)
    two_their = swap(two_away, SWAP_Y)
    vec_cols = jnp.pad(sums.astype(BF16).T, ((0, 0), (0, BLOCK - 8)))
    sum_ov = core_rows(jnp.concatenate((dot_tn(ctx, dattn).astype(BF16), vec_cols), axis=1))
    back_a = attend_back_call(ids, slopes, pairs, stats, dctx_window, own_rows, 0, 1)
    grad_a, grad_away = group_grad_call(tokens, back_a)
    one_their, two_their, dctx_window, sum_ov, grad_a, grad_away, *back_a = together(
        one_their, two_their, dctx_window, sum_ov, grad_a, grad_away, *back_a
    )
    grad_a = slab_sum(grad_a, swap(grad_away, SWAP_CORE))
    two = slab_sum(two, two_their)
    two_their = z_send(two)
    one = jnp.concatenate((slab_sum(one, one_their), grad_a, sum_ov), axis=2)
    one, one_away = split_y(one, y)
    one_their = swap(one_away, SWAP_Y)
    back_b = attend_back_call(ids, slopes, pairs, stats, dctx_window, own_rows, 1, 1)
    grad_b, grad_away = group_grad_call(tokens, back_b)
    one_their, share_down, grad_b, grad_away, *rest = together(
        one_their, share_down, grad_b, grad_away, *two_their, *back_b
    )
    two_their, back_b = rest[:3], rest[3:]

    one = slab_sum(one, one_their)
    one_their = z_send(one)
    b_y, b_away = split_y(slab_sum(grad_b, swap(grad_away, SWAP_CORE)), y)
    grad_b = trade_z(slab_sum(b_y, swap(b_away, SWAP_Y)))
    two_mine = z_sum(two, two_their)
    two_other = swap(two_mine, SWAP_X)
    down_other = swap(share_down, SWAP_X)
    djoined = jnp.concatenate(
        (back_a[0][HALO:-HALO], back_b[0][HALO:-HALO], back_a[1], back_b[1], back_a[2], back_b[2]), axis=1
    )
    grad_input = dfirst + dot_nt(djoined, whole_qkv)
    grad_b, two_other, down_other, grad_input, *one_their = together(
        grad_b, two_other, down_other, grad_input, *one_their
    )
    b_mine = jnp.sum(grad_b.astype(F32), axis=0).astype(BF16)
    one_mine = jnp.concatenate((z_sum(one, one_their), b_mine), axis=1)
    one_other = swap(one_mine, SWAP_X)
    two_sum, down_sum = slab_sum(two_mine, two_other), slab_sum(share_down, down_other)
    two_across, down_across = swap(two_sum, SWAP_CORE), swap(down_sum, SWAP_CORE)
    rest_sum = slab_sum(one_mine[:, cut:], one_other[:, cut:])
    parts = [
        one_mine, one_other, rest_sum, two_sum, down_sum,
        swap(one_mine, SWAP_CORE), swap(one_other, SWAP_CORE), swap(rest_sum, SWAP_CORE),
        two_across, down_across,
    ]

    def collect_plan():
        _, _, x, core = position()
        rows = shard // 2
        plan = []
        for swapped in (0, 1):
            side = core + swapped * (1 - 2 * core)
            first = 5 * swapped
            for flipped in (0, 1):
                to_row = aligned((x + flipped * (1 - 2 * x)) * rows, 16)
                plan.append((first + flipped, 0, rows, 0, cut, 2, to_row, aligned(side * ff, BLOCK)))
            plan.append((first + 3, 0, shard, 0, cut, 2, 0, aligned(side * ff + cut, BLOCK)))
            plan.append((first + 4, 0, ff // 8, 0, half, 3, 0, aligned(side * half, BLOCK)))
            to_row = aligned(side * rows, 16)
            later = 3 * half + width + BLOCK
            for third in range(3):
                for part in (0, 1):
                    plan.append(
                        (first + 2, 0, rows, part * later + third * half, half, 0, to_row,
                         third * width + part * half)
                    )
            plan.append((first + 2, 0, rows, 3 * half, width, 1, to_row, 0))
            plan.append((first + 2, 0, rows, 3 * half + width, BLOCK, 4, to_row, 0))
        return plan

    *shards, squares = collect_call(
        parts, collect_plan, 24,
        [(shard, 3 * width), (shard, width), (shard, 2 * ff), (ff // 8, width), (shard, BLOCK)],
    )
    shards[4] = shards[4][:, :6].T
    squares = squares[:1]
    for how in (SWAP_Y, SWAP_Z[1], SWAP_Z[2]):
        squares = squares + swap(squares, how)
    grad_norm = jnp.sqrt(squares[0, :1])
    updates = updated(masters, firsts, seconds, shards, grad_norm, clip_norm)
    return (result, grad_input, *updates, grad_norm)


def solution(mesh):
    rows_split = P(("dp", "head"), None)
    mats, vecs = P("dp", None), P(None, "dp")
    state = (mats,) * 4 + (vecs,)
    in_specs = (rows_split, P("dp"), rows_split, P()) + state * 3
    out_specs = (rows_split, rows_split) + (mats,) * 16 + (vecs,) * 4 + (P(),)
    cube = mesh.shape["dp"] == 8 and mesh.shape["head"] == 4
    body = cube_body if cube else plain_body
    return jax.shard_map(body, mesh=mesh, in_specs=in_specs, out_specs=out_specs, check_vma=False)
```
